32 devices in a mesh: dp: 8 (over z, y), tensor: 4 (over x, core).
Axes of the slice: x: 2, y: 2, z: 4, core: 2. Of those that a mesh axis runs over, the one named last changes fastest.
Arguments:
- hidden_in: bfloat16 [16384, 768], P(('dp', 'tensor')), may hold values from -6 to 6
- cotangent: bfloat16 [16384, 768], P(('dp', 'tensor')), may hold values from -6 to 6
- group_ids: int32 [16384], P(('dp', 'tensor')), may hold values from 0 to 15
- weight_table: float32 [8], replicated, may hold values from 0.3 to 3
- table_index: int32 [16], replicated, may hold values from 0 to 7
- qkv_weight: bfloat16 [768, 3, 768], P('dp', None, 'tensor'), may hold values from -0.21875 to 0.21875
- out_weight: bfloat16 [768, 768], P('tensor', 'dp'), may hold values from -0.75 to 0.75
- up_weight: bfloat16 [768, 3072], P('dp', 'tensor'), may hold values from -0.21875 to 0.21875
- down_weight: bfloat16 [3072, 768], P('tensor', 'dp'), may hold values from -0.109375 to 0.109375
- norm1_gain: bfloat16 [768], P('dp'), may hold values from 0.5 to 1.5
- norm1_bias: bfloat16 [768], P('dp'), may hold values from -1 to 1
- norm2_gain: bfloat16 [768], P('dp'), may hold values from 0.5 to 1.5
- norm2_bias: bfloat16 [768], P('dp'), may hold values from -1 to 1
Outputs:
- block_output: float32 [16384, 768], P(('dp', 'tensor'))
- input_grad: float32 [16384, 768], P(('dp', 'tensor'))
- qkv_weight_grad: float32 [768, 3, 768], P('dp', None, 'tensor')
- out_weight_grad: float32 [768, 768], P('tensor', 'dp')
- up_weight_grad: float32 [768, 3072], P('dp', 'tensor')
- down_weight_grad: float32 [3072, 768], P('tensor', 'dp')
- norm1_gain_grad: float32 [768], P(('dp', 'tensor'))
- norm1_bias_grad: float32 [768], P(('dp', 'tensor'))
- norm2_gain_grad: float32 [768], P(('dp', 'tensor'))
- norm2_bias_grad: float32 [768], P(('dp', 'tensor'))
- group_counts: float32 [16], replicated
The draws below stay inside these ranges and needn't reach their ends.
All inputs are finite; a program needn't handle non-finite values.
Results may differ from the reference program's by a relative error of at most 0.017.
Values may be sent and summed in bfloat16 or wider, within the bound.
A program may use at most 128 MiB of HBM per device.

```python
import math
import jax
import jax.numpy as jnp
from jax import lax

D = 768
HEADS = 12
HEAD_DIM = 64
FF = 3072
LENGTH = 1024
GROUPS = 16
TABLE = 8
TOKENS = 16384


def with_ends(values, rng, smallest, high):
    shape = values.shape
    index_at = [jax.random.randint(jax.random.fold_in(rng, axis), (), 0, shape[axis]) for axis in range(len(shape))]
    values = values.at[tuple(index_at)].set(smallest)
    longest = shape.index(max(shape))
    index_at[longest] = (index_at[longest] + 1) % shape[longest]
    return values.at[tuple(index_at)].set(high)


def block_levels(key, shape, pieces, smallest, top_value):
    factor_of, own = 1.0, jax.random.fold_in(key, 6)
    for position, blocks in pieces:
        heights = jnp.exp(jax.random.uniform(jax.random.fold_in(own, position), (blocks,), jnp.float32, smallest / len(pieces), top_value / len(pieces)))
        factor_of = factor_of * jnp.repeat(heights, shape[position] // blocks).reshape([-1 if axis == position else 1 for axis in range(len(shape))])
    return factor_of


def gaussian(own_key, extent, width, reach, pieces=(), held_as=jnp.bfloat16):
    result = jax.random.normal(own_key, extent, jnp.float32) * width
    if len(pieces) > 0:
        result = block_levels(own_key, extent, pieces, -0.22, 0.18) * result
    return jnp.clip(result, min=-reach, max=reach).astype(held_as)


def setup_inputs(seed: int = 0) -> dict:
    keys = jax.random.split(jax.random.key(seed), 14)
    return {
        "hidden_in": gaussian(keys[0], (TOKENS, D), 1.0, 6.0, ((0, 32),)),
        "cotangent": gaussian(keys[1], (TOKENS, D), 1.0, 6.0, ((0, 32),)),
        "group_ids": with_ends(jax.random.randint(keys[2], (TOKENS,), 0, GROUPS), jax.random.fold_in(keys[2], 1), 0, GROUPS - 1).astype(jnp.int32),
        "weight_table": jnp.clip(jnp.exp(jax.random.uniform(keys[3], (TABLE,), jnp.float32, math.log(0.3), math.log(3.0))), 0.3, 3.0),
        "table_index": with_ends(jax.random.randint(keys[4], (GROUPS,), 0, TABLE), jax.random.fold_in(keys[4], 1), 0, TABLE - 1).astype(jnp.int32),
        "qkv_weight": gaussian(keys[5], (D, 3, D), D ** -0.5, 0.21875, ((0, 8), (2, 4))),
        "out_weight": gaussian(keys[6], (D, D), HEAD_DIM ** -0.5, 0.75, ((0, 4), (1, 8))),
        "up_weight": gaussian(keys[7], (D, FF), D ** -0.5, 0.21875, ((0, 8), (1, 4))),
        "down_weight": gaussian(keys[8], (FF, D), FF ** -0.5, 0.109375, ((0, 4), (1, 8))),
        "norm1_gain": jnp.clip(1.0 + 0.1 * jax.random.normal(keys[9], (D,), jnp.float32), 0.5, 1.5).astype(jnp.bfloat16),
        "norm1_bias": gaussian(keys[10], (D,), 0.2, 1.0, ((0, 8),)),
        "norm2_gain": jnp.clip(1.0 + 0.1 * jax.random.normal(keys[11], (D,), jnp.float32), 0.5, 1.5).astype(jnp.bfloat16),
        "norm2_bias": gaussian(keys[12], (D,), 0.2, 1.0, ((0, 8),)),
    }


EPSILON = 1e-05
MASKED_SCORE = -1e+30
HIGHEST = lax.Precision.HIGHEST

@jax.custom_vjp
def low(v):
    return lax.optimization_barrier(v.astype(jnp.bfloat16)).astype(jnp.float32)

@jax.custom_vjp
def low_back(v):
    return v

def low_keep(v):
    return (low(v), None)

def low_pass(kept, grad):
    return (grad,)

def back_keep(v):
    return (v, None)

def back_low(kept, grad):
    return (low(grad),)
low.defvjp(low_keep, low_pass)
low_back.defvjp(back_keep, back_low)

def norm_rows(inputs, gain, shift):
    center = inputs - lax.optimization_barrier(jnp.mean(inputs, -1, keepdims=True))
    variance = lax.optimization_barrier(jnp.mean(center * center, -1, keepdims=True))
    return center * lax.rsqrt(variance + EPSILON) * gain + shift

def layer(params, inputs):
    qkv_weight, out_weight, up_weight, down_weight, gain_one, bias_one, gain_two, bias_two = params
    length = inputs.shape[0]
    normed = low(norm_rows(inputs, gain_one, bias_one))
    projected = jnp.dot(normed, qkv_weight.reshape(D, 3 * D), precision=HIGHEST)
    projected = low_back(low(projected)).reshape(length, 3, HEADS, HEAD_DIM)
    scores = jnp.einsum('qhd,khd->hqk', projected[:, 0], projected[:, 1], precision=HIGHEST) * HEAD_DIM ** (-0.5)
    scores = low_back(scores)
    query_pos = lax.broadcasted_iota(jnp.int32, scores.shape, 1)
    key_pos = lax.broadcasted_iota(jnp.int32, scores.shape, 2)
    scores = jnp.where(key_pos <= query_pos, scores, MASKED_SCORE)
    probs = jax.nn.softmax(scores, axis=-1)
    context = jnp.einsum('hqk,khd->qhd', low(probs), projected[:, 2], precision=HIGHEST).reshape(length, D)
    context = low_back(low(context))
    attended = low_back(jnp.dot(context, out_weight, precision=HIGHEST))
    middle = inputs + attended
    normed_two = low(norm_rows(middle, gain_two, bias_two))
    pre_act = low_back(jnp.dot(normed_two, up_weight, precision=HIGHEST))
    activ = low(jax.nn.gelu(pre_act, approximate=True))
    return middle + jnp.dot(activ, down_weight, precision=HIGHEST)

def reference(hidden_in, cotangent, group_ids, weight_table, table_index, qkv_weight, out_weight, up_weight, down_weight, norm1_gain, norm1_bias, norm2_gain, norm2_bias):
    member = (group_ids[:, None] == jnp.arange(GROUPS, dtype=jnp.int32)[None, :]).astype(jnp.float32)
    group_counts = lax.optimization_barrier(jnp.sum(member, 0))
    table_hits = table_index[:, None] == jnp.arange(TABLE, dtype=jnp.int32)[None, :]
    group_weight = lax.optimization_barrier(jnp.sum(jnp.where(table_hits, weight_table[None, :], 0.0), 1))
    group_scale = group_weight * (TOKENS / GROUPS) / jnp.maximum(group_counts, 1.0)
    row_scale = lax.optimization_barrier(jnp.sum(jnp.where(member > 0.5, group_scale[None, :], 0.0), 1))
    upstream = low(cotangent.astype(jnp.float32) * row_scale[:, None])
    params = (qkv_weight.astype(jnp.float32), out_weight.astype(jnp.float32), up_weight.astype(jnp.float32), down_weight.astype(jnp.float32), norm1_gain.astype(jnp.float32), norm1_bias.astype(jnp.float32), norm2_gain.astype(jnp.float32), norm2_bias.astype(jnp.float32))
    sequences = TOKENS // LENGTH
    inputs_seq = hidden_in.astype(jnp.float32).reshape(sequences, LENGTH, D)
    upstream_seq = upstream.reshape(sequences, LENGTH, D)

    def one_sequence(running, packed):
        inputs, grads = packed
        output, pullback = jax.vjp(layer, params, inputs)
        grad_params, grad_inputs = pullback(grads)
        running = jax.tree.map(lambda first, second: first + second, running, grad_params)
        return (running, (output, grad_inputs))
    zeros = jax.tree.map(jnp.zeros_like, params)
    totals, (outputs, grad_inputs) = lax.scan(one_sequence, zeros, (inputs_seq, upstream_seq))
    return (outputs.reshape(TOKENS, D), grad_inputs.reshape(TOKENS, D), totals[0], totals[1], totals[2], totals[3], totals[4], totals[5], totals[6], totals[7], group_counts)
```

```python
import functools

import jax
import jax.numpy as jnp
from jax import lax
from jax.experimental import pallas as pl
from jax.experimental.pallas import tpu as pltpu
from jax.sharding import PartitionSpec as P

D = 768
HEAD_DIM = 64
LENGTH = 1024
HALF = 512
GROUPS = 16
TABLE = 8
NB = 8
RB = D // NB
HEADROWS = 144
EPSILON = 1e-05
MASKED_SCORE = -1e30
GELU_C = 0.7978845608028654
GELU_A = 0.044715
MESH = pl.DeviceIdType.MESH
F32 = jnp.float32
BF16 = jnp.bfloat16
NT = (((1,), (1,)), ((), ()))
TN = (((0,), (0,)), ((), ()))
NN = (((1,), (0,)), ((), ()))
VMEM_LIMIT = 66_000_000


def mm(a, b, dims=NN):
    return lax.dot_general(a, b, dims, preferred_element_type=F32)


class Place:
    def __init__(self):
        self.d = lax.axis_index("dp")
        self.t = lax.axis_index("tensor")
        self.z = lax.div(self.d, 2)
        self.y = lax.rem(self.d, 2)
        self.x = lax.div(self.t, 2)
        self.c = lax.rem(self.t, 2)
        c = self.c
        self.sibling = (self.d, self.t + 1 - 2 * c)
        self.x1 = lax.rem(self.x + c, 2)
        self.y1 = lax.rem(self.y + 1 - c, 2)
        self.x2 = lax.rem(self.x + 1 - c, 2)
        self.y2 = lax.rem(self.y + c, 2)
        self.p1 = (2 * self.z + self.y1, 2 * self.x1 + c)
        self.p2 = (2 * self.z + self.y2, 2 * self.x2 + c)
        self.up = (self.d + 2, self.t)
        self.dn = (self.d - 2, self.t)
        self.has_up = self.z < 3
        self.has_dn = self.z > 0


def entry_barrier(pos, net):
    bar = pltpu.get_barrier_semaphore()
    pl.semaphore_signal(bar, inc=1, device_id=pos.sibling, device_id_type=MESH)
    if not net:
        pl.semaphore_wait(bar, 1)
        return
    pl.semaphore_signal(bar, inc=1, device_id=pos.p1, device_id_type=MESH)
    pl.semaphore_signal(bar, inc=1, device_id=pos.p2, device_id_type=MESH)

    @pl.when(pos.has_up)
    def _():
        pl.semaphore_signal(bar, inc=1, device_id=pos.up, device_id_type=MESH)

    @pl.when(pos.has_dn)
    def _():
        pl.semaphore_signal(bar, inc=1, device_id=pos.dn, device_id_type=MESH)

    pl.semaphore_wait(bar, 3 + jnp.where(pos.has_up, 1, 0) + jnp.where(pos.has_dn, 1, 0))


class Gather:
    def __init__(self, pos, g, own, full, ssem, rsem):
        self.pos, self.g, self.own, self.full = pos, g, own, full
        self.ssem, self.rsem = ssem, rsem

    def copy(self, b, dd, link, zz, dev, src=None):
        slot = self.full.at[b, dd]
        return pltpu.make_async_remote_copy(
            src_ref=slot if src is None else src,
            dst_ref=slot,
            send_sem=self.ssem.at[self.g, link, zz],
            recv_sem=self.rsem.at[self.g, b, dd],
            device_id=dev,
            device_id_type=MESH,
        )

    def wait(self, b, dd):
        self.copy(b, dd, 0, 0, self.pos.p1).wait_recv()

    def start(self):
        p = self.pos
        own = self.own
        self.copy(p.x, p.d, 2, p.z, p.p1, own).start()
        self.copy(p.x, p.d, 3, p.z, p.p2, own).start()

        @pl.when(p.has_up)
        def _():
            self.copy(p.x, p.d, 0, p.z, p.up, own).start()

        @pl.when(p.has_dn)
        def _():
            self.copy(p.x, p.d, 1, p.z, p.dn, own).start()

    def line(self, k):
        p = self.pos

        @pl.when(p.z - k >= 0)
        def _():
            zz = p.z - k
            self.wait(p.x, 2 * zz + p.y)

            @pl.when(p.has_up)
            def _():
                self.copy(p.x, 2 * zz + p.y, 0, zz, p.up).start()

            self.copy(p.x, 2 * zz + p.y, 2, zz, p.p1).start()
            self.copy(p.x, 2 * zz + p.y, 3, zz, p.p2).start()

        @pl.when(p.z + k <= 3)
        def _():
            zz = p.z + k
            self.wait(p.x, 2 * zz + p.y)

            @pl.when(p.has_dn)
            def _():
                self.copy(p.x, 2 * zz + p.y, 1, zz, p.dn).start()

            self.copy(p.x, 2 * zz + p.y, 2, zz, p.p1).start()
            self.copy(p.x, 2 * zz + p.y, 3, zz, p.p2).start()

    def side(self, k):
        p = self.pos

        def forward(zz):
            self.wait(p.x1, 2 * zz + p.y1)
            self.copy(p.x1, 2 * zz + p.y1, 4, zz, p.p2).start()

        if k == 0:
            forward(p.z)
            return

        @pl.when(p.z - k >= 0)
        def _():
            forward(p.z - k)

        @pl.when(p.z + k <= 3)
        def _():
            forward(p.z + k)

    def step(self, k):
        if k == 0:
            self.start()
        if 1 <= k <= 3:
            self.line(k)
        if k >= 1:
            self.side(k - 1)

    def finish(self):
        p = self.pos
        for zz in range(4):
            self.wait(p.x2, 2 * zz + p.y2)
            self.wait(1 - p.x, 2 * zz + 1 - p.y)

    def drain(self):
        p = self.pos
        for zz in range(4):
            dd = 2 * zz + p.y

            @pl.when(p.has_up & (zz <= p.z))
            def _():
                self.copy(p.x, dd, 0, zz, p.up).wait_send()

            @pl.when(p.has_dn & (zz >= p.z))
            def _():
                self.copy(p.x, dd, 1, zz, p.dn).wait_send()

            self.copy(p.x, dd, 2, zz, p.p1).wait_send()
            self.copy(p.x, dd, 3, zz, p.p2).wait_send()
            self.copy(p.x1, 2 * zz + p.y1, 4, zz, p.p2).wait_send()


class Reduce:
    def __init__(self, pos, g, part, r2, rz, ssem, rsem):
        self.pos, self.g, self.part, self.r2, self.rz = pos, g, part, r2, rz
        self.ssem, self.rsem = ssem, rsem

    def copy(self, src, dst, link, zz, dev):
        return pltpu.make_async_remote_copy(
            src_ref=src,
            dst_ref=dst,
            send_sem=self.ssem.at[self.g, link, zz],
            recv_sem=self.rsem.at[self.g, link, zz],
            device_id=dev,
            device_id_type=MESH,
        )

    def to_p2(self, which, zz):
        p = self.pos
        b, dd = (p.x2, 2 * zz + p.y2) if which == 0 else (1 - p.x, 2 * zz + 1 - p.y)
        return self.copy(self.part.at[b, dd], self.r2.at[which, zz], which, zz, p.p2)

    def to_p1(self, zz):
        p = self.pos
        return self.copy(self.part.at[p.x1, 2 * zz + p.y1], self.rz.at[0, zz], 2, zz, p.p1)

    def to_z(self, way, zz):
        p = self.pos
        return self.copy(
            self.part.at[p.x, 2 * zz + p.y], self.rz.at[1 + way, zz], 3 + way, zz, p.dn if way else p.up
        )

    def add(self, b, dd, other):
        total = self.part[b, dd].astype(F32) + other.astype(F32)
        self.part[b, dd] = total.astype(self.part.dtype)

    def start(self):
        for which in (1, 0):
            for zz in range(4):
                self.to_p2(which, zz).start()

    def middle(self):
        p = self.pos
        for zz in range(4):
            self.to_p2(1, zz).wait_recv()
            self.add(p.x1, 2 * zz + p.y1, self.r2[1, zz])
            self.to_p1(zz).start()
        for zz in range(4):
            self.to_p2(0, zz).wait_recv()
            self.add(p.x, 2 * zz + p.y, self.r2[0, zz])

    def line(self):
        p = self.pos
        for zz in range(4):
            self.to_p1(zz).wait_recv()
            self.add(p.x, 2 * zz + p.y, self.rz[0, zz])
        for zz in (3, 2, 1):

            @pl.when(zz > p.z)
            def _():
                @pl.when(p.has_dn)
                def _():
                    self.to_z(0, zz).wait_recv()
                    self.add(p.x, 2 * zz + p.y, self.rz[1, zz])

                self.to_z(0, zz).start()

            dz = 3 - zz

            @pl.when(dz < p.z)
            def _():
                @pl.when(p.has_up)
                def _():
                    self.to_z(1, dz).wait_recv()
                    self.add(p.x, 2 * dz + p.y, self.rz[2, dz])

                self.to_z(1, dz).start()

    def finish(self, out):
        p = self.pos
        out[...] = self.part[p.x, p.d].astype(F32)

        @pl.when(p.has_dn)
        def _():
            self.to_z(0, p.z).wait_recv()
            out[...] += self.rz[1, p.z].astype(F32)

        @pl.when(p.has_up)
        def _():
            self.to_z(1, p.z).wait_recv()
            out[...] += self.rz[2, p.z].astype(F32)

    def drain(self):
        p = self.pos
        for zz in range(4):
            self.to_p2(1, zz).wait_send()
            self.to_p2(0, zz).wait_send()
            self.to_p1(zz).wait_send()

            @pl.when(zz > p.z)
            def _():
                self.to_z(0, zz).wait_send()

            @pl.when(zz < p.z)
            def _():
                self.to_z(1, zz).wait_send()


def rows(start, size):
    return pl.ds(pl.multiple_of(start, size), size)


def swap(pos, src, dst, sems, i):
    return pltpu.make_async_remote_copy(
        src_ref=src,
        dst_ref=dst,
        send_sem=sems.at[0, i],
        recv_sem=sems.at[1, i],
        device_id=pos.sibling,
        device_id_type=MESH,
    )


def norm_stats(values):
    center = values - jnp.mean(values, -1, keepdims=True)
    inv = lax.rsqrt(jnp.mean(center * center, -1, keepdims=True) + EPSILON)
    return center * inv, inv


def lane_half(shape, which):
    lane = lax.broadcasted_iota(jnp.int32, shape, 1)
    return (lane < HEAD_DIM) if which == 0 else (lane >= HEAD_DIM)


def only(values, which):
    return jnp.where(lane_half(values.shape, which), values, jnp.zeros_like(values))


def roll_half(values):
    return pltpu.roll(values.astype(F32), HEAD_DIM, 1).astype(BF16)


def unpack_heads(raw, wh):
    @pl.loop(0, NB)
    def _(dd):
        at = pl.multiple_of(dd * RB, 16)
        for part in range(4):
            wh[part, 0, pl.ds(at, RB)] = raw[0, dd, part, 0:96]
            wh[part, 1, pl.ds(at, RB)] = raw[1, dd, part, 0:96]
            first, second = raw[0, dd, part, 96:144], raw[1, dd, part, 96:144]
            left = lane_half(first.shape, 0)
            wh[part, 2, pl.ds(at, 48)] = jnp.where(left, first, roll_half(second))
            wh[part, 2, pl.ds(at + 48, 48)] = jnp.where(left, roll_half(first), second)


def pack_heads(gh, raw):
    @pl.loop(0, NB)
    def _(dd):
        at = pl.multiple_of(dd * RB, 16)
        for part in range(4):
            raw[0, dd, part, 0:96] = gh[part, 0, pl.ds(at, RB)]
            raw[1, dd, part, 0:96] = gh[part, 1, pl.ds(at, RB)]
            top, bottom = gh[part, 2, pl.ds(at, 48)], gh[part, 2, pl.ds(at + 48, 48)]
            left = lane_half(top.shape, 0)
            raw[0, dd, part, 96:144] = jnp.where(left, top, roll_half(bottom))
            raw[1, dd, part, 96:144] = jnp.where(left, roll_half(top), bottom)


def cat_pairs(ref, parts, pick):
    return jnp.concatenate([pick(ref, part, pair) for part in parts for pair in range(3)], axis=1)


def transpose_rows(src, dst):
    @pl.loop(0, LENGTH // 128)
    def _(i):
        r = rows(i * 128, 128)
        dst[:, r] = src[r, :].T


def forward_kernel(net, scale_tokens, *refs):
    (hid, cot, ids, table, weights, small, own1, own2, own3) = refs[:9]
    (o_block, o_counts, o_param, o_mid, o_heads, o_up, o_down, o_nrmT, o_qkv, o_lse, o_ctx, o_n2T, o_act, o_slope, o_ups, o_upsT) = refs[9:25]
    (
        v_small, v_raw, v_up, v_down, v_heads, v_param, v_counts, v_cnt, v_nrm, v_nrmT, v_qkv, v_lse, v_ctx,
        v_mid, v_n2, v_n2T, v_act, v_slope, v_ups, v_upsT, v_send, v_recv, v_acc, v_block,
        ssem, rsem, swsem, osem,
    ) = refs[25:]
    pos = Place()
    c = pos.c
    mine = c * HALF
    theirs = HALF - mine
    entry_barrier(pos, net)
    lanes = lax.broadcasted_iota(jnp.int32, (HALF, 128), 1)
    member = ids[...] == lanes
    own_counts = jnp.sum(member.astype(F32), 0, keepdims=True)

    puts = []

    def put(src, dst):
        cp = pltpu.make_async_copy(src, dst, osem.at[len(puts)])
        cp.start()
        puts.append(cp)

    if net:
        v_cnt[2] = small[...]
        v_cnt[2, 4:5, :] = own_counts
        g0 = Gather(pos, 0, v_cnt.at[2], v_small, ssem, rsem)
        g1 = Gather(pos, 1, own1, v_raw, ssem, rsem)
        g2 = Gather(pos, 2, own2, v_up, ssem, rsem)
        g3 = Gather(pos, 3, own3, v_down, ssem, rsem)
        g0.step(0)
        g1.step(0)
        v_small[pos.x, pos.d] = v_cnt[2]
        v_raw[pos.x, pos.d] = own1[...]
        v_up[pos.x, pos.d] = own2[...]
        v_down[pos.x, pos.d] = own3[...]
        for k in (1, 2, 3, 4):
            g0.step(k)
            g1.step(k)
        g0.finish()
        g2.step(0)
        v_param[...] = jnp.zeros_like(v_param)
        total = jnp.zeros((8, 128), F32)
        for dd in range(NB):
            row = lax.broadcasted_iota(jnp.int32, (128, D), 0)
            col = lax.broadcasted_iota(jnp.int32, (128, D), 1)
            place = ((col == row + RB * dd) & (row < RB)).astype(BF16)
            block = v_small[pos.x, dd]
            v_param[...] += mm(block.astype(BF16), place)
            total += v_small[0, dd] + v_small[1, dd]
        v_cnt[0] = total
        swap(pos, v_cnt.at[0], v_cnt.at[1], swsem, 0).start()
    else:
        v_param[...] = small[...]
        v_cnt[0] = jnp.broadcast_to(own_counts, (8, 128))
        cps = [
            pltpu.make_async_copy(own1, v_raw, osem.at[16]),
            pltpu.make_async_copy(own2, v_up, osem.at[17]),
            pltpu.make_async_copy(own3, v_down, osem.at[18]),
        ]
        for cp in cps:
            cp.start()
        for cp in cps:
            cp.wait()

    @pl.loop(0, HALF // 64)
    def _(i):
        r = rows(i * 64, 64)
        hat, _inv = norm_stats(hid[r, :].astype(F32))
        normed = hat * v_param[0:1, :] + v_param[1:2, :]
        v_nrm[rows(mine + i * 64, 64), :] = normed.astype(BF16)

    swap_nrm = swap(pos, v_nrm.at[rows(mine, HALF)], v_nrm.at[rows(mine, HALF)], swsem, 1)
    swap_nrm.start()

    if net:
        swap(pos, v_cnt.at[0], v_cnt.at[1], swsem, 0).wait()
        counts = (v_cnt[0] + v_cnt[1])[4:5, :]
        v_counts[...] = jnp.broadcast_to(counts, (8, 128))
        index = table[0:1, :]
        weight = jnp.zeros((1, 128), F32)
        for r in range(TABLE):
            weight = weight + jnp.where(index == r, weights[r], 0.0)
        group_scale = weight * scale_tokens / jnp.maximum(counts, 1.0)
    else:
        v_counts[...] = table[...].astype(F32)
        group_scale = weights[0:1, :]

    row_scale = jnp.sum(jnp.where(member, group_scale, 0.0), 1, keepdims=True)
    v_ups[rows(mine, HALF), :] = (cot[...].astype(F32) * row_scale).astype(BF16)
    swap_ups = swap(pos, v_ups.at[rows(mine, HALF)], v_ups.at[rows(mine, HALF)], swsem, 2)
    swap_ups.start()

    if net:
        g1.finish()
    unpack_heads(v_raw, v_heads)
    put(v_heads, o_heads)
    put(v_param, o_param)
    put(v_counts, o_counts)

    if net:
        g2.step(1)
    for half, start in enumerate((mine, theirs)):
        if half == 1:
            swap(pos, v_nrm.at[rows(theirs, HALF)], v_nrm.at[rows(theirs, HALF)], swsem, 1).wait_recv()
        lhs = v_nrm[rows(start, HALF), :]
        for part in range(3):
            rhs = cat_pairs(v_heads, (part,), lambda ref, a, b: ref[a, b])
            res = mm(lhs, rhs).astype(BF16)
            if part == 0:
                res = (res.astype(F32) * HEAD_DIM**-0.5).astype(BF16)
            for pair in range(3):
                v_qkv[3 * part + pair, rows(start, HALF), :] = res[:, 128 * pair : 128 * pair + 128]
    put(v_qkv, o_qkv)
    if net:
        g2.step(2)

    @pl.loop(0, 3)
    def _(pair):
        if net:

            @pl.when(pair == 1)
            def _():
                g2.step(3)

            @pl.when(pair == 2)
            def _():
                g2.step(4)
                g3.step(0)

        for i in range(4):
            n = 256 * (i + 1)
            q = v_qkv[pair, 256 * i : n, :]
            out = jnp.zeros((256, 128), F32)
            for h in range(2):
                pieces = []
                peak = None
                for j in range(i + 1):
                    k = only(v_qkv[3 + pair, 256 * j : 256 * j + 256, :], h)
                    s = mm(k, q, NT)
                    if j == i:
                        key = lax.broadcasted_iota(jnp.int32, s.shape, 0)
                        query = lax.broadcasted_iota(jnp.int32, s.shape, 1)
                        s = jnp.where(key <= query, s, MASKED_SCORE)
                    top = jnp.max(s, 0, keepdims=True)
                    peak = top if peak is None else jnp.maximum(peak, top)
                    pieces.append(s)
                total = jnp.zeros((1, 256), F32)
                for j in range(i + 1):
                    e = jnp.exp(pieces[j] - peak)
                    total += jnp.sum(e, 0, keepdims=True)
                    pieces[j] = e
                inv = 1.0 / total
                for j in range(i + 1):
                    v = only(v_qkv[6 + pair, 256 * j : 256 * j + 256, :], h)
                    out += mm((pieces[j] * inv).astype(BF16), v, TN)
                v_lse[pair, h : h + 1, 256 * i : n] = peak + jnp.log(total)
            v_ctx[pair, 256 * i : n, :] = out.astype(BF16)

    put(v_lse, o_lse)
    put(v_ctx, o_ctx)
    if net:
        g3.step(1)

    w_out = cat_pairs(v_heads, (3,), lambda ref, a, b: ref[a, b])
    for half, start in enumerate((theirs, mine)):
        lhs = jnp.concatenate([v_ctx[pair, rows(start, HALF), :] for pair in range(3)], axis=1)
        res = mm(lhs, w_out, NT)
        if half == 0:
            v_send[0] = res.astype(BF16)
            swap(pos, v_send.at[0], v_recv.at[0], swsem, 3).start()
        else:
            v_acc[...] = res
    if net:
        g3.step(2)
    transpose_rows(v_nrm, v_nrmT)
    put(v_nrmT, o_nrmT)
    swap(pos, v_send.at[0], v_recv.at[0], swsem, 3).wait()

    @pl.loop(0, HALF // 64)
    def _(i):
        r = rows(i * 64, 64)
        middle = hid[r, :].astype(F32) + v_acc[r, :] + v_recv[0, r, :].astype(F32)
        v_mid[r, :] = middle
        hat, _inv = norm_stats(middle)
        v_n2[rows(mine + i * 64, 64), :] = (hat * v_param[2:3, :] + v_param[3:4, :]).astype(BF16)

    swap(pos, v_n2.at[rows(mine, HALF)], v_n2.at[rows(mine, HALF)], swsem, 4).start()
    put(v_mid, o_mid)
    if net:
        g2.finish()
        g3.step(3)
    put(v_up, o_up)

    for half, start in enumerate((mine, theirs)):
        if half == 1:
            swap(pos, v_n2.at[rows(theirs, HALF)], v_n2.at[rows(theirs, HALF)], swsem, 4).wait_recv()

        @pl.loop(0, 6)
        def _(tile):
            b = lax.div(tile, 3)
            cols = pl.ds(pl.multiple_of(lax.rem(tile, 3) * 256, 256), 256)
            pre = mm(v_n2[rows(start, HALF), :], v_up[b, :, :, cols].reshape(D, 256))
            square = pre * pre
            bend = jnp.tanh(GELU_C * pre * (1.0 + GELU_A * square))
            v_act[b, rows(start, HALF), cols] = (0.5 * pre * (1.0 + bend)).astype(BF16)
            slope = 0.5 * (1.0 + bend) + 0.5 * pre * (1.0 - bend * bend) * (GELU_C * (1.0 + 3.0 * GELU_A * square))
            v_slope[b, rows(start, HALF), cols] = slope.astype(BF16)

        if net and half == 0:
            g3.step(4)

    put(v_act, o_act)
    put(v_slope, o_slope)
    transpose_rows(v_n2, v_n2T)
    put(v_n2T, o_n2T)
    swap(pos, v_ups.at[rows(theirs, HALF)], v_ups.at[rows(theirs, HALF)], swsem, 2).wait_recv()
    put(v_ups, o_ups)
    transpose_rows(v_ups, v_upsT)
    put(v_upsT, o_upsT)
    if net:
        g3.finish()
    put(v_down, o_down)
    for half, start in enumerate((theirs, mine)):
        res = mm(v_act[0, rows(start, HALF), :], v_down[0].reshape(D, D), NT)
        res += mm(v_act[1, rows(start, HALF), :], v_down[1].reshape(D, D), NT)
        if half == 0:
            v_send[1] = res.astype(BF16)
            swap(pos, v_send.at[1], v_recv.at[1], swsem, 5).start()
        else:
            v_acc[...] = res
    swap(pos, v_send.at[1], v_recv.at[1], swsem, 5).wait()
    v_block[...] = v_mid[...] + v_acc[...] + v_recv[1].astype(F32)
    put(v_block, o_block)
    for i, ref in ((1, v_nrm), (2, v_ups), (4, v_n2)):
        swap(pos, ref.at[rows(mine, HALF)], ref.at[rows(mine, HALF)], swsem, i).wait_send()
    if net:
        for g in (g0, g1, g2, g3):
            g.drain()
    for cp in puts:
        cp.wait()


def backward_kernel(net, *refs):
    (hid, param, h_mid, h_heads, h_up, h_down, h_nrmT, h_qkv, h_lse, h_ctx, h_n2T, h_act, h_slope, h_ups, h_upsT) = refs[:15]
    nout = 5
    o_in, o_small, o1, o2, o3 = refs[15 : 15 + nout]
    (
        v_mid, v_heads, v_up, v_down, v_nrmT, v_qkv, v_lse, v_ctx, v_n2T, v_act, v_slope, v_ups, v_upsT,
        v_low, v_dmid, v_dctx, v_dqkv, v_dk, v_dv, v_acc, v_send, v_recv, v_gh, v_p0, v_p1, v_p2, v_p3,
        v_sums, v_swap, *nets,
    ) = refs[15 + nout : 15 + nout + 29] + tuple(refs[15 + nout + 29 :])
    swsem, lsem = nets[-2:]
    pos = Place()
    c = pos.c
    mine = c * HALF
    theirs = HALF - mine
    loads = {}
    for i, (src, dst) in enumerate(
        ((h_upsT, v_upsT), (h_act, v_act), (h_ups, v_ups), (h_down, v_down), (h_slope, v_slope), (h_n2T, v_n2T), (h_up, v_up),
         (h_mid, v_mid), (h_heads, v_heads), (h_ctx, v_ctx), (h_qkv, v_qkv), (h_lse, v_lse), (h_nrmT, v_nrmT))
    ):
        cp = pltpu.make_async_copy(src, dst, lsem.at[i])
        cp.start()
        loads[id(dst)] = cp
    loaded = lambda *which: [loads[id(w)].wait() for w in which]
    entry_barrier(pos, net)
    if net:
        r2_0, rz_0, r2_1, rz_1, r2_2, rz_2, r2_3, rz_3, ssem, rsem = nets[:-2]
        s0 = Reduce(pos, 0, v_p0, r2_0, rz_0, ssem, rsem)
        s1 = Reduce(pos, 1, v_p1, r2_1, rz_1, ssem, rsem)
        s2 = Reduce(pos, 2, v_p2, r2_2, rz_2, ssem, rsem)
        s3 = Reduce(pos, 3, v_p3, r2_3, rz_3, ssem, rsem)

    def tile_of(tile):
        return lax.div(tile, 3), pl.ds(pl.multiple_of(lax.rem(tile, 3) * 256, 256), 256)

    loaded(v_upsT, v_act)

    @pl.loop(0, 6)
    def _(tile):
        b, cols = tile_of(tile)
        res = mm(v_upsT[...], v_act[b, :, cols])
        v_p3[b, :, :, cols] = res.astype(BF16).reshape(NB, RB, 256)

    if net:
        s3.start()
    loaded(v_ups, v_down, v_slope, v_n2T)

    @pl.loop(0, 6)
    def _(tile):
        b, cols = tile_of(tile)
        res = mm(v_ups[...], v_down[b, :, :, cols].reshape(D, 256))
        pre = (res * v_slope[b, :, cols].astype(F32)).astype(BF16)
        v_slope[b, :, cols] = pre
        res = mm(v_n2T[...], pre)
        v_p2[b, :, :, cols] = res.astype(BF16).reshape(NB, RB, 256)

    if net:
        s3.middle()
        s2.start()
    loaded(v_up, v_mid)
    for half, start in enumerate((theirs, mine)):
        res = mm(v_slope[0, rows(start, HALF), :], v_up[0].reshape(D, D), NT)
        res += mm(v_slope[1, rows(start, HALF), :], v_up[1].reshape(D, D), NT)
        if half == 0:
            v_send[0] = res.astype(BF16)
            swap(pos, v_send.at[0], v_recv.at[0], swsem, 0).start()
        else:
            v_acc[...] = res
    swap(pos, v_send.at[0], v_recv.at[0], swsem, 0).wait()
    v_sums[...] = jnp.zeros_like(v_sums)

    def norm_back(upper, values, gain, at):
        hat, inv = norm_stats(values)
        scaled = upper * gain
        first = jnp.mean(scaled, -1, keepdims=True)
        second = jnp.mean(scaled * hat, -1, keepdims=True)
        v_sums[at : at + 1, :] += jnp.sum(upper * hat, 0, keepdims=True)
        v_sums[at + 1 : at + 2, :] += jnp.sum(upper, 0, keepdims=True)
        return inv * (scaled - first - hat * second)

    @pl.loop(0, HALF // 64)
    def _(i):
        r = rows(i * 64, 64)
        upper = v_acc[r, :] + v_recv[0, r, :].astype(F32)
        wide = rows(mine + i * 64, 64)
        d_mid = v_ups[wide, :].astype(F32) + norm_back(upper, v_mid[r, :], param[2:3, :], 2)
        v_dmid[r, :] = d_mid
        v_low[wide, :] = d_mid.astype(BF16)

    swap(pos, v_low.at[rows(mine, HALF)], v_low.at[rows(mine, HALF)], swsem, 1).start()
    if net:
        s3.line()
    loaded(v_heads, v_ctx)
    w_out = cat_pairs(v_heads, (3,), lambda ref, a, b: ref[a, b])
    for half, start in enumerate((mine, theirs)):
        if half == 1:
            swap(pos, v_low.at[rows(theirs, HALF)], v_low.at[rows(theirs, HALF)], swsem, 1).wait_recv()
        res = mm(v_low[rows(start, HALF), :], w_out).astype(BF16)
        for pair in range(3):
            v_dctx[pair, rows(start, HALF), :] = res[:, 128 * pair : 128 * pair + 128]
    transpose_rows(v_low, v_upsT)
    res = mm(v_upsT[...], jnp.concatenate([v_ctx[pair] for pair in range(3)], axis=1)).astype(BF16)
    for pair in range(3):
        v_gh[3, pair] = res[:, 128 * pair : 128 * pair + 128]
    if net:
        s3.finish(o3)
        s2.middle()
    loaded(v_qkv, v_lse, v_nrmT)

    @pl.loop(0, 3)
    def _(pair):
        if net:

            @pl.when(pair == 1)
            def _():
                s2.line()

            @pl.when(pair == 2)
            def _():
                s2.finish(o2)

        v_dk[...] = jnp.zeros_like(v_dk)
        v_dv[...] = jnp.zeros_like(v_dv)
        for i in range(4):
            n = 256 * (i + 1)
            q = v_qkv[pair, 256 * i : n, :]
            up = v_dctx[pair, 256 * i : n, :]
            qs = [only(q, h) for h in range(2)]
            ups = [only(up, h) for h in range(2)]
            dq = jnp.zeros((256, 128), F32)
            probs = [[], []]
            grads = [[], []]
            for h in range(2):
                lse = v_lse[pair, h : h + 1, 256 * i : n]
                delta = jnp.zeros((1, 256), F32)
                for j in range(i + 1):
                    at = slice(256 * j, 256 * j + 256)
                    s = mm(v_qkv[3 + pair, at, :], qs[h], NT)
                    p = jnp.exp(s - lse)
                    if j == i:
                        key = lax.broadcasted_iota(jnp.int32, s.shape, 0)
                        query = lax.broadcasted_iota(jnp.int32, s.shape, 1)
                        p = jnp.where(key <= query, p, 0.0)
                    dp = mm(v_qkv[6 + pair, at, :], ups[h], NT)
                    delta += jnp.sum(p * dp, 0, keepdims=True)
                    probs[h].append(p)
                    grads[h].append(dp)
                for j in range(i + 1):
                    grads[h][j] = (probs[h][j] * (grads[h][j] - delta)).astype(BF16)
                    probs[h][j] = probs[h][j].astype(BF16)
            for j in range(i + 1):
                at = slice(256 * j, 256 * j + 256)
                for h in range(2):
                    k = only(v_qkv[3 + pair, at, :], h)
                    dq += mm(grads[h][j], k, TN)
                v_dv[at, :] += mm(
                    jnp.concatenate([probs[0][j], probs[1][j]], axis=1), jnp.concatenate(ups, axis=0)
                )
                v_dk[at, :] += mm(
                    jnp.concatenate([grads[0][j], grads[1][j]], axis=1), jnp.concatenate(qs, axis=0)
                )
            v_dqkv[pair, 256 * i : n, :] = (dq * HEAD_DIM**-0.5).astype(BF16)
        v_dqkv[3 + pair] = v_dk[...].astype(BF16)
        v_dqkv[6 + pair] = v_dv[...].astype(BF16)

    for part in range(3):
        res = mm(v_nrmT[...], jnp.concatenate([v_dqkv[3 * part + pair] for pair in range(3)], axis=1)).astype(BF16)
        for pair in range(3):
            v_gh[part, pair] = res[:, 128 * pair : 128 * pair + 128]
    pack_heads(v_gh, v_p1)
    if net:
        s1.start()
    w_qkv = cat_pairs(v_heads, (0, 1, 2), lambda ref, a, b: ref[a, b])
    for half, start in enumerate((theirs, mine)):
        lhs = jnp.concatenate([v_dqkv[j, rows(start, HALF), :] for j in range(9)], axis=1)
        res = mm(lhs, w_qkv, NT)
        if half == 0:
            v_send[1] = res.astype(BF16)
            swap(pos, v_send.at[1], v_recv.at[1], swsem, 2).start()
        else:
            v_acc[...] = res
    swap(pos, v_send.at[1], v_recv.at[1], swsem, 2).wait()

    @pl.loop(0, HALF // 64)
    def _(i):
        r = rows(i * 64, 64)
        upper = v_acc[r, :] + v_recv[1, r, :].astype(F32)
        o_in[r, :] = v_dmid[r, :] + norm_back(upper, hid[r, :].astype(F32), param[0:1, :], 0)

    v_swap[0] = v_sums[...]
    swap(pos, v_swap.at[0], v_swap.at[1], swsem, 3).start()
    if net:
        s1.middle()
    swap(pos, v_swap.at[0], v_swap.at[1], swsem, 3).wait()
    both = v_swap[0] + v_swap[1]
    if net:
        for dd in range(NB):
            piece = jnp.concatenate([both[:, RB * dd : RB * dd + RB], jnp.zeros((8, 128 - RB), F32)], axis=1)
            v_p0[0, dd] = piece
            v_p0[1, dd] = piece
        s0.start()
        s0.middle()
        s1.line()
        s0.line()
        s1.finish(o1)
        s0.finish(o_small)
        for s in (s0, s1, s2, s3):
            s.drain()
    else:
        o_small[...] = both
        o1[...] = v_p1[...]
        o2[...] = v_p2[...]
        o3[...] = v_p3[...]
    swap(pos, v_low.at[rows(mine, HALF)], v_low.at[rows(mine, HALF)], swsem, 1).wait_send()


def pack_rows(block):
    third = block[:, :, 128:].reshape(4, 2, 48, 64).transpose(0, 2, 1, 3).reshape(4, 48, 128)
    return jnp.concatenate([block[:, :, :128], third], axis=1)


def unpack_rows(packed):
    third = packed[:, 96:].reshape(4, 48, 2, 64).transpose(0, 2, 1, 3).reshape(4, 96, 64)
    return jnp.concatenate([packed[:, :96], third], axis=2)


def shards(
    hidden_in, cotangent, group_ids, weight_table, table_index, qkv_weight, out_weight, up_weight, down_weight,
    norm1_gain, norm1_bias, norm2_gain, norm2_bias,
):
    n_dp, n_t = lax.axis_size("dp"), lax.axis_size("tensor")
    net = n_dp == NB and n_t == 4
    t = lax.axis_index("tensor")
    core = lax.rem(t, 2)
    tokens = hidden_in.shape[0] * n_dp * n_t
    scale_tokens = tokens / GROUPS
    heads = jnp.concatenate([qkv_weight.transpose(1, 0, 2), out_weight.T[None]], axis=0)
    vectors = jnp.stack([norm1_gain, norm1_bias, norm2_gain, norm2_bias]).astype(F32)
    ids = group_ids.reshape(HALF, 1)
    down = down_weight.T
    if net:
        own = (pack_rows(heads), up_weight, down)
        small = jnp.pad(vectors, ((0, 4), (0, 128 - RB)))
        table = jnp.pad(table_index[None, :], ((0, 7), (0, 128 - GROUPS)), constant_values=-1)
        weights = weight_table
        weight_spec = pl.BlockSpec(memory_space=pltpu.SMEM)
        own_spec = pl.BlockSpec(memory_space=pltpu.VMEM)
    else:

        def whole(block, axis):
            full = lax.all_gather(block, "dp", axis=axis, tiled=True)
            every = lax.all_gather(full, "tensor", axis=0)
            pair = lax.dynamic_index_in_dim(every.reshape((n_t // 2, 2) + full.shape), core, 1, keepdims=False)
            return pair

        heads_all = whole(heads, 1).reshape(2, 4, NB, RB, 192).transpose(0, 2, 1, 3, 4)
        own = (
            jax.vmap(jax.vmap(pack_rows))(heads_all),
            whole(up_weight, 0).reshape(2, NB, RB, D),
            whole(down, 0).reshape(2, NB, RB, D),
        )
        small = jnp.pad(lax.all_gather(vectors, "dp", axis=1, tiled=True), ((0, 4), (0, 0)))
        member = (group_ids[:, None] == jnp.arange(GROUPS, dtype=jnp.int32)[None, :]).astype(F32)
        counts = lax.psum(jnp.sum(member, 0), ("dp", "tensor"))
        hits = table_index[:, None] == jnp.arange(TABLE, dtype=jnp.int32)[None, :]
        scale = jnp.sum(jnp.where(hits, weight_table[None, :], 0.0), 1) * scale_tokens / jnp.maximum(counts, 1.0)
        weights = jnp.pad(scale[None, :], ((0, 7), (0, 128 - GROUPS)))
        table = jnp.pad(counts.astype(jnp.int32)[None, :], ((0, 7), (0, 128 - GROUPS)))
        weight_spec = pl.BlockSpec(memory_space=pltpu.VMEM)
        own_spec = pl.BlockSpec(memory_space=pl.ANY)

    def sds(shape, dtype=BF16):
        return jax.ShapeDtypeStruct(shape, dtype)

    vspec = pl.BlockSpec(memory_space=pltpu.VMEM)
    aspec = pl.BlockSpec(memory_space=pl.ANY)
    saved = [
        sds((HALF, D), F32), sds((8, 128), F32), sds((8, D), F32), sds((HALF, D), F32), sds((4, 3, D, 128)),
        sds((2, NB, RB, D)), sds((2, NB, RB, D)), sds((D, LENGTH)), sds((9, LENGTH, 128)), sds((3, 8, LENGTH), F32),
        sds((3, LENGTH, 128)), sds((D, LENGTH)), sds((2, LENGTH, D)), sds((2, LENGTH, D)), sds((LENGTH, D)), sds((D, LENGTH)),
    ]
    vm = pltpu.VMEM
    dma = pltpu.SemaphoreType.DMA
    outs = pl.pallas_call(
        functools.partial(forward_kernel, net, scale_tokens),
        out_shape=saved,
        in_specs=[vspec, vspec, vspec, vspec, weight_spec, vspec, own_spec, own_spec, own_spec],
        out_specs=[aspec] * len(saved),
        scratch_shapes=[
            vm((2, NB, 8, 128), F32), vm((2, NB, 4, HEADROWS, 128), BF16), vm((2, NB, RB, D), BF16), vm((2, NB, RB, D), BF16),
            vm((4, 3, D, 128), BF16), vm((8, D), F32), vm((8, 128), F32), vm((3, 8, 128), F32),
            vm((LENGTH, D), BF16), vm((D, LENGTH), BF16), vm((9, LENGTH, 128), BF16), vm((3, 8, LENGTH), F32), vm((3, LENGTH, 128), BF16),
            vm((HALF, D), F32), vm((LENGTH, D), BF16), vm((D, LENGTH), BF16), vm((2, LENGTH, D), BF16), vm((2, LENGTH, D), BF16),
            vm((LENGTH, D), BF16), vm((D, LENGTH), BF16), vm((2, HALF, D), BF16), vm((2, HALF, D), BF16), vm((HALF, D), F32), vm((HALF, D), F32),
            dma((4, 5, 4)), dma((4, 2, NB)), dma((2, 6)), dma((19,)),
        ],
        compiler_params=pltpu.CompilerParams(collective_id=0, has_side_effects=True, vmem_limit_bytes=VMEM_LIMIT),
        name="block_forward",
    )(hidden_in, cotangent, ids, table, weights, small, *own)
    (block_output, counts_out, param, mid, heads_w, up_w, down_w, nrmT, qkv, lse, ctx, n2T, act, slope, ups, upsT) = outs

    slot = [(8, 128), (4, HEADROWS, 128), (RB, D), (RB, D)]
    kind = [F32, BF16, BF16, BF16]
    net_scratch = []
    if net:
        for s, k in zip(slot, kind):
            net_scratch += [vm((2, 4) + s, k), vm((3, 4) + s, k)]
        net_scratch += [dma((4, 5, 4)), dma((4, 5, 4))]
        grad_shapes = [sds(s, F32) for s in slot]
    else:
        grad_shapes = [sds((8, D), F32)] + [sds((2, NB) + s) for s in slot[1:]]
    out2 = pl.pallas_call(
        functools.partial(backward_kernel, net),
        out_shape=[sds((HALF, D), F32)] + grad_shapes,
        in_specs=[vspec, vspec] + [aspec] * 13,
        out_specs=[vspec] * 5,
        scratch_shapes=[
            vm((HALF, D), F32), vm((4, 3, D, 128), BF16), vm((2, NB, RB, D), BF16), vm((2, NB, RB, D), BF16), vm((D, LENGTH), BF16),
            vm((9, LENGTH, 128), BF16), vm((3, 8, LENGTH), F32), vm((3, LENGTH, 128), BF16), vm((D, LENGTH), BF16),
            vm((2, LENGTH, D), BF16), vm((2, LENGTH, D), BF16), vm((LENGTH, D), BF16), vm((D, LENGTH), BF16),
            vm((LENGTH, D), BF16), vm((HALF, D), F32), vm((3, LENGTH, 128), BF16), vm((9, LENGTH, 128), BF16),
            vm((LENGTH, 128), F32), vm((LENGTH, 128), F32), vm((HALF, D), F32), vm((2, HALF, D), BF16), vm((2, HALF, D), BF16),
            vm((4, 3, D, 128), BF16), vm((2, NB, 8, 128), F32), vm((2, NB, 4, HEADROWS, 128), BF16), vm((2, NB, RB, D), BF16), vm((2, NB, RB, D), BF16),
            vm((8, D), F32), vm((2, 8, D), F32),
            *net_scratch, dma((2, 4)), dma((13,)),
        ],
        compiler_params=pltpu.CompilerParams(collective_id=1, has_side_effects=True, vmem_limit_bytes=VMEM_LIMIT),
        name="block_backward",
    )(hidden_in, param, mid, heads_w, up_w, down_w, nrmT, qkv, lse, ctx, n2T, act, slope, ups, upsT)
    input_grad, sums, g1, g2, g3 = out2
    if net:
        piece = lax.dynamic_slice_in_dim(sums[:4], t * 24, 24, 1)
        norms = [piece[0], piece[1], piece[2], piece[3]]
        grad_heads, grad_up, grad_down = unpack_rows(g1), g2, g3
    else:

        def owned(part):
            base = jnp.zeros((n_t // 2, 2) + part.shape[1:], F32)
            base = lax.dynamic_update_index_in_dim(base, part.astype(F32), core, 1)
            flat = base.reshape((n_t,) + part.shape[1:])
            mine = lax.psum_scatter(flat, "tensor", scatter_dimension=0, tiled=False)
            return lax.psum_scatter(mine, "dp", scatter_dimension=0, tiled=True)

        gh = jax.vmap(jax.vmap(unpack_rows))(g1)
        gh = gh.transpose(0, 1, 3, 2, 4).reshape(2, D, 4, 192)
        grad_heads = owned(gh).transpose(1, 0, 2)
        grad_up, grad_down = owned(g2.reshape(2, D, D)), owned(g3.reshape(2, D, D))
        half_sums = jnp.where(core == 0, sums, 0.0)
        norms = [
            lax.psum_scatter(half_sums[i], ("dp", "tensor"), scatter_dimension=0, tiled=True) for i in range(4)
        ]
    return (
        block_output,
        input_grad,
        grad_heads[:3].transpose(1, 0, 2),
        grad_heads[3].T,
        grad_up,
        grad_down.T,
        norms[0],
        norms[1],
        norms[2],
        norms[3],
        counts_out[0, :GROUPS],
    )


def solution(mesh):
    both = ("dp", "tensor")
    return jax.shard_map(
        shards,
        mesh=mesh,
        in_specs=(
            P(both, None), P(both, None), P(both), P(), P(), P("dp", None, "tensor"), P("tensor", "dp"), P("dp", "tensor"),
            P("tensor", "dp"), P("dp"), P("dp"), P("dp"), P("dp"),
        ),
        out_specs=(
            P(both, None), P(both, None), P("dp", None, "tensor"), P("tensor", "dp"), P("dp", "tensor"), P("tensor", "dp"),
            P(both), P(both), P(both), P(both), P(),
        ),
        check_vma=False,
    )
```

```python
import functools

import jax
import jax.numpy as jnp
from jax import lax
from jax.experimental import pallas as pl
from jax.experimental.pallas import tpu as pltpu
from jax.sharding import PartitionSpec as P

D = 768
HEAD_DIM = 64
LENGTH = 1024
HALF = 512
GROUPS = 16
TABLE = 8
NB = 8
RB = D // NB
HEADROWS = 144
EPSILON = 1e-05
MASKED_SCORE = -1e30
GELU_C = 0.7978845608028654
GELU_A = 0.044715
MESH = pl.DeviceIdType.MESH
F32 = jnp.float32
BF16 = jnp.bfloat16
NT = (((1,), (1,)), ((), ()))
TN = (((0,), (0,)), ((), ()))
NN = (((1,), (0,)), ((), ()))
VMEM_LIMIT = 66_000_000


def mm(a, b, dims=NN):
    return lax.dot_general(a, b, dims, preferred_element_type=F32)


class Place:
    def __init__(self):
        self.d = lax.axis_index("dp")
        self.t = lax.axis_index("tensor")
        self.z = lax.div(self.d, 2)
        self.y = lax.rem(self.d, 2)
        self.x = lax.div(self.t, 2)
        self.c = lax.rem(self.t, 2)
        c = self.c
        self.sibling = (self.d, self.t + 1 - 2 * c)
        self.x1 = lax.rem(self.x + c, 2)
        self.y1 = lax.rem(self.y + 1 - c, 2)
        self.x2 = lax.rem(self.x + 1 - c, 2)
        self.y2 = lax.rem(self.y + c, 2)
        self.p1 = (2 * self.z + self.y1, 2 * self.x1 + c)
        self.p2 = (2 * self.z + self.y2, 2 * self.x2 + c)
        self.up = (self.d + 2, self.t)
        self.dn = (self.d - 2, self.t)
        self.has_up = self.z < 3
        self.has_dn = self.z > 0


def entry_barrier(pos, net):
    bar = pltpu.get_barrier_semaphore()
    pl.semaphore_signal(bar, inc=1, device_id=pos.sibling, device_id_type=MESH)
    if not net:
        pl.semaphore_wait(bar, 1)
        return
    pl.semaphore_signal(bar, inc=1, device_id=pos.p1, device_id_type=MESH)
    pl.semaphore_signal(bar, inc=1, device_id=pos.p2, device_id_type=MESH)

    @pl.when(pos.has_up)
    def _():
        pl.semaphore_signal(bar, inc=1, device_id=pos.up, device_id_type=MESH)

    @pl.when(pos.has_dn)
    def _():
        pl.semaphore_signal(bar, inc=1, device_id=pos.dn, device_id_type=MESH)

    pl.semaphore_wait(bar, 3 + jnp.where(pos.has_up, 1, 0) + jnp.where(pos.has_dn, 1, 0))


class Gather:
    def __init__(self, pos, g, own, full, ssem, rsem):
        self.pos, self.g, self.own, self.full = pos, g, own, full
        self.ssem, self.rsem = ssem, rsem

    def copy(self, b, dd, link, zz, dev, src=None):
        slot = self.full.at[b, dd]
        return pltpu.make_async_remote_copy(
            src_ref=slot if src is None else src,
            dst_ref=slot,
            send_sem=self.ssem.at[self.g, link, zz],
            recv_sem=self.rsem.at[self.g, b, dd],
            device_id=dev,
            device_id_type=MESH,
        )

    def wait(self, b, dd):
        self.copy(b, dd, 0, 0, self.pos.p1).wait_recv()

    def start(self):
        p = self.pos
        own = self.own
        self.copy(p.x, p.d, 2, p.z, p.p1, own).start()
        self.copy(p.x, p.d, 3, p.z, p.p2, own).start()

        @pl.when(p.has_up)
        def _():
            self.copy(p.x, p.d, 0, p.z, p.up, own).start()

        @pl.when(p.has_dn)
        def _():
            self.copy(p.x, p.d, 1, p.z, p.dn, own).start()

    def line(self, k):
        p = self.pos

        @pl.when(p.z - k >= 0)
        def _():
            zz = p.z - k
            self.wait(p.x, 2 * zz + p.y)

            @pl.when(p.has_up)
            def _():
                self.copy(p.x, 2 * zz + p.y, 0, zz, p.up).start()

            self.copy(p.x, 2 * zz + p.y, 2, zz, p.p1).start()
            self.copy(p.x, 2 * zz + p.y, 3, zz, p.p2).start()

        @pl.when(p.z + k <= 3)
        def _():
            zz = p.z + k
            self.wait(p.x, 2 * zz + p.y)

            @pl.when(p.has_dn)
            def _():
                self.copy(p.x, 2 * zz + p.y, 1, zz, p.dn).start()

            self.copy(p.x, 2 * zz + p.y, 2, zz, p.p1).start()
            self.copy(p.x, 2 * zz + p.y, 3, zz, p.p2).start()

    def side(self, k):
        p = self.pos

        def forward(zz):
            self.wait(p.x1, 2 * zz + p.y1)
            self.copy(p.x1, 2 * zz + p.y1, 4, zz, p.p2).start()

        if k == 0:
            forward(p.z)
            return

        @pl.when(p.z - k >= 0)
        def _():
            forward(p.z - k)

        @pl.when(p.z + k <= 3)
        def _():
            forward(p.z + k)

    def step(self, k):
        if k == 0:
            self.start()
        if 1 <= k <= 3:
            self.line(k)
        if k >= 1:
            self.side(k - 1)

    def finish(self):
        p = self.pos
        for zz in range(4):
            self.wait(p.x2, 2 * zz + p.y2)
            self.wait(1 - p.x, 2 * zz + 1 - p.y)

    def drain(self):
        p = self.pos
        for zz in range(4):
            dd = 2 * zz + p.y

            @pl.when(p.has_up & (zz <= p.z))
            def _():
                self.copy(p.x, dd, 0, zz, p.up).wait_send()

            @pl.when(p.has_dn & (zz >= p.z))
            def _():
                self.copy(p.x, dd, 1, zz, p.dn).wait_send()

            self.copy(p.x, dd, 2, zz, p.p1).wait_send()
            self.copy(p.x, dd, 3, zz, p.p2).wait_send()
            self.copy(p.x1, 2 * zz + p.y1, 4, zz, p.p2).wait_send()


class Reduce:
    def __init__(self, pos, g, part, r2, rz, ssem, rsem):
        self.pos, self.g, self.part, self.r2, self.rz = pos, g, part, r2, rz
        self.ssem, self.rsem = ssem, rsem

    def copy(self, src, dst, link, zz, dev):
        return pltpu.make_async_remote_copy(
            src_ref=src,
            dst_ref=dst,
            send_sem=self.ssem.at[self.g, link, zz],
            recv_sem=self.rsem.at[self.g, link, zz],
            device_id=dev,
            device_id_type=MESH,
        )

    def to_p2(self, which, zz):
        p = self.pos
        b, dd = (p.x2, 2 * zz + p.y2) if which == 0 else (1 - p.x, 2 * zz + 1 - p.y)
        return self.copy(self.part.at[b, dd], self.r2.at[which, zz], which, zz, p.p2)

    def to_p1(self, zz):
        p = self.pos
        return self.copy(self.part.at[p.x1, 2 * zz + p.y1], self.rz.at[0, zz], 2, zz, p.p1)

    def to_z(self, way, zz):
        p = self.pos
        return self.copy(
            self.part.at[p.x, 2 * zz + p.y], self.rz.at[1 + way, zz], 3 + way, zz, p.dn if way else p.up
        )

    def add(self, b, dd, other):
        total = self.part[b, dd].astype(F32) + other.astype(F32)
        self.part[b, dd] = total.astype(self.part.dtype)

    def start(self):
        for which in (1, 0):
            for zz in range(4):
                self.to_p2(which, zz).start()

    def mid1(self):
        p = self.pos
        for zz in range(4):
            self.to_p2(1, zz).wait_recv()
            self.add(p.x1, 2 * zz + p.y1, self.r2[1, zz])
            self.to_p1(zz).start()

    def mid0(self):
        p = self.pos
        for zz in range(4):
            self.to_p2(0, zz).wait_recv()
            self.add(p.x, 2 * zz + p.y, self.r2[0, zz])

    def join(self):
        p = self.pos
        for zz in range(4):
            self.to_p1(zz).wait_recv()
            self.add(p.x, 2 * zz + p.y, self.rz[0, zz])

    def chain(self):
        p = self.pos
        for zz in (3, 2, 1):

            @pl.when(zz > p.z)
            def _():
                @pl.when(p.has_dn)
                def _():
                    self.to_z(0, zz).wait_recv()
                    self.add(p.x, 2 * zz + p.y, self.rz[1, zz])

                self.to_z(0, zz).start()

            dz = 3 - zz

            @pl.when(dz < p.z)
            def _():
                @pl.when(p.has_up)
                def _():
                    self.to_z(1, dz).wait_recv()
                    self.add(p.x, 2 * dz + p.y, self.rz[2, dz])

                self.to_z(1, dz).start()

    def finish(self, out):
        p = self.pos
        out[...] = self.part[p.x, p.d].astype(F32)

        @pl.when(p.has_dn)
        def _():
            self.to_z(0, p.z).wait_recv()
            out[...] += self.rz[1, p.z].astype(F32)

        @pl.when(p.has_up)
        def _():
            self.to_z(1, p.z).wait_recv()
            out[...] += self.rz[2, p.z].astype(F32)

    def drain(self):
        p = self.pos
        for zz in range(4):
            self.to_p2(1, zz).wait_send()
            self.to_p2(0, zz).wait_send()
            self.to_p1(zz).wait_send()

            @pl.when(zz > p.z)
            def _():
                self.to_z(0, zz).wait_send()

            @pl.when(zz < p.z)
            def _():
                self.to_z(1, zz).wait_send()


def rows(start, size):
    return pl.ds(pl.multiple_of(start, size), size)


def swap(pos, src, dst, sems, i):
    return pltpu.make_async_remote_copy(
        src_ref=src,
        dst_ref=dst,
        send_sem=sems.at[0, i],
        recv_sem=sems.at[1, i],
        device_id=pos.sibling,
        device_id_type=MESH,
    )


def norm_stats(values):
    center = values - jnp.mean(values, -1, keepdims=True)
    inv = lax.rsqrt(jnp.mean(center * center, -1, keepdims=True) + EPSILON)
    return center * inv, inv


def lane_half(shape, which):
    lane = lax.broadcasted_iota(jnp.int32, shape, 1)
    return (lane < HEAD_DIM) if which == 0 else (lane >= HEAD_DIM)


def only(values, which):
    return jnp.where(lane_half(values.shape, which), values, jnp.zeros_like(values))


def roll_half(values):
    return pltpu.roll(values.astype(F32), HEAD_DIM, 1).astype(BF16)


def unpack_heads(raw, wh):
    @pl.loop(0, NB)
    def _(dd):
        at = pl.multiple_of(dd * RB, 16)
        for part in range(4):
            wh[part, 0, pl.ds(at, RB)] = raw[0, dd, part, 0:96]
            wh[part, 1, pl.ds(at, RB)] = raw[1, dd, part, 0:96]
            first, second = raw[0, dd, part, 96:144], raw[1, dd, part, 96:144]
            left = lane_half(first.shape, 0)
            wh[part, 2, pl.ds(at, 48)] = jnp.where(left, first, roll_half(second))
            wh[part, 2, pl.ds(at + 48, 48)] = jnp.where(left, roll_half(first), second)


def pack_heads(gh, raw):
    @pl.loop(0, NB)
    def _(dd):
        at = pl.multiple_of(dd * RB, 16)
        for part in range(4):
            raw[0, dd, part, 0:96] = gh[part, 0, pl.ds(at, RB)]
            raw[1, dd, part, 0:96] = gh[part, 1, pl.ds(at, RB)]
            top, bottom = gh[part, 2, pl.ds(at, 48)], gh[part, 2, pl.ds(at + 48, 48)]
            left = lane_half(top.shape, 0)
            raw[0, dd, part, 96:144] = jnp.where(left, top, roll_half(bottom))
            raw[1, dd, part, 96:144] = jnp.where(left, roll_half(top), bottom)


def cat_pairs(ref, parts, pick):
    return jnp.concatenate([pick(ref, part, pair) for part in parts for pair in range(3)], axis=1)


def transpose_rows(src, dst):
    @pl.loop(0, LENGTH // 128)
    def _(i):
        r = rows(i * 128, 128)
        dst[:, r] = src[r, :].T


def forward_kernel(net, scale_tokens, nin, *refs):
    hid, cot, ids, table, weights, *given = refs[:nin]
    refs = refs[nin - 9 :]
    (o_block, o_counts, o_param, o_mid, o_heads, o_up, o_down, o_nrmT, o_qkv, o_lse, o_ctx, o_n2T, o_act, o_slope, o_ups, o_upsT) = refs[9:25]
    (
        v_small, v_raw, v_up, v_down, v_heads, v_param, v_counts, v_cnt, v_nrm, v_nrmT, v_qkv, v_lse, v_ctx,
        v_mid, v_n2, v_n2T, v_act, v_slope, v_ups, v_upsT, v_send, v_recv, v_acc, v_block, own1,
        ssem, rsem, swsem, osem,
    ) = refs[25:]
    pos = Place()
    c = pos.c
    mine = c * HALF
    theirs = HALF - mine
    lanes = lax.broadcasted_iota(jnp.int32, (HALF, 128), 1)
    row_ids = jnp.broadcast_to(ids[...].astype(F32), (128, HALF)).T
    member = row_ids == lanes.astype(F32)
    own_counts = jnp.sum(member.astype(F32), 0, keepdims=True)

    puts = []

    def put(src, dst):
        cp = pltpu.make_async_copy(src, dst, osem.at[len(puts)])
        cp.start()
        puts.append(cp)

    if net:
        qkv_w, out_w, own2, own3, *vectors = given
        v_cnt[2] = jnp.zeros((8, 128), F32)
        for i in range(4):
            v_cnt[2, i : i + 1, 0:RB] = vectors[i][...].astype(F32)
        v_cnt[2, 4:5, :] = own_counts
        for part in range(4):
            block = qkv_w[part] if part < 3 else out_w[...].T
            own1[part, 0:RB] = block[:, 0:128]
            own1[part, RB:HEADROWS] = jnp.concatenate([block[0:48, 128:192], block[48:96, 128:192]], axis=1)
        entry_barrier(pos, net)
        g0 = Gather(pos, 0, v_cnt.at[2], v_small, ssem, rsem)
        g1 = Gather(pos, 1, own1, v_raw, ssem, rsem)
        g2 = Gather(pos, 2, own2, v_up, ssem, rsem)
        g3 = Gather(pos, 3, own3, v_down, ssem, rsem)
        g0.step(0)
        g1.step(0)
        v_small[pos.x, pos.d] = v_cnt[2]
        v_raw[pos.x, pos.d] = own1[...]
        v_up[pos.x, pos.d] = own2[...]
        v_down[pos.x, pos.d] = own3[...]
        for k in (1, 2, 3):
            g0.step(k)
            g1.step(k)
        g2.step(0)
        g0.step(4)
        g1.step(4)
        g0.finish()
        v_param[...] = jnp.zeros_like(v_param)
        total = jnp.zeros((8, 128), F32)
        for dd in range(NB):
            row = lax.broadcasted_iota(jnp.int32, (128, D), 0)
            col = lax.broadcasted_iota(jnp.int32, (128, D), 1)
            place = ((col == row + RB * dd) & (row < RB)).astype(BF16)
            block = v_small[pos.x, dd]
            v_param[...] += mm(block.astype(BF16), place)
            total += v_small[0, dd] + v_small[1, dd]
        v_cnt[0] = total
        swap(pos, v_cnt.at[0], v_cnt.at[1], swsem, 0).start()
    else:
        small, in1, in2, in3 = given
        entry_barrier(pos, net)
        v_param[...] = small[...]
        cps = [
            pltpu.make_async_copy(in1, v_raw, osem.at[16]),
            pltpu.make_async_copy(in2, v_up, osem.at[17]),
            pltpu.make_async_copy(in3, v_down, osem.at[18]),
        ]
        for cp in cps:
            cp.start()
        for cp in cps:
            cp.wait()

    @pl.loop(0, HALF // 64)
    def _(i):
        r = rows(i * 64, 64)
        hat, _inv = norm_stats(hid[r, :].astype(F32))
        normed = hat * v_param[0:1, :] + v_param[1:2, :]
        v_nrm[rows(mine + i * 64, 64), :] = normed.astype(BF16)

    swap_nrm = swap(pos, v_nrm.at[rows(mine, HALF)], v_nrm.at[rows(mine, HALF)], swsem, 1)
    swap_nrm.start()

    if net:
        swap(pos, v_cnt.at[0], v_cnt.at[1], swsem, 0).wait()
        counts = (v_cnt[0] + v_cnt[1])[4:5, :]
        v_counts[...] = jnp.full(v_counts.shape, -1, jnp.int32)
        v_counts[0:1, 0:GROUPS] = table[...]
        index = v_counts[0:1, :]
        weight = jnp.zeros((1, 128), F32)
        for r in range(TABLE):
            weight = weight + jnp.where(index == r, weights[r], 0.0)
        group_scale = weight * scale_tokens / jnp.maximum(counts, 1.0)
        o_counts[...] = counts[:, 0:GROUPS]
    else:
        o_counts[...] = table[...]
        group_scale = weights[0:1, :]

    row_scale = jnp.sum(jnp.where(member, group_scale, 0.0), 1, keepdims=True)
    v_ups[rows(mine, HALF), :] = (cot[...].astype(F32) * row_scale).astype(BF16)
    swap_ups = swap(pos, v_ups.at[rows(mine, HALF)], v_ups.at[rows(mine, HALF)], swsem, 2)
    swap_ups.start()

    if net:
        g2.step(1)
        g2.step(2)
        g1.finish()
    unpack_heads(v_raw, v_heads)
    put(v_heads, o_heads)
    put(v_param, o_param)

    for half, start in enumerate((mine, theirs)):
        if half == 1:
            swap(pos, v_nrm.at[rows(theirs, HALF)], v_nrm.at[rows(theirs, HALF)], swsem, 1).wait_recv()
        lhs = v_nrm[rows(start, HALF), :]
        for part in range(3):
            rhs = cat_pairs(v_heads, (part,), lambda ref, a, b: ref[a, b])
            res = mm(lhs, rhs).astype(BF16)
            if part == 0:
                res = (res.astype(F32) * HEAD_DIM**-0.5).astype(BF16)
            for pair in range(3):
                v_qkv[3 * part + pair, rows(start, HALF), :] = res[:, 128 * pair : 128 * pair + 128]
    put(v_qkv, o_qkv)
    if net:
        g2.step(3)
        g3.step(0)

    @pl.loop(0, 3)
    def _(pair):
        if net:

            @pl.when(pair == 1)
            def _():
                g2.step(4)
                g3.step(1)

            @pl.when(pair == 2)
            def _():
                g3.step(2)

        for i in range(4):
            n = 256 * (i + 1)
            q = v_qkv[pair, 256 * i : n, :]
            out = jnp.zeros((256, 128), F32)
            for h in range(2):
                pieces = []
                peak = None
                for j in range(i + 1):
                    k = only(v_qkv[3 + pair, 256 * j : 256 * j + 256, :], h)
                    s = mm(k, q, NT)
                    if j == i:
                        key = lax.broadcasted_iota(jnp.int32, s.shape, 0)
                        query = lax.broadcasted_iota(jnp.int32, s.shape, 1)
                        s = jnp.where(key <= query, s, MASKED_SCORE)
                    top = jnp.max(s, 0, keepdims=True)
                    peak = top if peak is None else jnp.maximum(peak, top)
                    pieces.append(s)
                total = jnp.zeros((1, 256), F32)
                for j in range(i + 1):
                    e = jnp.exp(pieces[j] - peak)
                    total += jnp.sum(e, 0, keepdims=True)
                    pieces[j] = e
                inv = 1.0 / total
                for j in range(i + 1):
                    v = only(v_qkv[6 + pair, 256 * j : 256 * j + 256, :], h)
                    out += mm((pieces[j] * inv).astype(BF16), v, TN)
                v_lse[pair, h : h + 1, 256 * i : n] = peak + jnp.log(total)
            v_ctx[pair, 256 * i : n, :] = out.astype(BF16)

    put(v_lse, o_lse)
    put(v_ctx, o_ctx)
    if net:
        g3.step(3)

    w_out = cat_pairs(v_heads, (3,), lambda ref, a, b: ref[a, b])
    for half, start in enumerate((theirs, mine)):
        lhs = jnp.concatenate([v_ctx[pair, rows(start, HALF), :] for pair in range(3)], axis=1)
        res = mm(lhs, w_out, NT)
        if half == 0:
            v_send[0] = res.astype(BF16)
            swap(pos, v_send.at[0], v_recv.at[0], swsem, 3).start()
        else:
            v_acc[...] = res
    transpose_rows(v_nrm, v_nrmT)
    put(v_nrmT, o_nrmT)
    swap(pos, v_send.at[0], v_recv.at[0], swsem, 3).wait()

    @pl.loop(0, HALF // 64)
    def _(i):
        r = rows(i * 64, 64)
        middle = hid[r, :].astype(F32) + v_acc[r, :] + v_recv[0, r, :].astype(F32)
        v_mid[r, :] = middle
        hat, _inv = norm_stats(middle)
        v_n2[rows(mine + i * 64, 64), :] = (hat * v_param[2:3, :] + v_param[3:4, :]).astype(BF16)

    swap(pos, v_n2.at[rows(mine, HALF)], v_n2.at[rows(mine, HALF)], swsem, 4).start()
    put(v_mid, o_mid)
    if net:
        g3.step(4)
        g2.finish()
    put(v_up, o_up)

    for half, start in enumerate((mine, theirs)):
        if half == 1:
            swap(pos, v_n2.at[rows(theirs, HALF)], v_n2.at[rows(theirs, HALF)], swsem, 4).wait_recv()

        @pl.loop(0, 6)
        def _(tile):
            b = lax.div(tile, 3)
            cols = pl.ds(pl.multiple_of(lax.rem(tile, 3) * 256, 256), 256)
            pre = mm(v_n2[rows(start, HALF), :], v_up[b, :, :, cols].reshape(D, 256))
            square = pre * pre
            bend = jnp.tanh(GELU_C * pre * (1.0 + GELU_A * square))
            v_act[b, rows(start, HALF), cols] = (0.5 * pre * (1.0 + bend)).astype(BF16)
            slope = 0.5 * (1.0 + bend) + 0.5 * pre * (1.0 - bend * bend) * (GELU_C * (1.0 + 3.0 * GELU_A * square))
            v_slope[b, rows(start, HALF), cols] = slope.astype(BF16)

    put(v_act, o_act)
    put(v_slope, o_slope)
    transpose_rows(v_n2, v_n2T)
    put(v_n2T, o_n2T)
    swap(pos, v_ups.at[rows(theirs, HALF)], v_ups.at[rows(theirs, HALF)], swsem, 2).wait_recv()
    put(v_ups, o_ups)
    transpose_rows(v_ups, v_upsT)
    put(v_upsT, o_upsT)
    if net:
        g3.finish()
    put(v_down, o_down)
    for half, start in enumerate((theirs, mine)):
        res = mm(v_act[0, rows(start, HALF), :], v_down[0].reshape(D, D), NT)
        res += mm(v_act[1, rows(start, HALF), :], v_down[1].reshape(D, D), NT)
        if half == 0:
            v_send[1] = res.astype(BF16)
            swap(pos, v_send.at[1], v_recv.at[1], swsem, 5).start()
        else:
            v_acc[...] = res
    swap(pos, v_send.at[1], v_recv.at[1], swsem, 5).wait()
    v_block[...] = v_mid[...] + v_acc[...] + v_recv[1].astype(F32)
    put(v_block, o_block)
    for i, ref in ((1, v_nrm), (2, v_ups), (4, v_n2)):
        swap(pos, ref.at[rows(mine, HALF)], ref.at[rows(mine, HALF)], swsem, i).wait_send()
    if net:
        for g in (g0, g1, g2, g3):
            g.drain()
    for cp in puts:
        cp.wait()


def backward_kernel(net, *refs):
    (hid, param, h_mid, h_heads, h_up, h_down, h_nrmT, h_qkv, h_lse, h_ctx, h_n2T, h_act, h_slope, h_ups, h_upsT) = refs[:15]
    nout = 6
    o_in, o_small, o1, o_out, o2, o3 = refs[15 : 15 + nout]
    (
        v_mid, v_heads, v_up, v_down, v_nrmT, v_qkv, v_lse, v_ctx, v_n2T, v_act, v_slope, v_ups, v_upsT,
        v_low, v_dmid, v_dctx, v_dqkv, v_dk, v_dv, v_acc, v_send, v_recv, v_gh, v_p0, v_p1, v_p2, v_p3,
        v_sums, v_swap, v_own, *nets,
    ) = refs[15 + nout :]
    swsem, lsem = nets[-2:]
    pos = Place()
    c = pos.c
    mine = c * HALF
    theirs = HALF - mine
    loads = {}
    for i, (src, dst) in enumerate(
        ((h_upsT, v_upsT), (h_act, v_act), (h_ups, v_ups), (h_down, v_down), (h_slope, v_slope), (h_n2T, v_n2T), (h_up, v_up),
         (h_mid, v_mid), (h_heads, v_heads), (h_ctx, v_ctx), (h_qkv, v_qkv), (h_lse, v_lse), (h_nrmT, v_nrmT))
    ):
        cp = pltpu.make_async_copy(src, dst, lsem.at[i])
        cp.start()
        loads[id(dst)] = cp
    loaded = lambda *which: [loads[id(w)].wait() for w in which]
    entry_barrier(pos, net)
    if net:
        r2_0, rz_0, r2_1, rz_1, r2_2, rz_2, r2_3, rz_3, ssem, rsem = nets[:-2]
        s0 = Reduce(pos, 0, v_p0, r2_0, rz_0, ssem, rsem)
        s1 = Reduce(pos, 1, v_p1, r2_1, rz_1, ssem, rsem)
        s2 = Reduce(pos, 2, v_p2, r2_2, rz_2, ssem, rsem)
        s3 = Reduce(pos, 3, v_p3, r2_3, rz_3, ssem, rsem)

    def tile_of(tile):
        return lax.div(tile, 3), pl.ds(pl.multiple_of(lax.rem(tile, 3) * 256, 256), 256)

    loaded(v_upsT, v_act)

    @pl.loop(0, 6)
    def _(tile):
        b, cols = tile_of(tile)
        res = mm(v_upsT[...], v_act[b, :, cols])
        v_p3[b, :, :, cols] = res.astype(BF16).reshape(NB, RB, 256)

    if net:
        s3.start()
    loaded(v_ups, v_down, v_slope, v_n2T)

    @pl.loop(0, 6)
    def _(tile):
        b, cols = tile_of(tile)
        res = mm(v_ups[...], v_down[b, :, :, cols].reshape(D, 256))
        pre = (res * v_slope[b, :, cols].astype(F32)).astype(BF16)
        v_slope[b, :, cols] = pre
        res = mm(v_n2T[...], pre)
        v_p2[b, :, :, cols] = res.astype(BF16).reshape(NB, RB, 256)

    if net:
        s2.start()
    loaded(v_up, v_mid)
    for half, start in enumerate((theirs, mine)):
        res = mm(v_slope[0, rows(start, HALF), :], v_up[0].reshape(D, D), NT)
        res += mm(v_slope[1, rows(start, HALF), :], v_up[1].reshape(D, D), NT)
        if half == 0:
            v_send[0] = res.astype(BF16)
            swap(pos, v_send.at[0], v_recv.at[0], swsem, 0).start()
        else:
            v_acc[...] = res
    if net:
        s3.mid1()
    swap(pos, v_send.at[0], v_recv.at[0], swsem, 0).wait()
    v_sums[...] = jnp.zeros_like(v_sums)

    def norm_back(upper, values, gain, at):
        hat, inv = norm_stats(values)
        scaled = upper * gain
        first = jnp.mean(scaled, -1, keepdims=True)
        second = jnp.mean(scaled * hat, -1, keepdims=True)
        v_sums[at : at + 1, :] += jnp.sum(upper * hat, 0, keepdims=True)
        v_sums[at + 1 : at + 2, :] += jnp.sum(upper, 0, keepdims=True)
        return inv * (scaled - first - hat * second)

    @pl.loop(0, HALF // 64)
    def _(i):
        r = rows(i * 64, 64)
        upper = v_acc[r, :] + v_recv[0, r, :].astype(F32)
        wide = rows(mine + i * 64, 64)
        d_mid = v_ups[wide, :].astype(F32) + norm_back(upper, v_mid[r, :], param[2:3, :], 2)
        v_dmid[r, :] = d_mid
        v_low[wide, :] = d_mid.astype(BF16)

    swap(pos, v_low.at[rows(mine, HALF)], v_low.at[rows(mine, HALF)], swsem, 1).start()
    loaded(v_heads, v_ctx)
    w_out = cat_pairs(v_heads, (3,), lambda ref, a, b: ref[a, b])
    for half, start in enumerate((mine, theirs)):
        if half == 1:
            swap(pos, v_low.at[rows(theirs, HALF)], v_low.at[rows(theirs, HALF)], swsem, 1).wait_recv()
        res = mm(v_low[rows(start, HALF), :], w_out).astype(BF16)
        for pair in range(3):
            v_dctx[pair, rows(start, HALF), :] = res[:, 128 * pair : 128 * pair + 128]
    transpose_rows(v_low, v_upsT)
    res = mm(v_upsT[...], jnp.concatenate([v_ctx[pair] for pair in range(3)], axis=1)).astype(BF16)
    for pair in range(3):
        v_gh[3, pair] = res[:, 128 * pair : 128 * pair + 128]
    if net:
        s3.mid0()
    loaded(v_qkv, v_lse, v_nrmT)

    @pl.loop(0, 3)
    def _(pair):
        if net:

            @pl.when(pair == 2)
            def _():
                s3.join()
                s2.mid1()

        v_dk[...] = jnp.zeros_like(v_dk)
        v_dv[...] = jnp.zeros_like(v_dv)
        for i in range(4):
            n = 256 * (i + 1)
            q = v_qkv[pair, 256 * i : n, :]
            up = v_dctx[pair, 256 * i : n, :]
            qs = [only(q, h) for h in range(2)]
            ups = [only(up, h) for h in range(2)]
            dq = jnp.zeros((256, 128), F32)
            probs = [[], []]
            grads = [[], []]
            for h in range(2):
                lse = v_lse[pair, h : h + 1, 256 * i : n]
                delta = jnp.zeros((1, 256), F32)
                for j in range(i + 1):
                    at = slice(256 * j, 256 * j + 256)
                    s = mm(v_qkv[3 + pair, at, :], qs[h], NT)
                    p = jnp.exp(s - lse)
                    if j == i:
                        key = lax.broadcasted_iota(jnp.int32, s.shape, 0)
                        query = lax.broadcasted_iota(jnp.int32, s.shape, 1)
                        p = jnp.where(key <= query, p, 0.0)
                    dp = mm(v_qkv[6 + pair, at, :], ups[h], NT)
                    delta += jnp.sum(p * dp, 0, keepdims=True)
                    probs[h].append(p)
                    grads[h].append(dp)
                for j in range(i + 1):
                    grads[h][j] = (probs[h][j] * (grads[h][j] - delta)).astype(BF16)
                    probs[h][j] = probs[h][j].astype(BF16)
            for j in range(i + 1):
                at = slice(256 * j, 256 * j + 256)
                for h in range(2):
                    k = only(v_qkv[3 + pair, at, :], h)
                    dq += mm(grads[h][j], k, TN)
                v_dv[at, :] += mm(
                    jnp.concatenate([probs[0][j], probs[1][j]], axis=1), jnp.concatenate(ups, axis=0)
                )
                v_dk[at, :] += mm(
                    jnp.concatenate([grads[0][j], grads[1][j]], axis=1), jnp.concatenate(qs, axis=0)
                )
            v_dqkv[pair, 256 * i : n, :] = (dq * HEAD_DIM**-0.5).astype(BF16)
        v_dqkv[3 + pair] = v_dk[...].astype(BF16)
        v_dqkv[6 + pair] = v_dv[...].astype(BF16)

    for part in range(3):
        res = mm(v_nrmT[...], jnp.concatenate([v_dqkv[3 * part + pair] for pair in range(3)], axis=1)).astype(BF16)
        for pair in range(3):
            v_gh[part, pair] = res[:, 128 * pair : 128 * pair + 128]
    pack_heads(v_gh, v_p1)
    if net:
        s1.start()
    w_qkv = cat_pairs(v_heads, (0, 1, 2), lambda ref, a, b: ref[a, b])
    for half, start in enumerate((theirs, mine)):
        lhs = jnp.concatenate([v_dqkv[j, rows(start, HALF), :] for j in range(9)], axis=1)
        res = mm(lhs, w_qkv, NT)
        if half == 0:
            v_send[1] = res.astype(BF16)
            swap(pos, v_send.at[1], v_recv.at[1], swsem, 2).start()
        else:
            v_acc[...] = res
    if net:
        s3.chain()
        s2.mid0()
    swap(pos, v_send.at[1], v_recv.at[1], swsem, 2).wait()

    @pl.loop(0, HALF // 64)
    def _(i):
        r = rows(i * 64, 64)
        upper = v_acc[r, :] + v_recv[1, r, :].astype(F32)
        o_in[r, :] = v_dmid[r, :] + norm_back(upper, hid[r, :].astype(F32), param[0:1, :], 0)

    v_swap[0] = v_sums[...]
    swap(pos, v_swap.at[0], v_swap.at[1], swsem, 3).start()
    swap(pos, v_swap.at[0], v_swap.at[1], swsem, 3).wait()
    both = v_swap[0] + v_swap[1]
    if net:
        for dd in range(NB):
            piece = jnp.concatenate([both[:, RB * dd : RB * dd + RB], jnp.zeros((8, 128 - RB), F32)], axis=1)
            v_p0[0, dd] = piece
            v_p0[1, dd] = piece
        s0.start()
        s1.mid1()
        s2.join()
        s2.chain()
        s3.finish(o3)
        s1.mid0()
        s0.mid1()
        s0.mid0()
        s1.join()
        s1.chain()
        s0.join()
        s0.chain()
        s2.finish(o2)
        s1.finish(v_own)
        s0.finish(v_swap.at[0, :, 0:128])
        for part in range(4):
            tail = v_own[part, RB:HEADROWS]
            block = jnp.concatenate([tail[:, 0:64], tail[:, 64:128]], axis=0)
            whole_rows = jnp.concatenate([v_own[part, 0:RB], block], axis=1)
            if part < 3:
                o1[part] = whole_rows
            else:
                o_out[...] = whole_rows.T
        o_small[...] = pltpu.roll(v_swap[0, :, 0:128], lax.rem(128 - 24 * pos.t, 128), 1)[:, 0:24]
        for s in (s0, s1, s2, s3):
            s.drain()
    else:
        o_small[...] = both
        o_out[...] = jnp.zeros_like(o_out)
        o1[...] = v_p1[...]
        o2[...] = v_p2[...]
        o3[...] = v_p3[...]
    swap(pos, v_low.at[rows(mine, HALF)], v_low.at[rows(mine, HALF)], swsem, 1).wait_send()


def pack_rows(block):
    third = block[:, :, 128:].reshape(4, 2, 48, 64).transpose(0, 2, 1, 3).reshape(4, 48, 128)
    return jnp.concatenate([block[:, :, :128], third], axis=1)


def unpack_rows(packed):
    third = packed[:, 96:].reshape(4, 48, 2, 64).transpose(0, 2, 1, 3).reshape(4, 96, 64)
    return jnp.concatenate([packed[:, :96], third], axis=2)


def shards(
    hidden_in, cotangent, group_ids, weight_table, table_index, qkv_weight, out_weight, up_weight, down_weight,
    norm1_gain, norm1_bias, norm2_gain, norm2_bias,
):
    n_dp, n_t = lax.axis_size("dp"), lax.axis_size("tensor")
    net = n_dp == NB and n_t == 4
    t = lax.axis_index("tensor")
    core = lax.rem(t, 2)
    tokens = hidden_in.shape[0] * n_dp * n_t
    scale_tokens = tokens / GROUPS
    ids = group_ids.reshape(1, HALF)
    down = down_weight.T
    vspec = pl.BlockSpec(memory_space=pltpu.VMEM)
    aspec = pl.BlockSpec(memory_space=pl.ANY)
    if net:
        vectors = [v.reshape(1, RB) for v in (norm1_gain, norm1_bias, norm2_gain, norm2_bias)]
        table, weights = table_index.reshape(1, GROUPS), weight_table
        given = [qkv_weight.transpose(1, 0, 2), out_weight, up_weight, down, *vectors]
        weight_spec = pl.BlockSpec(memory_space=pltpu.SMEM)
        given_specs = [vspec] * len(given)
    else:

        def whole(block, axis):
            full = lax.all_gather(block, "dp", axis=axis, tiled=True)
            every = lax.all_gather(full, "tensor", axis=0)
            pair = lax.dynamic_index_in_dim(every.reshape((n_t // 2, 2) + full.shape), core, 1, keepdims=False)
            return pair

        heads = jnp.concatenate([qkv_weight.transpose(1, 0, 2), out_weight.T[None]], axis=0)
        vectors = jnp.stack([norm1_gain, norm1_bias, norm2_gain, norm2_bias]).astype(F32)
        heads_all = whole(heads, 1).reshape(2, 4, NB, RB, 192).transpose(0, 2, 1, 3, 4)
        given = [
            jnp.pad(lax.all_gather(vectors, "dp", axis=1, tiled=True), ((0, 4), (0, 0))),
            jax.vmap(jax.vmap(pack_rows))(heads_all),
            whole(up_weight, 0).reshape(2, NB, RB, D),
            whole(down, 0).reshape(2, NB, RB, D),
        ]
        member = (group_ids[:, None] == jnp.arange(GROUPS, dtype=jnp.int32)[None, :]).astype(F32)
        counts = lax.psum(jnp.sum(member, 0), ("dp", "tensor"))
        hits = table_index[:, None] == jnp.arange(TABLE, dtype=jnp.int32)[None, :]
        scale = jnp.sum(jnp.where(hits, weight_table[None, :], 0.0), 1) * scale_tokens / jnp.maximum(counts, 1.0)
        weights = jnp.pad(scale[None, :], ((0, 7), (0, 128 - GROUPS)))
        table = counts.reshape(1, GROUPS)
        weight_spec = vspec
        given_specs = [vspec, aspec, aspec, aspec]

    def sds(shape, dtype=BF16):
        return jax.ShapeDtypeStruct(shape, dtype)

    saved = [
        sds((HALF, D), F32), sds((1, GROUPS), F32), sds((8, D), F32), sds((HALF, D), F32), sds((4, 3, D, 128)),
        sds((2, NB, RB, D)), sds((2, NB, RB, D)), sds((D, LENGTH)), sds((9, LENGTH, 128)), sds((3, 8, LENGTH), F32),
        sds((3, LENGTH, 128)), sds((D, LENGTH)), sds((2, LENGTH, D)), sds((2, LENGTH, D)), sds((LENGTH, D)), sds((D, LENGTH)),
    ]
    vm = pltpu.VMEM
    dma = pltpu.SemaphoreType.DMA
    outs = pl.pallas_call(
        functools.partial(forward_kernel, net, scale_tokens, 5 + len(given)),
        out_shape=saved,
        in_specs=[vspec, vspec, vspec, vspec, weight_spec, *given_specs],
        out_specs=[aspec, vspec] + [aspec] * (len(saved) - 2),
        scratch_shapes=[
            vm((2, NB, 8, 128), F32), vm((2, NB, 4, HEADROWS, 128), BF16), vm((2, NB, RB, D), BF16), vm((2, NB, RB, D), BF16),
            vm((4, 3, D, 128), BF16), vm((8, D), F32), vm((8, 128), jnp.int32), vm((3, 8, 128), F32),
            vm((LENGTH, D), BF16), vm((D, LENGTH), BF16), vm((9, LENGTH, 128), BF16), vm((3, 8, LENGTH), F32), vm((3, LENGTH, 128), BF16),
            vm((HALF, D), F32), vm((LENGTH, D), BF16), vm((D, LENGTH), BF16), vm((2, LENGTH, D), BF16), vm((2, LENGTH, D), BF16),
            vm((LENGTH, D), BF16), vm((D, LENGTH), BF16), vm((2, HALF, D), BF16), vm((2, HALF, D), BF16), vm((HALF, D), F32), vm((HALF, D), F32), vm((4, HEADROWS, 128), BF16),
            dma((4, 5, 4)), dma((4, 2, NB)), dma((2, 6)), dma((19,)),
        ],
        compiler_params=pltpu.CompilerParams(collective_id=0, has_side_effects=True, vmem_limit_bytes=VMEM_LIMIT),
        name="block_forward",
    )(hidden_in, cotangent, ids, table, weights, *given)
    (block_output, counts_out, param, mid, heads_w, up_w, down_w, nrmT, qkv, lse, ctx, n2T, act, slope, ups, upsT) = outs

    slot = [(8, 128), (4, HEADROWS, 128), (RB, D), (RB, D)]
    kind = [F32, BF16, BF16, BF16]
    net_scratch = []
    if net:
        for s, k in zip(slot, kind):
            net_scratch += [vm((2, 4) + s, k), vm((3, 4) + s, k)]
        net_scratch += [dma((4, 5, 4)), dma((4, 5, 4))]
        grad_shapes = [sds((8, 24), F32), sds((3, RB, 192), F32), sds((192, RB), F32), sds((RB, D), F32), sds((RB, D), F32)]
    else:
        slots = [sds((2, NB) + s) for s in slot[1:]]
        grad_shapes = [sds((8, D), F32), slots[0], sds((8, 128), F32), slots[1], slots[2]]
    out2 = pl.pallas_call(
        functools.partial(backward_kernel, net),
        out_shape=[sds((HALF, D), F32)] + grad_shapes,
        in_specs=[vspec, vspec] + [aspec] * 13,
        out_specs=[vspec] * 6,
        scratch_shapes=[
            vm((HALF, D), F32), vm((4, 3, D, 128), BF16), vm((2, NB, RB, D), BF16), vm((2, NB, RB, D), BF16), vm((D, LENGTH), BF16),
            vm((9, LENGTH, 128), BF16), vm((3, 8, LENGTH), F32), vm((3, LENGTH, 128), BF16), vm((D, LENGTH), BF16),
            vm((2, LENGTH, D), BF16), vm((2, LENGTH, D), BF16), vm((LENGTH, D), BF16), vm((D, LENGTH), BF16),
            vm((LENGTH, D), BF16), vm((HALF, D), F32), vm((3, LENGTH, 128), BF16), vm((9, LENGTH, 128), BF16),
            vm((LENGTH, 128), F32), vm((LENGTH, 128), F32), vm((HALF, D), F32), vm((2, HALF, D), BF16), vm((2, HALF, D), BF16),
            vm((4, 3, D, 128), BF16), vm((2, NB, 8, 128), F32), vm((2, NB, 4, HEADROWS, 128), BF16), vm((2, NB, RB, D), BF16), vm((2, NB, RB, D), BF16),
            vm((8, D), F32), vm((2, 8, D), F32), vm((4, HEADROWS, 128), F32),
            *net_scratch, dma((2, 4)), dma((13,)),
        ],
        compiler_params=pltpu.CompilerParams(collective_id=1, has_side_effects=True, vmem_limit_bytes=VMEM_LIMIT),
        name="block_backward",
    )(hidden_in, param, mid, heads_w, up_w, down_w, nrmT, qkv, lse, ctx, n2T, act, slope, ups, upsT)
    input_grad, sums, g1, grad_out, g2, g3 = out2
    if net:
        norms = [sums[i] for i in range(4)]
        grad_qkv, grad_up, grad_down = g1, g2, g3
    else:

        def owned(part):
            base = jnp.zeros((n_t // 2, 2) + part.shape[1:], F32)
            base = lax.dynamic_update_index_in_dim(base, part.astype(F32), core, 1)
            flat = base.reshape((n_t,) + part.shape[1:])
            mine = lax.psum_scatter(flat, "tensor", scatter_dimension=0, tiled=False)
            return lax.psum_scatter(mine, "dp", scatter_dimension=0, tiled=True)

        gh = jax.vmap(jax.vmap(unpack_rows))(g1)
        gh = gh.transpose(0, 1, 3, 2, 4).reshape(2, D, 4, 192)
        grad_heads = owned(gh).transpose(1, 0, 2)
        grad_qkv, grad_out = grad_heads[:3], grad_heads[3].T
        grad_up, grad_down = owned(g2.reshape(2, D, D)), owned(g3.reshape(2, D, D))
        half_sums = jnp.where(core == 0, sums, 0.0)
        norms = [
            lax.psum_scatter(half_sums[i], ("dp", "tensor"), scatter_dimension=0, tiled=True) for i in range(4)
        ]
    return (
        block_output,
        input_grad,
        grad_qkv.transpose(1, 0, 2),
        grad_out,
        grad_up,
        grad_down.T,
        norms[0],
        norms[1],
        norms[2],
        norms[3],
        counts_out.reshape(GROUPS),
    )


def solution(mesh):
    both = ("dp", "tensor")
    return jax.shard_map(
        shards,
        mesh=mesh,
        in_specs=(
            P(both, None), P(both, None), P(both), P(), P(), P("dp", None, "tensor"), P("tensor", "dp"), P("dp", "tensor"),
            P("tensor", "dp"), P("dp"), P("dp"), P("dp"), P("dp"),
        ),
        out_specs=(
            P(both, None), P(both, None), P("dp", None, "tensor"), P("tensor", "dp"), P("dp", "tensor"), P("tensor", "dp"),
            P(both), P(both), P(both), P(both), P(),
        ),
        check_vma=False,
    )
```

```python
import functools

import jax
import jax.numpy as jnp
from jax import lax
from jax.experimental import pallas as pl
from jax.experimental.pallas import tpu as pltpu
from jax.sharding import PartitionSpec as P

D = 768
HEAD_DIM = 64
LENGTH = 1024
HALF = 512
GROUPS = 16
TABLE = 8
NB = 8
RB = D // NB
ORDER = (0, 3, 1, 2)
EPSILON = 1e-05
MASKED_SCORE = -1e30
GELU_C = 0.7978845608028654
GELU_A = 0.044715
MESH = pl.DeviceIdType.MESH
F32 = jnp.float32
BF16 = jnp.bfloat16
NT = (((1,), (1,)), ((), ()))
TN = (((0,), (0,)), ((), ()))
NN = (((1,), (0,)), ((), ()))
VMEM_LIMIT = 66_000_000


def mm(a, b, dims=NN):
    return lax.dot_general(a, b, dims, preferred_element_type=F32)


class Place:
    def __init__(self):
        self.d = lax.axis_index("dp")
        self.t = lax.axis_index("tensor")
        self.z = lax.div(self.d, 2)
        self.y = lax.rem(self.d, 2)
        self.x = lax.div(self.t, 2)
        self.c = lax.rem(self.t, 2)
        c = self.c
        self.sibling = (self.d, self.t + 1 - 2 * c)
        self.x1 = lax.rem(self.x + c, 2)
        self.y1 = lax.rem(self.y + 1 - c, 2)
        self.x2 = lax.rem(self.x + 1 - c, 2)
        self.y2 = lax.rem(self.y + c, 2)
        self.p1 = (2 * self.z + self.y1, 2 * self.x1 + c)
        self.p2 = (2 * self.z + self.y2, 2 * self.x2 + c)
        self.up = (self.d + 2, self.t)
        self.dn = (self.d - 2, self.t)
        self.has_up = self.z < 3
        self.has_dn = self.z > 0


def entry_barrier(pos, net):
    bar = pltpu.get_barrier_semaphore()
    pl.semaphore_signal(bar, inc=1, device_id=pos.sibling, device_id_type=MESH)
    if not net:
        pl.semaphore_wait(bar, 1)
        return
    pl.semaphore_signal(bar, inc=1, device_id=pos.p1, device_id_type=MESH)
    pl.semaphore_signal(bar, inc=1, device_id=pos.p2, device_id_type=MESH)

    @pl.when(pos.has_up)
    def _():
        pl.semaphore_signal(bar, inc=1, device_id=pos.up, device_id_type=MESH)

    @pl.when(pos.has_dn)
    def _():
        pl.semaphore_signal(bar, inc=1, device_id=pos.dn, device_id_type=MESH)

    pl.semaphore_wait(bar, 3 + jnp.where(pos.has_up, 1, 0) + jnp.where(pos.has_dn, 1, 0))


class Gather:
    def __init__(self, pos, g, own, full, ssem, rsem):
        self.pos, self.g, self.own, self.full = pos, g, own, full
        self.ssem, self.rsem = ssem, rsem

    def copy(self, b, dd, link, zz, dev, src=None):
        slot = self.full.at[b, dd]
        return pltpu.make_async_remote_copy(
            src_ref=slot if src is None else src,
            dst_ref=slot,
            send_sem=self.ssem.at[self.g, link, zz],
            recv_sem=self.rsem.at[self.g, b, dd],
            device_id=dev,
            device_id_type=MESH,
        )

    def wait(self, b, dd):
        self.copy(b, dd, 0, 0, self.pos.p1).wait_recv()

    def start(self):
        p = self.pos
        own = self.own
        self.copy(p.x, p.d, 2, p.z, p.p1, own).start()
        self.copy(p.x, p.d, 3, p.z, p.p2, own).start()

        @pl.when(p.has_up)
        def _():
            self.copy(p.x, p.d, 0, p.z, p.up, own).start()

        @pl.when(p.has_dn)
        def _():
            self.copy(p.x, p.d, 1, p.z, p.dn, own).start()

    def line(self, k):
        p = self.pos

        @pl.when(p.z - k >= 0)
        def _():
            zz = p.z - k
            self.wait(p.x, 2 * zz + p.y)

            @pl.when(p.has_up)
            def _():
                self.copy(p.x, 2 * zz + p.y, 0, zz, p.up).start()

            self.copy(p.x, 2 * zz + p.y, 2, zz, p.p1).start()
            self.copy(p.x, 2 * zz + p.y, 3, zz, p.p2).start()

        @pl.when(p.z + k <= 3)
        def _():
            zz = p.z + k
            self.wait(p.x, 2 * zz + p.y)

            @pl.when(p.has_dn)
            def _():
                self.copy(p.x, 2 * zz + p.y, 1, zz, p.dn).start()

            self.copy(p.x, 2 * zz + p.y, 2, zz, p.p1).start()
            self.copy(p.x, 2 * zz + p.y, 3, zz, p.p2).start()

    def side(self, k):
        p = self.pos

        def forward(zz):
            self.wait(p.x1, 2 * zz + p.y1)
            self.copy(p.x1, 2 * zz + p.y1, 4, zz, p.p2).start()

        if k == 0:
            forward(p.z)
            return

        @pl.when(p.z - k >= 0)
        def _():
            forward(p.z - k)

        @pl.when(p.z + k <= 3)
        def _():
            forward(p.z + k)

    def step(self, k):
        if k == 0:
            self.start()
        if 1 <= k <= 3:
            self.line(k)
        if k >= 1:
            self.side(k - 1)

    def finish(self):
        p = self.pos
        for zz in range(4):
            self.wait(p.x2, 2 * zz + p.y2)
            self.wait(1 - p.x, 2 * zz + 1 - p.y)

    def drain(self):
        p = self.pos
        for zz in range(4):
            dd = 2 * zz + p.y

            @pl.when(p.has_up & (zz <= p.z))
            def _():
                self.copy(p.x, dd, 0, zz, p.up).wait_send()

            @pl.when(p.has_dn & (zz >= p.z))
            def _():
                self.copy(p.x, dd, 1, zz, p.dn).wait_send()

            self.copy(p.x, dd, 2, zz, p.p1).wait_send()
            self.copy(p.x, dd, 3, zz, p.p2).wait_send()
            self.copy(p.x1, 2 * zz + p.y1, 4, zz, p.p2).wait_send()


class Reduce:
    def __init__(self, pos, g, slot, r2, rz, ssem, rsem):
        self.pos, self.g, self.slot, self.r2, self.rz = pos, g, slot, r2, rz
        self.ssem, self.rsem = ssem, rsem

    def copy(self, src, dst, link, zz, dev):
        return pltpu.make_async_remote_copy(
            src_ref=src,
            dst_ref=dst,
            send_sem=self.ssem.at[self.g, link, zz],
            recv_sem=self.rsem.at[self.g, link, zz],
            device_id=dev,
            device_id_type=MESH,
        )

    def to_p2(self, which, zz):
        p = self.pos
        b, dd = (p.x2, 2 * zz + p.y2) if which == 0 else (1 - p.x, 2 * zz + 1 - p.y)
        return self.copy(self.slot(b, dd), self.r2.at[which, zz], which, zz, p.p2)

    def to_p1(self, zz):
        p = self.pos
        return self.copy(self.slot(p.x1, 2 * zz + p.y1), self.rz.at[zz], 2, zz, p.p1)

    def to_z(self, way, zz):
        p = self.pos
        place = self.rz.at[4 + zz if way else 5 + zz]
        return self.copy(self.slot(p.x, 2 * zz + p.y), place, 3 + way, zz, p.dn if way else p.up)

    def add(self, b, dd, other):
        ref = self.slot(b, dd)
        ref[...] = (ref[...].astype(F32) + other.astype(F32)).astype(ref.dtype)

    def start(self):
        for which in (1, 0):
            for zz in ORDER:
                self.to_p2(which, zz).start()

    def mid1(self):
        p = self.pos
        for zz in ORDER:
            self.to_p2(1, zz).wait_recv()
            self.add(p.x1, 2 * zz + p.y1, self.r2[1, zz])
            self.to_p1(zz).start()

    def mid0(self):
        p = self.pos
        for zz in ORDER:
            self.to_p2(0, zz).wait_recv()
            self.add(p.x, 2 * zz + p.y, self.r2[0, zz])

    def join(self):
        p = self.pos
        for zz in ORDER:
            self.to_p1(zz).wait_recv()
            self.add(p.x, 2 * zz + p.y, self.rz[zz])

    def hop(self, h):
        p = self.pos
        for zz in range(3, h, -1):

            @pl.when(p.z == h)
            def _():
                if h > 0:
                    self.to_z(0, zz).wait_recv()
                    self.add(p.x, 2 * zz + p.y, self.rz[5 + zz])
                self.to_z(0, zz).start()

            dz = 3 - zz

            @pl.when(p.z == 3 - h)
            def _():
                if h > 0:
                    self.to_z(1, dz).wait_recv()
                    self.add(p.x, 2 * dz + p.y, self.rz[4 + dz])
                self.to_z(1, dz).start()

    def finish(self, out):
        p = self.pos
        out[...] = self.slot(p.x, p.d)[...].astype(F32)

        @pl.when(p.has_dn)
        def _():
            self.to_z(0, p.z).wait_recv()
            out[...] += self.rz[5 + p.z].astype(F32)

        @pl.when(p.has_up)
        def _():
            self.to_z(1, p.z).wait_recv()
            out[...] += self.rz[4 + p.z].astype(F32)

    def drain(self):
        p = self.pos
        for zz in range(4):
            self.to_p2(1, zz).wait_send()
            self.to_p2(0, zz).wait_send()
            self.to_p1(zz).wait_send()

            @pl.when(zz > p.z)
            def _():
                self.to_z(0, zz).wait_send()

            @pl.when(zz < p.z)
            def _():
                self.to_z(1, zz).wait_send()


def rows(start, size):
    return pl.ds(pl.multiple_of(start, size), size)


def swap(pos, src, dst, sems, i):
    return pltpu.make_async_remote_copy(
        src_ref=src,
        dst_ref=dst,
        send_sem=sems.at[0, i],
        recv_sem=sems.at[1, i],
        device_id=pos.sibling,
        device_id_type=MESH,
    )


def norm_stats(values):
    center = values - jnp.mean(values, -1, keepdims=True)
    inv = lax.rsqrt(jnp.mean(center * center, -1, keepdims=True) + EPSILON)
    return center * inv, inv


def lane_half(shape, which):
    lane = lax.broadcasted_iota(jnp.int32, shape, 1)
    return (lane < HEAD_DIM) if which == 0 else (lane >= HEAD_DIM)


def only(values, which):
    return jnp.where(lane_half(values.shape, which), values, jnp.zeros_like(values))


def roll_half(values):
    return pltpu.roll(values.astype(F32), HEAD_DIM, 1).astype(BF16)


def unpack_heads(raw, first, count, wh):
    @pl.loop(0, NB)
    def _(dd):
        at = pl.multiple_of(dd * RB, 16)
        for i in range(count):
            one, two = raw[0, dd, first + i], raw[1, dd, first + i]
            left = lane_half(one.shape, 0)
            wh[first + i, pl.ds(at, 48)] = jnp.where(left, one, roll_half(two))
            wh[first + i, pl.ds(at + 48, 48)] = jnp.where(left, roll_half(one), two)


def pack_head(grad, raw, i):
    left = lane_half((48, 128), 0)
    for dd in range(NB):
        top, bottom = grad[RB * dd : RB * dd + 48], grad[RB * dd + 48 : RB * dd + 96]
        raw[0, dd, i] = jnp.where(left, top, roll_half(bottom))
        raw[1, dd, i] = jnp.where(left, roll_half(top), bottom)


def fold(block):
    return jnp.concatenate([block[0:48], block[48:96]], axis=1)


def unfold(block):
    return jnp.concatenate([block[:, 0:64], block[:, 64:128]], axis=0)


def transpose_rows(src, dst):
    @pl.loop(0, LENGTH // 128)
    def _(i):
        r = rows(i * 128, 128)
        dst[:, r] = src[r, :].T


def cat(pieces):
    return jnp.concatenate(pieces, axis=1)


def block_kernel(net, scale_tokens, nin, *refs):
    hid, cot, ids, table, weights, *given = refs[:nin]
    o_block, o_counts, o_in, o_small, o_qkv, o_out, o_up, o_down = refs[nin : nin + 8]
    (
        v_small, v_cnt, v_param, v_index, own_q, own_o, v_rq, v_ro, v_up, v_down, v_wh, v_wo,
        v_nrm, v_nrmT, v_n2, v_n2T, v_ups, v_upsT, v_qkv, v_lse, v_ctx, v_dctx, v_mid, v_act, v_slope,
        v_send, v_recv, v_acc, v_dk, v_dv, v_p2, v_p3, v_sums, v_swap, swsem, lsem, *nets,
    ) = refs[nin + 8 :]
    v_low, v_lowT = v_nrm, v_upsT
    pos = Place()
    mine = pos.c * HALF
    theirs = HALF - mine

    def exchange(i, src, dst):
        return swap(pos, src, dst, swsem, i)

    def exchange_rows(i, ref):
        return swap(pos, ref.at[rows(mine, HALF)], ref.at[rows(mine, HALF)], swsem, i)

    row_ids = jnp.broadcast_to(ids[...].astype(F32), (128, HALF)).T
    member = row_ids == lax.broadcasted_iota(jnp.int32, (HALF, 128), 1).astype(F32)
    own_counts = jnp.sum(member.astype(F32), 0, keepdims=True)

    if net:
        qkv_w, out_w, own_up, own_down, *vectors = given
        v_p0, r2_0, rz_0, r2_q, rz_q, r2_o, rz_o, r2_2, rz_2, r2_3, rz_3, f_q, f_o, gssem, grsem, rssem, rrsem = nets
        v_cnt[2] = jnp.zeros((8, 128), F32)
        for i in range(4):
            v_cnt[2, i : i + 1, 0:RB] = vectors[i][...].astype(F32)
        v_cnt[2, 4:5, :] = own_counts
        out_rows = out_w[...].T
        for j in range(3):
            for part in range(3):
                own_q[3 * j + part] = fold(qkv_w[part][:, 64 * j : 64 * j + 64])
            own_o[j] = fold(out_rows[:, 64 * j : 64 * j + 64])
        entry_barrier(pos, net)
        g0 = Gather(pos, 0, v_cnt.at[2], v_small, gssem, grsem)
        gq = Gather(pos, 1, own_q, v_rq, gssem, grsem)
        go = Gather(pos, 2, own_o, v_ro, gssem, grsem)
        g2 = Gather(pos, 3, own_up, v_up, gssem, grsem)
        g3 = Gather(pos, 4, own_down, v_down, gssem, grsem)
        s0 = Reduce(pos, 0, lambda b, dd: v_p0.at[b, dd], r2_0, rz_0, rssem, rrsem)
        so = Reduce(pos, 1, lambda b, dd: v_ro.at[b, dd], r2_o, rz_o, rssem, rrsem)
        s2 = Reduce(pos, 2, lambda b, dd: v_p2.at[b, dd], r2_2, rz_2, rssem, rrsem)
        s3 = Reduce(pos, 3, lambda b, dd: v_p3.at[b, dd], r2_3, rz_3, rssem, rrsem)

        def sq(j):
            return Reduce(
                pos, 4 + j, lambda b, dd: v_rq.at[b, dd, pl.ds(3 * j, 3)], r2_q.at[j], rz_q.at[j], rssem, rrsem
            )

        g0.step(0)
        gq.step(0)
        v_small[pos.x, pos.d] = v_cnt[2]
        v_rq[pos.x, pos.d] = own_q[...]
        v_ro[pos.x, pos.d] = own_o[...]
        v_up[pos.x, pos.d] = own_up[...]
        v_down[pos.x, pos.d] = own_down[...]
        for k in (1, 2, 3):
            g0.step(k)
            gq.step(k)
        go.step(0)
        g2.step(0)
        g0.step(4)
        gq.step(4)
        g0.finish()
        v_param[...] = jnp.zeros_like(v_param)
        total = jnp.zeros((8, 128), F32)
        for dd in range(NB):
            row = lax.broadcasted_iota(jnp.int32, (128, D), 0)
            col = lax.broadcasted_iota(jnp.int32, (128, D), 1)
            place = ((col == row + RB * dd) & (row < RB)).astype(BF16)
            block = v_small[pos.x, dd]
            v_param[...] += mm(block.astype(BF16), place)
            total += v_small[0, dd] + v_small[1, dd]
        v_cnt[0] = total
        exchange(0, v_cnt.at[0], v_cnt.at[1]).start()
    else:
        vectors, *wide = given
        entry_barrier(pos, net)
        v_param[...] = vectors[...]
        cps = [pltpu.make_async_copy(a, b, lsem.at[i]) for i, (a, b) in enumerate(zip(wide, (v_rq, v_ro, v_up, v_down)))]
        for cp in cps:
            cp.start()
        for cp in cps:
            cp.wait()

    @pl.loop(0, HALF // 64)
    def _(i):
        r = rows(i * 64, 64)
        hat, _inv = norm_stats(hid[r, :].astype(F32))
        v_nrm[rows(mine + i * 64, 64), :] = (hat * v_param[0:1, :] + v_param[1:2, :]).astype(BF16)

    exchange_rows(1, v_nrm).start()

    if net:
        exchange(0, v_cnt.at[0], v_cnt.at[1]).wait()
        counts = (v_cnt[0] + v_cnt[1])[4:5, :]
        v_index[...] = jnp.full(v_index.shape, -1, jnp.int32)
        v_index[0:1, 0:GROUPS] = table[...]
        index = v_index[0:1, :]
        weight = jnp.zeros((1, 128), F32)
        for r in range(TABLE):
            weight = weight + jnp.where(index == r, weights[r], 0.0)
        group_scale = weight * scale_tokens / jnp.maximum(counts, 1.0)
        o_counts[...] = counts[:, 0:GROUPS]
    else:
        o_counts[...] = table[...]
        group_scale = weights[0:1, :]
    row_scale = jnp.sum(jnp.where(member, group_scale, 0.0), 1, keepdims=True)
    v_ups[rows(mine, HALF), :] = (cot[...].astype(F32) * row_scale).astype(BF16)
    exchange_rows(2, v_ups).start()

    if net:
        go.step(1)
        g2.step(1)
        go.step(2)
        g2.step(2)
        gq.finish()
    unpack_heads(v_rq, 0, 9, v_wh)
    if net:
        go.step(3)
        g2.step(3)
        go.step(4)
        g3.step(0)

    for half, start in enumerate((mine, theirs)):
        if half == 1:
            exchange_rows(1, v_nrm).wait_send()
            swap(pos, v_nrm.at[rows(theirs, HALF)], v_nrm.at[rows(theirs, HALF)], swsem, 1).wait_recv()
        lhs = v_nrm[rows(start, HALF), :]
        for part in range(3):
            res = mm(lhs, cat([v_wh[3 * j + part] for j in range(3)])).astype(BF16)
            if part == 0:
                res = (res.astype(F32) * HEAD_DIM**-0.5).astype(BF16)
            for j in range(3):
                v_qkv[3 * part + j, rows(start, HALF), :] = res[:, 128 * j : 128 * j + 128]

    @pl.loop(0, 3)
    def _(pair):
        if net:

            @pl.when(pair == 1)
            def _():
                g2.step(4)
                g3.step(1)

            @pl.when(pair == 2)
            def _():
                g3.step(2)

        for i in range(4):
            n = 256 * (i + 1)
            q = v_qkv[pair, 256 * i : n, :]
            out = jnp.zeros((256, 128), F32)
            for h in range(2):
                pieces = []
                peak = None
                for j in range(i + 1):
                    k = only(v_qkv[3 + pair, 256 * j : 256 * j + 256, :], h)
                    s = mm(k, q, NT)
                    if j == i:
                        key = lax.broadcasted_iota(jnp.int32, s.shape, 0)
                        query = lax.broadcasted_iota(jnp.int32, s.shape, 1)
                        s = jnp.where(key <= query, s, MASKED_SCORE)
                    top = jnp.max(s, 0, keepdims=True)
                    peak = top if peak is None else jnp.maximum(peak, top)
                    pieces.append(s)
                total = jnp.zeros((1, 256), F32)
                for j in range(i + 1):
                    e = jnp.exp(pieces[j] - peak)
                    total += jnp.sum(e, 0, keepdims=True)
                    pieces[j] = e
                inv = 1.0 / total
                for j in range(i + 1):
                    v = only(v_qkv[6 + pair, 256 * j : 256 * j + 256, :], h)
                    out += mm((pieces[j] * inv).astype(BF16), v, TN)
                v_lse[pair, h : h + 1, 256 * i : n] = peak + jnp.log(total)
            v_ctx[pair, 256 * i : n, :] = out.astype(BF16)

    if net:
        g3.step(3)
        go.finish()
    unpack_heads(v_ro, 0, 3, v_wo)

    w_out = cat([v_wo[j] for j in range(3)])
    for half, start in enumerate((theirs, mine)):
        lhs = cat([v_ctx[j, rows(start, HALF), :] for j in range(3)])
        res = mm(lhs, w_out, NT)
        if half == 0:
            v_send[0] = res.astype(BF16)
            exchange(3, v_send.at[0], v_recv.at[0]).start()
        else:
            v_acc[...] = res
    if net:
        g3.step(4)
    transpose_rows(v_nrm, v_nrmT)
    exchange(3, v_send.at[0], v_recv.at[0]).wait()

    @pl.loop(0, HALF // 64)
    def _(i):
        r = rows(i * 64, 64)
        middle = hid[r, :].astype(F32) + v_acc[r, :] + v_recv[0, r, :].astype(F32)
        v_mid[r, :] = middle
        hat, _inv = norm_stats(middle)
        v_n2[rows(mine + i * 64, 64), :] = (hat * v_param[2:3, :] + v_param[3:4, :]).astype(BF16)

    exchange_rows(4, v_n2).start()
    exchange_rows(2, v_ups).wait_send()
    swap(pos, v_ups.at[rows(theirs, HALF)], v_ups.at[rows(theirs, HALF)], swsem, 2).wait_recv()
    transpose_rows(v_ups, v_upsT)
    if net:
        g2.finish()

    for half, start in enumerate((mine, theirs)):
        if half == 1:
            swap(pos, v_n2.at[rows(theirs, HALF)], v_n2.at[rows(theirs, HALF)], swsem, 4).wait_recv()

        @pl.loop(0, 6)
        def _(tile):
            b = lax.div(tile, 3)
            cols = pl.ds(pl.multiple_of(lax.rem(tile, 3) * 256, 256), 256)
            pre = mm(v_n2[rows(start, HALF), :], v_up[b, :, :, cols].reshape(D, 256))
            square = pre * pre
            bend = jnp.tanh(GELU_C * pre * (1.0 + GELU_A * square))
            v_act[b, rows(start, HALF), cols] = (0.5 * pre * (1.0 + bend)).astype(BF16)
            slope = 0.5 * (1.0 + bend) + 0.5 * pre * (1.0 - bend * bend) * (GELU_C * (1.0 + 3.0 * GELU_A * square))
            v_slope[b, rows(start, HALF), cols] = slope.astype(BF16)

    exchange_rows(4, v_n2).wait_send()
    transpose_rows(v_n2, v_n2T)

    def tile_of(tile):
        return lax.div(tile, 3), pl.ds(pl.multiple_of(lax.rem(tile, 3) * 256, 256), 256)

    @pl.loop(0, 6)
    def _(tile):
        b, cols = tile_of(tile)
        res = mm(v_upsT[...], v_act[b, :, cols])
        v_p3[b, :, :, cols] = res.astype(BF16).reshape(NB, RB, 256)

    if net:
        s3.start()
        g3.finish()
        gq.drain()
        go.drain()

    @pl.loop(0, 6)
    def _(tile):
        b, cols = tile_of(tile)
        res = mm(v_ups[...], v_down[b, :, :, cols].reshape(D, 256))
        pre = (res * v_slope[b, :, cols].astype(F32)).astype(BF16)
        v_slope[b, :, cols] = pre
        res = mm(v_n2T[...], pre)
        v_p2[b, :, :, cols] = res.astype(BF16).reshape(NB, RB, 256)

    if net:
        s2.start()
    for half, start in enumerate((theirs, mine)):
        res = mm(v_slope[0, rows(start, HALF), :], v_up[0].reshape(D, D), NT)
        res += mm(v_slope[1, rows(start, HALF), :], v_up[1].reshape(D, D), NT)
        if half == 0:
            v_send[0] = res.astype(BF16)
            exchange(5, v_send.at[0], v_recv.at[0]).start()
        else:
            v_acc[...] = res
    if net:
        s3.mid1()
    exchange(5, v_send.at[0], v_recv.at[0]).wait()
    v_sums[...] = jnp.zeros_like(v_sums)

    def norm_back(upper, values, gain, at):
        hat, inv = norm_stats(values)
        scaled = upper * gain
        first = jnp.mean(scaled, -1, keepdims=True)
        second = jnp.mean(scaled * hat, -1, keepdims=True)
        v_sums[at : at + 1, :] += jnp.sum(upper * hat, 0, keepdims=True)
        v_sums[at + 1 : at + 2, :] += jnp.sum(upper, 0, keepdims=True)
        return inv * (scaled - first - hat * second)

    @pl.loop(0, HALF // 64)
    def _(i):
        r = rows(i * 64, 64)
        wide = rows(mine + i * 64, 64)
        upper = v_acc[r, :] + v_recv[0, r, :].astype(F32)
        d_mid = v_ups[wide, :].astype(F32) + norm_back(upper, v_mid[r, :], v_param[2:3, :], 2)
        o_in[r, :] = d_mid
        v_low[wide, :] = d_mid.astype(BF16)

    exchange_rows(6, v_low).start()
    for half, start in enumerate((mine, theirs)):
        if half == 1:
            swap(pos, v_low.at[rows(theirs, HALF)], v_low.at[rows(theirs, HALF)], swsem, 6).wait_recv()
        res = mm(v_low[rows(start, HALF), :], w_out).astype(BF16)
        for j in range(3):
            v_dctx[j, rows(start, HALF), :] = res[:, 128 * j : 128 * j + 128]
    transpose_rows(v_low, v_lowT)
    res = mm(v_lowT[...], cat([v_ctx[j] for j in range(3)])).astype(BF16)
    for j in range(3):
        pack_head(res[:, 128 * j : 128 * j + 128], v_ro, j)
    if net:
        so.start()
        s3.mid0()

    @pl.loop(0, 3)
    def _(pair):
        if net:

            @pl.when(pair == 1)
            def _():
                s3.join()
                s3.hop(0)

            @pl.when(pair == 2)
            def _():
                s2.mid1()
                s3.hop(1)

        v_dk[...] = jnp.zeros_like(v_dk)
        v_dv[...] = jnp.zeros_like(v_dv)
        for i in range(4):
            n = 256 * (i + 1)
            q = v_qkv[pair, 256 * i : n, :]
            up = v_dctx[pair, 256 * i : n, :]
            qs = [only(q, h) for h in range(2)]
            ups = [only(up, h) for h in range(2)]
            dq = jnp.zeros((256, 128), F32)
            probs = [[], []]
            grads = [[], []]
            for h in range(2):
                lse = v_lse[pair, h : h + 1, 256 * i : n]
                delta = jnp.zeros((1, 256), F32)
                for j in range(i + 1):
                    at = slice(256 * j, 256 * j + 256)
                    s = mm(v_qkv[3 + pair, at, :], qs[h], NT)
                    p = jnp.exp(s - lse)
                    if j == i:
                        key = lax.broadcasted_iota(jnp.int32, s.shape, 0)
                        query = lax.broadcasted_iota(jnp.int32, s.shape, 1)
                        p = jnp.where(key <= query, p, 0.0)
                    dp = mm(v_qkv[6 + pair, at, :], ups[h], NT)
                    delta += jnp.sum(p * dp, 0, keepdims=True)
                    probs[h].append(p)
                    grads[h].append(dp)
                for j in range(i + 1):
                    grads[h][j] = (probs[h][j] * (grads[h][j] - delta)).astype(BF16)
                    probs[h][j] = probs[h][j].astype(BF16)
            for j in range(i + 1):
                at = slice(256 * j, 256 * j + 256)
                for h in range(2):
                    k = only(v_qkv[3 + pair, at, :], h)
                    dq += mm(grads[h][j], k, TN)
                v_dv[at, :] += mm(cat([probs[0][j], probs[1][j]]), jnp.concatenate(ups, axis=0))
                v_dk[at, :] += mm(cat([grads[0][j], grads[1][j]]), jnp.concatenate(qs, axis=0))
            v_qkv[pair, 256 * i : n, :] = (dq * HEAD_DIM**-0.5).astype(BF16)
        v_qkv[3 + pair] = v_dk[...].astype(BF16)
        v_qkv[6 + pair] = v_dv[...].astype(BF16)
        res = mm(v_nrmT[...], cat([v_qkv[3 * part + pair] for part in range(3)])).astype(BF16)
        for part in range(3):
            pack_head(res[:, 128 * part : 128 * part + 128], v_rq, 3 * pair + part)
        if net:
            sq(pair).start()

    w_qkv = cat([v_wh[3 * j + part] for part in range(3) for j in range(3)])
    for half, start in enumerate((theirs, mine)):
        lhs = cat([v_qkv[i, rows(start, HALF), :] for i in range(9)])
        res = mm(lhs, w_qkv, NT)
        if half == 0:
            v_send[1] = res.astype(BF16)
            exchange(7, v_send.at[1], v_recv.at[1]).start()
        else:
            v_acc[...] = res
    if net:
        q0, q1, q2 = sq(0), sq(1), sq(2)
        s2.mid0()
        s3.hop(2)
        so.mid1()
        so.mid0()
    exchange(7, v_send.at[1], v_recv.at[1]).wait()

    @pl.loop(0, HALF // 64)
    def _(i):
        r = rows(i * 64, 64)
        upper = v_acc[r, :] + v_recv[1, r, :].astype(F32)
        o_in[r, :] = o_in[r, :] + norm_back(upper, hid[r, :].astype(F32), v_param[0:1, :], 0)

    v_swap[0] = v_sums[...]
    exchange(8, v_swap.at[0], v_swap.at[1]).start()
    if net:
        s2.join()
        s2.hop(0)
        q0.mid1()
        q0.mid0()
        so.join()
        so.hop(0)
        s2.hop(1)
    exchange(8, v_swap.at[0], v_swap.at[1]).wait()
    both = v_swap[0] + v_swap[1]
    if net:
        for dd in range(NB):
            piece = cat([both[:, RB * dd : RB * dd + RB], jnp.zeros((8, 128 - RB), F32)])
            v_p0[0, dd] = piece
            v_p0[1, dd] = piece
        s0.start()
        q1.mid1()
        q1.mid0()

    for half, start in enumerate((theirs, mine)):
        res = mm(v_act[0, rows(start, HALF), :], v_down[0].reshape(D, D), NT)
        res += mm(v_act[1, rows(start, HALF), :], v_down[1].reshape(D, D), NT)
        if half == 0:
            v_send[0] = res.astype(BF16)
            exchange(9, v_send.at[0], v_recv.at[0]).start()
            if net:
                s2.hop(2)
                q0.join()
                q0.hop(0)
                so.hop(1)
                q2.mid1()
                q2.mid0()
        else:
            o_block[...] = v_mid[...] + res
    if net:
        q1.join()
        q1.hop(0)
        so.hop(2)
        q0.hop(1)
        s0.mid1()
        s0.mid0()
        q2.join()
        q2.hop(0)
        q1.hop(1)
        q0.hop(2)
        s0.join()
        s0.hop(0)
        q2.hop(1)
        q1.hop(2)
        s0.hop(1)
        q2.hop(2)
        s0.hop(2)
    exchange(9, v_send.at[0], v_recv.at[0]).wait()
    o_block[...] += v_recv[0].astype(F32)
    if net:
        s3.finish(o_down)
        s2.finish(o_up)
        so.finish(f_o)
        o_out[...] = cat([unfold(f_o[j]) for j in range(3)]).T
        q0.finish(f_q.at[0])
        q1.finish(f_q.at[1])
        q2.finish(f_q.at[2])
        for part in range(3):
            o_qkv[part] = cat([unfold(f_q[j, part]) for j in range(3)])
        s0.finish(v_swap.at[0, :, 0:128])
        o_small[...] = pltpu.roll(v_swap[0, :, 0:128], lax.rem(128 - 24 * pos.t, 128), 1)[:, 0:24]
        for g in (g0, g2, g3, s0, so, s2, s3, q0, q1, q2):
            g.drain()
    else:
        o_small[...] = both
        o_qkv[...] = v_rq[...]
        o_out[...] = v_ro[...]
        o_up[...] = v_p2[...]
        o_down[...] = v_p3[...]
    exchange_rows(6, v_low).wait_send()


def fold_rows(block):
    return block.reshape(2, 48, 3, 64).transpose(2, 1, 0, 3).reshape(3, 48, 128)


def unfold_rows(packed):
    return packed.reshape(3, 48, 2, 64).transpose(2, 1, 0, 3).reshape(RB, 192)


def shards(
    hidden_in, cotangent, group_ids, weight_table, table_index, qkv_weight, out_weight, up_weight, down_weight,
    norm1_gain, norm1_bias, norm2_gain, norm2_bias,
):
    n_dp, n_t = lax.axis_size("dp"), lax.axis_size("tensor")
    net = n_dp == NB and n_t == 4
    core = lax.rem(lax.axis_index("tensor"), 2)
    scale_tokens = hidden_in.shape[0] * n_dp * n_t / GROUPS
    ids = group_ids.reshape(1, HALF)
    down = down_weight.T
    vm, dma = pltpu.VMEM, pltpu.SemaphoreType.DMA
    vspec = pl.BlockSpec(memory_space=pltpu.VMEM)
    aspec = pl.BlockSpec(memory_space=pl.ANY)
    norm_vectors = (norm1_gain, norm1_bias, norm2_gain, norm2_bias)
    s_q, s_o, s_w = (3, 48, 128), (3, 48, 128), (RB, D)
    if net:
        vectors = [v.reshape(1, RB) for v in norm_vectors]
        table, weights = table_index.reshape(1, GROUPS), weight_table
        given = [qkv_weight.transpose(1, 0, 2), out_weight, up_weight, down, *vectors]
        weight_spec = pl.BlockSpec(memory_space=pltpu.SMEM)
        given_specs = [vspec] * len(given)
        grads = [((8, 24), F32), ((3, RB, 192), F32), ((192, RB), F32), (s_w, F32), (s_w, F32)]
        nets = [vm((2, NB, 8, 128), F32), vm((2, 4, 8, 128), F32), vm((9, 8, 128), F32)]
        nets += [vm((3, 2, 4) + s_q, BF16), vm((3, 9) + s_q, BF16)]
        for s in (s_o, s_w, s_w):
            nets += [vm((2, 4) + s, BF16), vm((9,) + s, BF16)]
        nets += [vm((3,) + s_q, F32), vm(s_o, F32)]
        nets += [dma((5, 5, 4)), dma((5, 2, NB)), dma((7, 5, 4)), dma((7, 5, 4))]
    else:

        def whole(block, axis):
            full = lax.all_gather(block, "dp", axis=axis, tiled=True)
            every = lax.all_gather(full, "tensor", axis=0)
            return lax.dynamic_index_in_dim(every.reshape((n_t // 2, 2) + full.shape), core, 1, keepdims=False)

        heads = jnp.concatenate([qkv_weight.transpose(1, 0, 2), out_weight.T[None]], axis=0)
        heads = whole(heads, 1).reshape(2, 4, NB, RB, 192).transpose(0, 2, 1, 3, 4)
        folded = jax.vmap(jax.vmap(jax.vmap(fold_rows)))(heads)
        given = [
            jnp.pad(lax.all_gather(jnp.stack(norm_vectors).astype(F32), "dp", axis=1, tiled=True), ((0, 4), (0, 0))),
            folded[:, :, :3].transpose(0, 1, 3, 2, 4, 5).reshape(2, NB, 9, 48, 128),
            folded[:, :, 3],
            whole(up_weight, 0).reshape(2, NB, RB, D),
            whole(down, 0).reshape(2, NB, RB, D),
        ]
        member = (group_ids[:, None] == jnp.arange(GROUPS, dtype=jnp.int32)[None, :]).astype(F32)
        counts = lax.psum(jnp.sum(member, 0), ("dp", "tensor"))
        hits = table_index[:, None] == jnp.arange(TABLE, dtype=jnp.int32)[None, :]
        scale = jnp.sum(jnp.where(hits, weight_table[None, :], 0.0), 1) * scale_tokens / jnp.maximum(counts, 1.0)
        weights = jnp.pad(scale[None, :], ((0, 7), (0, 128 - GROUPS)))
        table = counts.reshape(1, GROUPS)
        weight_spec = vspec
        given_specs = [vspec, aspec, aspec, aspec, aspec]
        grads = [((8, D), F32), ((2, NB, 9, 48, 128), BF16), ((2, NB, 3, 48, 128), BF16)]
        grads += [((2, NB) + s_w, BF16), ((2, NB) + s_w, BF16)]
        nets = []
    shapes = [((HALF, D), F32), ((1, GROUPS), F32), ((HALF, D), F32), *grads]
    outs = pl.pallas_call(
        functools.partial(block_kernel, net, scale_tokens, 5 + len(given)),
        out_shape=[jax.ShapeDtypeStruct(*s) for s in shapes],
        in_specs=[vspec, vspec, vspec, vspec, weight_spec, *given_specs],
        out_specs=[vspec] * len(shapes),
        scratch_shapes=[
            vm((2, NB, 8, 128), F32), vm((3, 8, 128), F32), vm((8, D), F32), vm((8, 128), jnp.int32), vm((9, 48, 128), BF16),
            vm((3, 48, 128), BF16), vm((2, NB, 9, 48, 128), BF16), vm((2, NB, 3, 48, 128), BF16), vm((2, NB, RB, D), BF16),
            vm((2, NB, RB, D), BF16), vm((9, D, 128), BF16), vm((3, D, 128), BF16),
            vm((LENGTH, D), BF16), vm((D, LENGTH), BF16), vm((LENGTH, D), BF16), vm((D, LENGTH), BF16), vm((LENGTH, D), BF16),
            vm((D, LENGTH), BF16), vm((9, LENGTH, 128), BF16), vm((3, 8, LENGTH), F32), vm((3, LENGTH, 128), BF16),
            vm((3, LENGTH, 128), BF16), vm((HALF, D), F32), vm((2, LENGTH, D), BF16), vm((2, LENGTH, D), BF16),
            vm((2, HALF, D), BF16), vm((2, HALF, D), BF16), vm((HALF, D), F32), vm((LENGTH, 128), F32), vm((LENGTH, 128), F32),
            vm((2, NB, RB, D), BF16), vm((2, NB, RB, D), BF16), vm((8, D), F32), vm((2, 8, D), F32),
            dma((2, 10)), dma((4,)), *nets,
        ],
        compiler_params=pltpu.CompilerParams(collective_id=0, has_side_effects=True, vmem_limit_bytes=VMEM_LIMIT),
        name="block",
    )(hidden_in, cotangent, ids, table, weights, *given)
    block_output, counts, input_grad, sums, grad_qkv, grad_out, grad_up, grad_down = outs
    if net:
        norms = [sums[i] for i in range(4)]
        grad_qkv = grad_qkv.transpose(1, 0, 2)
    else:

        def owned(part):
            base = jnp.zeros((n_t // 2, 2) + part.shape[1:], F32)
            base = lax.dynamic_update_index_in_dim(base, part.astype(F32), core, 1)
            flat = base.reshape((n_t,) + part.shape[1:])
            mine = lax.psum_scatter(flat, "tensor", scatter_dimension=0, tiled=False)
            return lax.psum_scatter(mine, "dp", scatter_dimension=0, tiled=True)

        parts = grad_qkv.reshape(2, NB, 3, 3, 48, 128).transpose(0, 1, 3, 2, 4, 5)
        parts = jax.vmap(jax.vmap(jax.vmap(unfold_rows)))(parts)
        grad_qkv = owned(parts.transpose(0, 1, 3, 2, 4).reshape(2, D, 3, 192))
        grad_out = owned(jax.vmap(jax.vmap(unfold_rows))(grad_out).reshape(2, D, 192)).T
        grad_up, grad_down = owned(grad_up.reshape(2, D, D)), owned(grad_down.reshape(2, D, D))
        half_sums = jnp.where(core == 0, sums, 0.0)
        norms = [lax.psum_scatter(half_sums[i], ("dp", "tensor"), scatter_dimension=0, tiled=True) for i in range(4)]
    return (
        block_output,
        input_grad,
        grad_qkv,
        grad_out,
        grad_up,
        grad_down.T,
        norms[0],
        norms[1],
        norms[2],
        norms[3],
        counts.reshape(GROUPS),
    )


def solution(mesh):
    both = ("dp", "tensor")
    return jax.shard_map(
        shards,
        mesh=mesh,
        in_specs=(
            P(both, None), P(both, None), P(both), P(), P(), P("dp", None, "tensor"), P("tensor", "dp"), P("dp", "tensor"),
            P("tensor", "dp"), P("dp"), P("dp"), P("dp"), P("dp"),
        ),
        out_specs=(
            P(both, None), P(both, None), P("dp", None, "tensor"), P("tensor", "dp"), P("dp", "tensor"), P("tensor", "dp"),
            P(both), P(both), P(both), P(both), P(),
        ),
        check_vma=False,
    )
```

```python
import functools

import jax
import jax.numpy as jnp
from jax import lax
from jax.experimental import pallas as pl
from jax.experimental.pallas import tpu as pltpu
from jax.sharding import PartitionSpec as P

D = 768
HEAD_DIM = 64
LENGTH = 1024
HALF = 512
GROUPS = 16
TABLE = 8
NB = 8
RB = D // NB
CUT = 512
EPSILON = 1e-05
MASKED_SCORE = -1e30
GELU_C = 0.7978845608028654
GELU_A = 0.044715
MESH = pl.DeviceIdType.MESH
F32 = jnp.float32
BF16 = jnp.bfloat16
NT = (((1,), (1,)), ((), ()))
TN = (((0,), (0,)), ((), ()))
NN = (((1,), (0,)), ((), ()))
VMEM_LIMIT = 66_000_000


def mm(a, b, dims=NN):
    return lax.dot_general(a, b, dims, preferred_element_type=F32)


class Place:
    def __init__(self):
        self.d = lax.axis_index("dp")
        self.t = lax.axis_index("tensor")
        self.z = lax.div(self.d, 2)
        self.y = lax.rem(self.d, 2)
        self.x = lax.div(self.t, 2)
        self.c = lax.rem(self.t, 2)
        c = self.c
        self.sibling = (self.d, self.t + 1 - 2 * c)
        self.x1 = lax.rem(self.x + c, 2)
        self.y1 = lax.rem(self.y + 1 - c, 2)
        self.x2 = lax.rem(self.x + 1 - c, 2)
        self.y2 = lax.rem(self.y + c, 2)
        self.p1 = (2 * self.z + self.y1, 2 * self.x1 + c)
        self.p2 = (2 * self.z + self.y2, 2 * self.x2 + c)
        self.others = [lax.rem(self.z + k, 4) for k in (1, 2, 3)]
        self.sources = [lax.rem(self.z + k, 4) for k in (3, 2, 1)]

    def at_z(self, zz):
        return (2 * zz + self.y, self.t)


def entry_barrier(pos, net):
    bar = pltpu.get_barrier_semaphore()
    pl.semaphore_signal(bar, inc=1, device_id=pos.sibling, device_id_type=MESH)
    if not net:
        pl.semaphore_wait(bar, 1)
        return
    for peer in (pos.p1, pos.p2, *[pos.at_z(zz) for zz in pos.others]):
        pl.semaphore_signal(bar, inc=1, device_id=peer, device_id_type=MESH)
    pl.semaphore_wait(bar, 6)


class Gather:
    def __init__(self, pos, g, own, slot, ssem, rsem):
        self.pos, self.g, self.own, self.slot = pos, g, own, slot
        self.ssem, self.rsem = ssem, rsem

    def copy(self, b, dd, link, i, dev, src=None):
        slot = self.slot(b, dd)
        return pltpu.make_async_remote_copy(
            src_ref=slot if src is None else src,
            dst_ref=slot,
            send_sem=self.ssem.at[self.g, link, i],
            recv_sem=self.rsem.at[self.g, b, dd],
            device_id=dev,
            device_id_type=MESH,
        )

    def wait(self, b, dd):
        self.copy(b, dd, 0, 0, self.pos.p1).wait_recv()

    def own_z(self):
        p = self.pos
        for zz in p.others:
            self.copy(p.x, p.d, 0, zz, p.at_z(zz), self.own).start()

    def own_xy(self):
        p = self.pos
        self.copy(p.x, p.d, 1, p.z, p.p1, self.own).start()
        self.copy(p.x, p.d, 2, p.z, p.p2, self.own).start()

    def line(self, *ks):
        p = self.pos
        for k in ks:
            zz = p.sources[k]
            dd = 2 * zz + p.y
            self.wait(p.x, dd)
            self.copy(p.x, dd, 1, zz, p.p1).start()
            self.copy(p.x, dd, 2, zz, p.p2).start()

    def side(self, *ks):
        p = self.pos
        for k in ks:
            zz = p.z if k == 0 else p.sources[k - 1]
            dd = 2 * zz + p.y1
            self.wait(p.x1, dd)
            self.copy(p.x1, dd, 3, zz, p.p2).start()

    def finish(self):
        p = self.pos
        for zz in range(4):
            self.wait(p.x2, 2 * zz + p.y2)
            self.wait(1 - p.x, 2 * zz + 1 - p.y)

    def drain(self):
        p = self.pos
        for zz in p.others:
            self.copy(p.x, p.d, 0, zz, p.at_z(zz), self.own).wait_send()
        for zz in range(4):
            self.copy(p.x, 2 * zz + p.y, 1, zz, p.p1).wait_send()
            self.copy(p.x, 2 * zz + p.y, 2, zz, p.p2).wait_send()
            self.copy(p.x1, 2 * zz + p.y1, 3, zz, p.p2).wait_send()


class GatherZ(Gather):
    def __init__(self, pos, g, own, slot, ssem, rsem, zsem):
        super().__init__(pos, g, own, slot, zsem, rsem)

    def copy(self, b, dd, link, i, dev, src=None):
        slot = self.slot(b, dd)
        return pltpu.make_async_remote_copy(
            src_ref=slot if src is None else src,
            dst_ref=slot,
            send_sem=self.ssem.at[link, i],
            recv_sem=self.rsem.at[self.g, b, dd],
            device_id=dev,
            device_id_type=MESH,
        )

    def column(self, col, zz):
        p = self.pos
        x, y = ((p.x, p.y), (p.x1, p.y1), (p.x2, p.y2), (1 - p.x, 1 - p.y))[col]
        return x, 2 * zz + y

    def own_xy(self):
        p = self.pos
        self.copy(p.x, p.d, 4, 0, p.p1, self.own).start()
        self.copy(p.x, p.d, 4, 1, p.p2, self.own).start()

    def side(self):
        p = self.pos
        b, dd = self.column(1, p.z)
        self.wait(b, dd)
        self.copy(b, dd, 4, 2, p.p2).start()

    def spread(self, *cols):
        p = self.pos
        for col in cols:
            b, dd = self.column(col, p.z)
            if col >= 2:
                self.wait(b, dd)
            for zz in p.others:
                self.copy(b, dd, col, zz, p.at_z(zz), self.own if col == 0 else None).start()

    def finish(self):
        for zz in self.pos.others:
            for col in range(4):
                self.wait(*self.column(col, zz))

    def drain(self):
        p = self.pos
        self.copy(p.x, p.d, 4, 0, p.p1, self.own).wait_send()
        self.copy(p.x, p.d, 4, 1, p.p2, self.own).wait_send()
        b, dd = self.column(1, p.z)
        self.copy(b, dd, 4, 2, p.p2).wait_send()
        for col in range(4):
            b, dd = self.column(col, p.z)
            for zz in p.others:
                self.copy(b, dd, col, zz, p.at_z(zz)).wait_send()


class Reduce:
    def __init__(self, pos, g, slot, r2, rz, ssem, rsem):
        self.pos, self.g, self.slot, self.r2, self.rz = pos, g, slot, r2, rz
        self.ssem, self.rsem = ssem, rsem

    def copy(self, src, dst, link, i, dev, j=None):
        return pltpu.make_async_remote_copy(
            src_ref=src,
            dst_ref=dst,
            send_sem=self.ssem.at[self.g, link, i],
            recv_sem=self.rsem.at[self.g, link, i if j is None else j],
            device_id=dev,
            device_id_type=MESH,
        )

    def to_p2(self, which, zz):
        p = self.pos
        b, dd = (p.x2, 2 * zz + p.y2) if which == 0 else (1 - p.x, 2 * zz + 1 - p.y)
        return self.copy(self.slot(b, dd), self.r2.at[which, zz], which, zz, p.p2)

    def to_p1(self, zz):
        p = self.pos
        return self.copy(self.slot(p.x1, 2 * zz + p.y1), self.rz.at[zz], 2, zz, p.p1)

    def to_z(self, zz):
        p = self.pos
        return self.copy(self.slot(p.x, 2 * zz + p.y), self.rz.at[4 + p.z], 3, zz, p.at_z(zz), p.z)

    def from_z(self, zz):
        p = self.pos
        return self.copy(self.slot(p.x, p.d), self.rz.at[4 + zz], 3, zz, p.at_z(zz))

    def add(self, b, dd, other):
        ref = self.slot(b, dd)
        ref[...] = (ref[...].astype(F32) + other.astype(F32)).astype(ref.dtype)

    def start(self):
        for which in (1, 0):
            for zz in range(4):
                self.to_p2(which, zz).start()

    def mid1(self):
        p = self.pos
        for zz in range(4):
            self.to_p2(1, zz).wait_recv()
            self.add(p.x1, 2 * zz + p.y1, self.r2[1, zz])
            self.to_p1(zz).start()

    def mid0(self):
        p = self.pos
        for zz in range(4):
            self.to_p2(0, zz).wait_recv()
            self.add(p.x, 2 * zz + p.y, self.r2[0, zz])

    def join(self):
        p = self.pos
        for zz in range(4):
            self.to_p1(zz).wait_recv()
            self.add(p.x, 2 * zz + p.y, self.rz[zz])
        for zz in p.others:
            self.to_z(zz).start()

    def finish(self, out):
        p = self.pos
        total = self.slot(p.x, p.d)[...].astype(F32)
        for zz in p.others:
            self.from_z(zz).wait_recv()
            total += self.rz[4 + zz].astype(F32)
        out[...] = total

    def drain(self):
        for zz in range(4):
            self.to_p2(1, zz).wait_send()
            self.to_p2(0, zz).wait_send()
            self.to_p1(zz).wait_send()
        for zz in self.pos.others:
            self.to_z(zz).wait_send()


class ReduceZ:
    def __init__(self, pos, slot, rl, rx, ssem, rsem):
        self.pos, self.slot, self.rl, self.rx = pos, slot, rl, rx
        self.ssem, self.rsem = ssem, rsem

    def column(self, col, zz):
        p = self.pos
        x, y = ((p.x, p.y), (p.x1, p.y1), (p.x2, p.y2), (1 - p.x, 1 - p.y))[col]
        return self.slot(x, 2 * zz + y)

    def copy(self, src, dst, link, i, dev, j=None):
        return pltpu.make_async_remote_copy(
            src_ref=src,
            dst_ref=dst,
            send_sem=self.ssem.at[link, i],
            recv_sem=self.rsem.at[link, i if j is None else j],
            device_id=dev,
            device_id_type=MESH,
        )

    def to_z(self, col, zz):
        p = self.pos
        return self.copy(self.column(col, zz), self.rl.at[col, p.z], col, zz, p.at_z(zz), p.z)

    def from_z(self, col, zz):
        p = self.pos
        return self.copy(self.column(col, p.z), self.rl.at[col, zz], col, zz, p.at_z(zz))

    def to_p2(self, which):
        return self.copy(self.column(2 + which, self.pos.z), self.rx.at[which], 4, which, self.pos.p2)

    def to_p1(self):
        return self.copy(self.column(1, self.pos.z), self.rx.at[2], 4, 2, self.pos.p1)

    def start(self):
        for col in (3, 2, 1, 0):
            for zz in self.pos.others:
                self.to_z(col, zz).start()

    def settle(self, col):
        p = self.pos
        ref = self.column(col, p.z)
        total = ref[...].astype(F32)
        for zz in p.others:
            self.from_z(col, zz).wait_recv()
            total += self.rl[col, zz].astype(F32)
        ref[...] = total.astype(ref.dtype)

    def cross2(self):
        for which in (1, 0):
            self.settle(2 + which)
            self.to_p2(which).start()
        self.settle(1)
        self.settle(0)

    def add(self, col, i):
        ref = self.column(col, self.pos.z)
        ref[...] = (ref[...].astype(F32) + self.rx[i].astype(F32)).astype(ref.dtype)

    def cross1(self):
        self.to_p2(1).wait_recv()
        self.add(1, 1)
        self.to_p1().start()
        self.to_p2(0).wait_recv()
        self.add(0, 0)

    def finish(self, out):
        self.to_p1().wait_recv()
        out[...] = self.column(0, self.pos.z)[...].astype(F32) + self.rx[2].astype(F32)

    def drain(self):
        self.to_p2(0).wait_send()
        self.to_p2(1).wait_send()
        self.to_p1().wait_send()
        for col in range(4):
            for zz in self.pos.others:
                self.to_z(col, zz).wait_send()


class Scatter:
    def __init__(self, pos, part, land, ssem, rsem):
        self.pos, self.part, self.land, self.ssem, self.rsem = pos, part, land, ssem, rsem
        self.me = 2 * pos.d + pos.x

    def copy(self, i, place):
        b, dd = i % 2, i // 2
        return pltpu.make_async_remote_copy(
            src_ref=self.part.at[b, dd],
            dst_ref=self.land.at[place],
            send_sem=self.ssem.at[i],
            recv_sem=self.rsem.at[place],
            device_id=(dd, 2 * b + self.pos.c),
            device_id_type=MESH,
        )

    def each(self, do):
        for i in range(2 * NB):

            @pl.when(i != self.me)
            def _():
                do(i)

    def start(self):
        self.each(lambda i: self.copy(i, self.me).start())

    def finish(self, out):
        out[...] = self.part[self.pos.x, self.pos.d]

        def take(i):
            self.copy(i, i).wait_recv()
            out[...] += self.land[i]

        self.each(take)

    def drain(self):
        self.each(lambda i: self.copy(i, self.me).wait_send())


def rows(start, size):
    return pl.ds(pl.multiple_of(start, size), size)


def swap(pos, src, dst, sems, i):
    return pltpu.make_async_remote_copy(
        src_ref=src,
        dst_ref=dst,
        send_sem=sems.at[0, i],
        recv_sem=sems.at[1, i],
        device_id=pos.sibling,
        device_id_type=MESH,
    )


def norm_stats(values):
    center = values - jnp.mean(values, -1, keepdims=True)
    inv = lax.rsqrt(jnp.mean(center * center, -1, keepdims=True) + EPSILON)
    return center * inv, inv


def lane_half(shape, which):
    lane = lax.broadcasted_iota(jnp.int32, shape, 1)
    return (lane < HEAD_DIM) if which == 0 else (lane >= HEAD_DIM)


def only(values, which):
    return jnp.where(lane_half(values.shape, which), values, jnp.zeros_like(values))


def roll_half(values):
    return pltpu.roll(values.astype(F32), HEAD_DIM, 1).astype(BF16)


def unpack_heads(raw, first, count, wh):
    @pl.loop(0, NB)
    def _(dd):
        at = pl.multiple_of(dd * RB, 16)
        for i in range(count):
            one, two = raw[0, dd, first + i], raw[1, dd, first + i]
            left = lane_half(one.shape, 0)
            wh[first + i, pl.ds(at, 48)] = jnp.where(left, one, roll_half(two))
            wh[first + i, pl.ds(at + 48, 48)] = jnp.where(left, roll_half(one), two)


def pack_head(grad, raw, i):
    left = lane_half((48, 128), 0)
    for dd in range(NB):
        top, bottom = grad[RB * dd : RB * dd + 48], grad[RB * dd + 48 : RB * dd + 96]
        raw[0, dd, i] = jnp.where(left, top, roll_half(bottom))
        raw[1, dd, i] = jnp.where(left, roll_half(top), bottom)


def fold(block):
    return jnp.concatenate([block[0:48], block[48:96]], axis=1)


def unfold(block):
    return jnp.concatenate([block[:, 0:64], block[:, 64:128]], axis=0)


def transpose_rows(src, dst):
    @pl.loop(0, LENGTH // 128)
    def _(i):
        r = rows(i * 128, 128)
        dst[:, r] = src[r, :].T


def cat(pieces):
    return jnp.concatenate(pieces, axis=1)


def block_kernel(net, scale_tokens, nin, *refs):
    hid, cot, ids, table, weights, *given = refs[:nin]
    o_block, o_counts, o_in, o_small, o_qkv, o_out, o_up, o_down = refs[nin : nin + 8]
    (
        v_small, v_cnt, v_param, v_index, own_q, own_o, v_rq, v_ro, v_up, v_down, v_wh, v_wo,
        v_nrm, v_nrmT, v_n2, v_n2T, v_ups, v_upsT, v_qkv, v_lse, v_ctx, v_dctx, v_mid, v_act, v_slope,
        v_send, v_recv, v_acc, v_dk, v_dv, v_p2, v_p3, v_sums, v_swap, swsem, lsem, *nets,
    ) = refs[nin + 8 :]
    v_low, v_lowT = v_nrm, v_upsT
    pos = Place()
    mine = pos.c * HALF
    theirs = HALF - mine

    def exchange(i, src, dst):
        return swap(pos, src, dst, swsem, i)

    def exchange_rows(i, ref):
        return swap(pos, ref.at[rows(mine, HALF)], ref.at[rows(mine, HALF)], swsem, i)

    row_ids = jnp.broadcast_to(ids[...].astype(F32), (128, HALF)).T
    member = row_ids == lax.broadcasted_iota(jnp.int32, (HALF, 128), 1).astype(F32)
    own_counts = jnp.sum(member.astype(F32), 0, keepdims=True)

    if net:
        qkv_w, out_w, own_up, own_down, *vectors = given
        (
            v_p0, land_0, ssem_0, rsem_0, r2_q, rz_q, r2_o, rz_o, r2_2, rz_2, r2_3, rz_3, rl_3, rx_3, f_q, f_o,
            gssem, grsem, gzsem, rssem, rrsem, rzssem, rzrsem,
        ) = nets
        v_cnt[2] = jnp.zeros((8, 128), F32)
        for i in range(4):
            v_cnt[2, i : i + 1, 0:RB] = vectors[i][...].astype(F32)
        v_cnt[2, 4:5, :] = own_counts
        out_rows = out_w[...].T
        for j in range(3):
            for part in range(3):
                own_q[3 * j + part] = fold(qkv_w[part][:, 64 * j : 64 * j + 64])
            own_o[j] = fold(out_rows[:, 64 * j : 64 * j + 64])
        entry_barrier(pos, net)
        left, right = slice(0, CUT), slice(CUT, D)
        g0 = Gather(pos, 0, v_cnt.at[2], lambda b, dd: v_small.at[b, dd], gssem, grsem)
        go = Gather(pos, 1, own_o, lambda b, dd: v_ro.at[b, dd], gssem, grsem)
        g2 = Gather(pos, 2, own_up, lambda b, dd: v_up.at[b, dd], gssem, grsem)
        g3 = Gather(pos, 3, own_down.at[:, left], lambda b, dd: v_down.at[b, dd, :, left], gssem, grsem)
        gz = GatherZ(pos, 7, own_down.at[:, right], lambda b, dd: v_down.at[b, dd, :, right], gssem, grsem, gzsem)
        s0 = Scatter(pos, v_p0, land_0, ssem_0, rsem_0)
        so = Reduce(pos, 1, lambda b, dd: v_ro.at[b, dd], r2_o, rz_o, rssem, rrsem)
        s2 = Reduce(pos, 2, lambda b, dd: v_p2.at[b, dd], r2_2, rz_2, rssem, rrsem)
        s3 = Reduce(pos, 3, lambda b, dd: v_p3.at[b, dd, :, left], r2_3, rz_3, rssem, rrsem)
        sz = ReduceZ(pos, lambda b, dd: v_p3.at[b, dd, :, right], rl_3, rx_3, rzssem, rzrsem)

        def gq(j):
            at = pl.ds(3 * j, 3)
            return Gather(pos, 4 + j, own_q.at[at], lambda b, dd: v_rq.at[b, dd, at], gssem, grsem)

        def sq(j):
            at = pl.ds(3 * j, 3)
            return Reduce(pos, 4 + j, lambda b, dd: v_rq.at[b, dd, at], r2_q.at[j], rz_q.at[j], rssem, rrsem)

        q0, q1, q2 = gq(0), gq(1), gq(2)
        for g in (g0, q0, q1, q2, go, g2):
            g.own_z()
        for g in (g0, q0, q1, q2, go):
            g.own_xy()
        v_small[pos.x, pos.d] = v_cnt[2]
        v_rq[pos.x, pos.d] = own_q[...]
        v_ro[pos.x, pos.d] = own_o[...]
        v_up[pos.x, pos.d] = own_up[...]
        v_down[pos.x, pos.d] = own_down[...]
        for k in range(3):
            g0.line(k)
            q0.line(k)
        g0.side(0, 1, 2, 3)
        q0.side(0, 1, 2, 3)
        q1.line(0, 1, 2)
        g0.finish()
        v_param[...] = jnp.zeros_like(v_param)
        total = jnp.zeros((8, 128), F32)
        for dd in range(NB):
            row = lax.broadcasted_iota(jnp.int32, (128, D), 0)
            col = lax.broadcasted_iota(jnp.int32, (128, D), 1)
            place = ((col == row + RB * dd) & (row < RB)).astype(BF16)
            block = v_small[pos.x, dd]
            v_param[...] += mm(block.astype(BF16), place)
            total += v_small[0, dd] + v_small[1, dd]
        v_cnt[0] = total
        exchange(0, v_cnt.at[0], v_cnt.at[1]).start()
    else:
        vectors, *wide = given
        entry_barrier(pos, net)
        v_param[...] = vectors[...]
        cps = [pltpu.make_async_copy(a, b, lsem.at[i]) for i, (a, b) in enumerate(zip(wide, (v_rq, v_ro, v_up, v_down)))]
        for cp in cps:
            cp.start()
        for cp in cps:
            cp.wait()

    @pl.loop(0, HALF // 64)
    def _(i):
        r = rows(i * 64, 64)
        hat, _inv = norm_stats(hid[r, :].astype(F32))
        v_nrm[rows(mine + i * 64, 64), :] = (hat * v_param[0:1, :] + v_param[1:2, :]).astype(BF16)

    exchange_rows(1, v_nrm).start()

    if net:
        exchange(0, v_cnt.at[0], v_cnt.at[1]).wait()
        counts = (v_cnt[0] + v_cnt[1])[4:5, :]
        v_index[...] = jnp.full(v_index.shape, -1, jnp.int32)
        v_index[0:1, 0:GROUPS] = table[...]
        index = v_index[0:1, :]
        weight = jnp.zeros((1, 128), F32)
        for r in range(TABLE):
            weight = weight + jnp.where(index == r, weights[r], 0.0)
        group_scale = weight * scale_tokens / jnp.maximum(counts, 1.0)
        o_counts[...] = counts[:, 0:GROUPS]
    else:
        o_counts[...] = table[...]
        group_scale = weights[0:1, :]
    row_scale = jnp.sum(jnp.where(member, group_scale, 0.0), 1, keepdims=True)
    v_ups[rows(mine, HALF), :] = (cot[...].astype(F32) * row_scale).astype(BF16)
    exchange_rows(2, v_ups).start()
    for i, ref, turned in ((1, v_nrm, v_nrmT), (2, v_ups, v_upsT)):
        exchange_rows(i, ref).wait_send()
        swap(pos, ref.at[rows(theirs, HALF)], ref.at[rows(theirs, HALF)], swsem, i).wait_recv()
        transpose_rows(ref, turned)

    def on(pair, k, *steps):
        @pl.when(pair == k)
        def _():
            for step in steps:
                step()

    @pl.loop(0, 3)
    def _(pair):
        if net:
            on(pair, 0, lambda: q1.side(0, 1, 2, 3), lambda: q2.line(0, 1, 2), g3.own_z)
            on(pair, 1, lambda: go.side(0, 1, 2, 3), lambda: g2.line(0))
            on(pair, 2, lambda: g2.line(2), lambda: g2.side(0), gz.side, lambda: gz.spread(0, 1))
            gq(pair).finish()
        unpack_heads(v_rq, 3 * pair, 3, v_wh)
        for half, start in enumerate((mine, theirs)):
            res = mm(v_nrm[rows(start, HALF), :], cat([v_wh[3 * pair + part] for part in range(3)])).astype(BF16)
            for part in range(3):
                piece = res[:, 128 * part : 128 * part + 128]
                if part == 0:
                    piece = (piece.astype(F32) * HEAD_DIM**-0.5).astype(BF16)
                v_qkv[3 * part + pair, rows(start, HALF), :] = piece
        if net:
            on(pair, 0, lambda: q2.side(0, 1, 2, 3), lambda: go.line(0, 1, 2), g2.own_xy)
            on(pair, 1, lambda: g2.line(1), gz.own_xy)

        def scores(i, h):
            q = v_qkv[pair, 256 * i : 256 * i + 256, :]
            pieces, peak = [], None
            for j in range(i + 1):
                k = only(v_qkv[3 + pair, 256 * j : 256 * j + 256, :], h)
                s = mm(k, q, NT)
                if j == i:
                    key = lax.broadcasted_iota(jnp.int32, s.shape, 0)
                    query = lax.broadcasted_iota(jnp.int32, s.shape, 1)
                    s = jnp.where(key <= query, s, MASKED_SCORE)
                top = jnp.max(s, 0, keepdims=True)
                peak = top if peak is None else jnp.maximum(peak, top)
                pieces.append(s)
            return pieces, peak

        tasks = [(i, h) for i in range(4) for h in range(2)]
        ahead = scores(*tasks[0])
        for at, (i, h) in enumerate(tasks):
            pieces, peak = ahead
            if at + 1 < len(tasks):
                ahead = scores(*tasks[at + 1])
            total = jnp.zeros((1, 256), F32)
            for j in range(i + 1):
                e = jnp.exp(pieces[j] - peak)
                total += jnp.sum(e, 0, keepdims=True)
                pieces[j] = e
            inv = 1.0 / total
            out = jnp.zeros((256, 128), F32) if h == 0 else out
            for j in range(i + 1):
                v = only(v_qkv[6 + pair, 256 * j : 256 * j + 256, :], h)
                out += mm((pieces[j] * inv).astype(BF16), v, TN)
            v_lse[pair, h : h + 1, 256 * i : 256 * i + 256] = peak + jnp.log(total)
            if h == 1:
                v_ctx[pair, 256 * i : 256 * i + 256, :] = out.astype(BF16)
            if net and (i, h) == (2, 1):
                on(pair, 2, lambda: g2.side(1))

    if net:
        g2.side(2, 3)
        g3.own_xy()
        g3.line(0)
        gz.spread(2, 3)
        go.finish()
    unpack_heads(v_ro, 0, 3, v_wo)

    w_out = cat([v_wo[j] for j in range(3)])
    for half, start in enumerate((theirs, mine)):
        lhs = cat([v_ctx[j, rows(start, HALF), :] for j in range(3)])
        res = mm(lhs, w_out, NT)
        if half == 0:
            v_send[0] = res.astype(BF16)
            exchange(3, v_send.at[0], v_recv.at[0]).start()
        else:
            v_acc[...] = res
    exchange(3, v_send.at[0], v_recv.at[0]).wait()

    @pl.loop(0, HALF // 64)
    def _(i):
        r = rows(i * 64, 64)
        middle = hid[r, :].astype(F32) + v_acc[r, :] + v_recv[0, r, :].astype(F32)
        v_mid[r, :] = middle
        hat, _inv = norm_stats(middle)
        v_n2[rows(mine + i * 64, 64), :] = (hat * v_param[2:3, :] + v_param[3:4, :]).astype(BF16)

    exchange_rows(4, v_n2).start()
    if net:
        g3.line(1, 2)
        g2.finish()

    for half, start in enumerate((mine, theirs)):
        if half == 1:
            swap(pos, v_n2.at[rows(theirs, HALF)], v_n2.at[rows(theirs, HALF)], swsem, 4).wait_recv()

        @pl.loop(0, 6)
        def _(tile):
            b = lax.div(tile, 3)
            cols = pl.ds(pl.multiple_of(lax.rem(tile, 3) * 256, 256), 256)
            pre = mm(v_n2[rows(start, HALF), :], v_up[b, :, :, cols].reshape(D, 256))
            square = pre * pre
            bend = jnp.tanh(pre * (GELU_C + GELU_C * GELU_A * square))
            half_up = 0.5 + 0.5 * bend
            act = pre * half_up
            v_act[b, rows(start, HALF), cols] = act.astype(BF16)
            slope = half_up + act * (1.0 - bend) * (GELU_C + 3.0 * GELU_C * GELU_A * square)
            v_slope[b, rows(start, HALF), cols] = slope.astype(BF16)

        if net and half == 0:
            g3.side(0, 1, 2, 3)

    exchange_rows(4, v_n2).wait_send()
    transpose_rows(v_n2, v_n2T)

    def tile_of(tile):
        return lax.div(tile, 3), pl.ds(pl.multiple_of(lax.rem(tile, 3) * 256, 256), 256)

    @pl.loop(0, 6)
    def _(tile):
        b, cols = tile_of(tile)
        res = mm(v_upsT[...], v_act[b, :, cols])
        v_p3[b, :, :, cols] = res.astype(BF16).reshape(NB, RB, 256)

    if net:
        s3.start()
        sz.start()
        g3.finish()
        gz.finish()
        for g in (go, q0, q1, q2):
            g.drain()

    @pl.loop(0, 6)
    def _(tile):
        b, cols = tile_of(tile)
        res = mm(v_ups[...], v_down[b, :, :, cols].reshape(D, 256))
        pre = (res * v_slope[b, :, cols].astype(F32)).astype(BF16)
        v_slope[b, :, cols] = pre
        res = mm(v_n2T[...], pre)
        v_p2[b, :, :, cols] = res.astype(BF16).reshape(NB, RB, 256)

    if net:
        s2.start()
    for half, start in enumerate((theirs, mine)):
        res = mm(v_slope[0, rows(start, HALF), :], v_up[0].reshape(D, D), NT)
        res += mm(v_slope[1, rows(start, HALF), :], v_up[1].reshape(D, D), NT)
        if half == 0:
            v_send[0] = res.astype(BF16)
            exchange(5, v_send.at[0], v_recv.at[0]).start()
            if net:
                s3.mid1()
        else:
            v_acc[...] = res
    exchange(5, v_send.at[0], v_recv.at[0]).wait()
    v_sums[...] = jnp.zeros_like(v_sums)

    def norm_back(upper, values, gain, at):
        hat, inv = norm_stats(values)
        scaled = upper * gain
        first = jnp.mean(scaled, -1, keepdims=True)
        second = jnp.mean(scaled * hat, -1, keepdims=True)
        v_sums[at : at + 1, :] += jnp.sum(upper * hat, 0, keepdims=True)
        v_sums[at + 1 : at + 2, :] += jnp.sum(upper, 0, keepdims=True)
        return inv * (scaled - first - hat * second)

    @pl.loop(0, HALF // 64)
    def _(i):
        r = rows(i * 64, 64)
        wide = rows(mine + i * 64, 64)
        upper = v_acc[r, :] + v_recv[0, r, :].astype(F32)
        d_mid = v_ups[wide, :].astype(F32) + norm_back(upper, v_mid[r, :], v_param[2:3, :], 2)
        o_in[r, :] = d_mid
        v_low[wide, :] = d_mid.astype(BF16)

    exchange_rows(6, v_low).start()
    if net:
        s3.mid0()
    for half, start in enumerate((mine, theirs)):
        if half == 1:
            swap(pos, v_low.at[rows(theirs, HALF)], v_low.at[rows(theirs, HALF)], swsem, 6).wait_recv()
        res = mm(v_low[rows(start, HALF), :], w_out).astype(BF16)
        for j in range(3):
            v_dctx[j, rows(start, HALF), :] = res[:, 128 * j : 128 * j + 128]
    transpose_rows(v_low, v_lowT)
    res = mm(v_lowT[...], cat([v_ctx[j] for j in range(3)])).astype(BF16)
    for j in range(3):
        pack_head(res[:, 128 * j : 128 * j + 128], v_ro, j)
    if net:
        so.start()

    @pl.loop(0, 3)
    def _(pair):
        if net:
            on(pair, 1, sz.cross2)
            on(pair, 2, s2.mid0, s2.join, so.mid1, so.mid0, sz.cross1)

        v_dk[...] = jnp.zeros_like(v_dk)
        v_dv[...] = jnp.zeros_like(v_dv)
        for i in range(4):
            n = 256 * (i + 1)
            q = v_qkv[pair, 256 * i : n, :]
            up = v_dctx[pair, 256 * i : n, :]
            qs = [only(q, h) for h in range(2)]
            ups = [only(up, h) for h in range(2)]
            dq = jnp.zeros((256, 128), F32)
            probs = [[], []]
            grads = [[], []]
            for h in range(2):
                lse = v_lse[pair, h : h + 1, 256 * i : n]
                delta = jnp.zeros((1, 256), F32)
                for j in range(i + 1):
                    at = slice(256 * j, 256 * j + 256)
                    s = mm(v_qkv[3 + pair, at, :], qs[h], NT)
                    p = jnp.exp(s - lse)
                    if j == i:
                        key = lax.broadcasted_iota(jnp.int32, s.shape, 0)
                        query = lax.broadcasted_iota(jnp.int32, s.shape, 1)
                        p = jnp.where(key <= query, p, 0.0)
                    dp = mm(v_qkv[6 + pair, at, :], ups[h], NT)
                    delta += jnp.sum(p * dp, 0, keepdims=True)
                    probs[h].append(p)
                    grads[h].append(dp)
                for j in range(i + 1):
                    grads[h][j] = (probs[h][j] * (grads[h][j] - delta)).astype(BF16)
                    probs[h][j] = probs[h][j].astype(BF16)
            for j in range(i + 1):
                at = slice(256 * j, 256 * j + 256)
                for h in range(2):
                    k = only(v_qkv[3 + pair, at, :], h)
                    dq += mm(grads[h][j], k, TN)
                v_dv[at, :] += mm(cat([probs[0][j], probs[1][j]]), jnp.concatenate(ups, axis=0))
                v_dk[at, :] += mm(cat([grads[0][j], grads[1][j]]), jnp.concatenate(qs, axis=0))
            v_qkv[pair, 256 * i : n, :] = (dq * HEAD_DIM**-0.5).astype(BF16)
            if net and i == 2:
                on(pair, 0, s3.join, s2.mid1)
        v_qkv[3 + pair] = v_dk[...].astype(BF16)
        v_qkv[6 + pair] = v_dv[...].astype(BF16)
        res = mm(v_nrmT[...], cat([v_qkv[3 * part + pair] for part in range(3)])).astype(BF16)
        for part in range(3):
            pack_head(res[:, 128 * part : 128 * part + 128], v_rq, 3 * pair + part)
        if net:
            sq(pair).start()

    w_qkv = cat([v_wh[3 * j + part] for part in range(3) for j in range(3)])
    if net:
        p0, p1, p2 = sq(0), sq(1), sq(2)
        p0.mid1()
        p0.mid0()
    for half, start in enumerate((theirs, mine)):
        lhs = cat([v_qkv[i, rows(start, HALF), :] for i in range(9)])
        res = mm(lhs, w_qkv, NT)
        if half == 0:
            v_send[1] = res.astype(BF16)
            exchange(7, v_send.at[1], v_recv.at[1]).start()
            if net:
                p1.mid1()
                p1.mid0()
        else:
            v_acc[...] = res
    if net:
        so.join()
    exchange(7, v_send.at[1], v_recv.at[1]).wait()

    @pl.loop(0, HALF // 64)
    def _(i):
        r = rows(i * 64, 64)
        upper = v_acc[r, :] + v_recv[1, r, :].astype(F32)
        o_in[r, :] = o_in[r, :] + norm_back(upper, hid[r, :].astype(F32), v_param[0:1, :], 0)

    v_swap[0] = v_sums[...]
    exchange(8, v_swap.at[0], v_swap.at[1]).start()
    if net:
        p0.join()
        p2.mid1()
        p2.mid0()
    exchange(8, v_swap.at[0], v_swap.at[1]).wait()
    both = v_swap[0] + v_swap[1]
    if net:
        for dd in range(NB):
            piece = cat([both[:, RB * dd : RB * dd + RB], jnp.zeros((8, 128 - RB), F32)])
            v_p0[0, dd] = piece
            v_p0[1, dd] = piece
        s0.start()

    for half, start in enumerate((theirs, mine)):
        res = mm(v_act[0, rows(start, HALF), :], v_down[0].reshape(D, D), NT)
        res += mm(v_act[1, rows(start, HALF), :], v_down[1].reshape(D, D), NT)
        if half == 0:
            v_send[0] = res.astype(BF16)
            exchange(9, v_send.at[0], v_recv.at[0]).start()
            if net:
                p1.join()
        else:
            o_block[...] = v_mid[...] + res
    if net:
        p2.join()
    exchange(9, v_send.at[0], v_recv.at[0]).wait()
    o_block[...] += v_recv[0].astype(F32)
    if net:
        s3.finish(o_down.at[:, left])
        sz.finish(o_down.at[:, right])
        s2.finish(o_up)
        so.finish(f_o)
        o_out[...] = cat([unfold(f_o[j]) for j in range(3)]).T
        p0.finish(f_q.at[0])
        p1.finish(f_q.at[1])
        p2.finish(f_q.at[2])
        for part in range(3):
            o_qkv[part] = cat([unfold(f_q[j, part]) for j in range(3)])
        s0.finish(v_swap.at[0, :, 0:128])
        o_small[...] = pltpu.roll(v_swap[0, :, 0:128], lax.rem(128 - 24 * pos.t, 128), 1)[:, 0:24]
        for g in (g0, g2, g3, gz, s0, so, s2, s3, sz, p0, p1, p2):
            g.drain()
    else:
        o_small[...] = both
        o_qkv[...] = v_rq[...]
        o_out[...] = v_ro[...]
        o_up[...] = v_p2[...]
        o_down[...] = v_p3[...]
    exchange_rows(6, v_low).wait_send()


def fold_rows(block):
    return block.reshape(2, 48, 3, 64).transpose(2, 1, 0, 3).reshape(3, 48, 128)


def unfold_rows(packed):
    return packed.reshape(3, 48, 2, 64).transpose(2, 1, 0, 3).reshape(RB, 192)


def shards(
    hidden_in, cotangent, group_ids, weight_table, table_index, qkv_weight, out_weight, up_weight, down_weight,
    norm1_gain, norm1_bias, norm2_gain, norm2_bias,
):
    n_dp, n_t = lax.axis_size("dp"), lax.axis_size("tensor")
    net = n_dp == NB and n_t == 4
    core = lax.rem(lax.axis_index("tensor"), 2)
    scale_tokens = hidden_in.shape[0] * n_dp * n_t / GROUPS
    ids = group_ids.reshape(1, HALF)
    down = down_weight.T
    vm, dma = pltpu.VMEM, pltpu.SemaphoreType.DMA
    vspec = pl.BlockSpec(memory_space=pltpu.VMEM)
    aspec = pl.BlockSpec(memory_space=pl.ANY)
    norm_vectors = (norm1_gain, norm1_bias, norm2_gain, norm2_bias)
    s_q, s_o, s_w = (3, 48, 128), (3, 48, 128), (RB, D)
    if net:
        vectors = [v.reshape(1, RB) for v in norm_vectors]
        table, weights = table_index.reshape(1, GROUPS), weight_table
        given = [qkv_weight.transpose(1, 0, 2), out_weight, up_weight, down, *vectors]
        weight_spec = pl.BlockSpec(memory_space=pltpu.SMEM)
        given_specs = [vspec] * len(given)
        grads = [((8, 24), F32), ((3, RB, 192), F32), ((192, RB), F32), (s_w, F32), (s_w, F32)]
        nets = [vm((2, NB, 8, 128), F32), vm((2 * NB, 8, 128), F32), dma((2 * NB,)), dma((2 * NB,))]
        nets += [vm((3, 2, 4) + s_q, BF16), vm((3, 8) + s_q, BF16)]
        for s in (s_o, s_w, (RB, CUT)):
            nets += [vm((2, 4) + s, BF16), vm((8,) + s, BF16)]
        nets += [vm((4, 4, RB, D - CUT), BF16), vm((3, RB, D - CUT), BF16)]
        nets += [vm((3,) + s_q, F32), vm(s_o, F32)]
        nets += [dma((7, 4, 4)), dma((8, 2, NB)), dma((5, 4)), dma((7, 4, 4)), dma((7, 4, 4)), dma((5, 4)), dma((5, 4))]
    else:

        def whole(block, axis):
            full = lax.all_gather(block, "dp", axis=axis, tiled=True)
            every = lax.all_gather(full, "tensor", axis=0)
            return lax.dynamic_index_in_dim(every.reshape((n_t // 2, 2) + full.shape), core, 1, keepdims=False)

        heads = jnp.concatenate([qkv_weight.transpose(1, 0, 2), out_weight.T[None]], axis=0)
        heads = whole(heads, 1).reshape(2, 4, NB, RB, 192).transpose(0, 2, 1, 3, 4)
        folded = jax.vmap(jax.vmap(jax.vmap(fold_rows)))(heads)
        given = [
            jnp.pad(lax.all_gather(jnp.stack(norm_vectors).astype(F32), "dp", axis=1, tiled=True), ((0, 4), (0, 0))),
            folded[:, :, :3].transpose(0, 1, 3, 2, 4, 5).reshape(2, NB, 9, 48, 128),
            folded[:, :, 3],
            whole(up_weight, 0).reshape(2, NB, RB, D),
            whole(down, 0).reshape(2, NB, RB, D),
        ]
        member = (group_ids[:, None] == jnp.arange(GROUPS, dtype=jnp.int32)[None, :]).astype(F32)
        counts = lax.psum(jnp.sum(member, 0), ("dp", "tensor"))
        hits = table_index[:, None] == jnp.arange(TABLE, dtype=jnp.int32)[None, :]
        scale = jnp.sum(jnp.where(hits, weight_table[None, :], 0.0), 1) * scale_tokens / jnp.maximum(counts, 1.0)
        weights = jnp.pad(scale[None, :], ((0, 7), (0, 128 - GROUPS)))
        table = counts.reshape(1, GROUPS)
        weight_spec = vspec
        given_specs = [vspec, aspec, aspec, aspec, aspec]
        grads = [((8, D), F32), ((2, NB, 9, 48, 128), BF16), ((2, NB, 3, 48, 128), BF16)]
        grads += [((2, NB) + s_w, BF16), ((2, NB) + s_w, BF16)]
        nets = []
    shapes = [((HALF, D), F32), ((1, GROUPS), F32), ((HALF, D), F32), *grads]
    outs = pl.pallas_call(
        functools.partial(block_kernel, net, scale_tokens, 5 + len(given)),
        out_shape=[jax.ShapeDtypeStruct(*s) for s in shapes],
        in_specs=[vspec, vspec, vspec, vspec, weight_spec, *given_specs],
        out_specs=[vspec] * len(shapes),
        scratch_shapes=[
            vm((2, NB, 8, 128), F32), vm((3, 8, 128), F32), vm((8, D), F32), vm((8, 128), jnp.int32), vm((9, 48, 128), BF16),
            vm((3, 48, 128), BF16), vm((2, NB, 9, 48, 128), BF16), vm((2, NB, 3, 48, 128), BF16), vm((2, NB, RB, D), BF16),
            vm((2, NB, RB, D), BF16), vm((9, D, 128), BF16), vm((3, D, 128), BF16),
            vm((LENGTH, D), BF16), vm((D, LENGTH), BF16), vm((LENGTH, D), BF16), vm((D, LENGTH), BF16), vm((LENGTH, D), BF16),
            vm((D, LENGTH), BF16), vm((9, LENGTH, 128), BF16), vm((3, 8, LENGTH), F32), vm((3, LENGTH, 128), BF16),
            vm((3, LENGTH, 128), BF16), vm((HALF, D), F32), vm((2, LENGTH, D), BF16), vm((2, LENGTH, D), BF16),
            vm((2, HALF, D), BF16), vm((2, HALF, D), BF16), vm((HALF, D), F32), vm((LENGTH, 128), F32), vm((LENGTH, 128), F32),
            vm((2, NB, RB, D), BF16), vm((2, NB, RB, D), BF16), vm((8, D), F32), vm((2, 8, D), F32),
            dma((2, 10)), dma((4,)), *nets,
        ],
        compiler_params=pltpu.CompilerParams(collective_id=0, has_side_effects=True, vmem_limit_bytes=VMEM_LIMIT),
        name="block",
    )(hidden_in, cotangent, ids, table, weights, *given)
    block_output, counts, input_grad, sums, grad_qkv, grad_out, grad_up, grad_down = outs
    if net:
        norms = [sums[i] for i in range(4)]
        grad_qkv = grad_qkv.transpose(1, 0, 2)
    else:

        def owned(part):
            base = jnp.zeros((n_t // 2, 2) + part.shape[1:], F32)
            base = lax.dynamic_update_index_in_dim(base, part.astype(F32), core, 1)
            flat = base.reshape((n_t,) + part.shape[1:])
            mine = lax.psum_scatter(flat, "tensor", scatter_dimension=0, tiled=False)
            return lax.psum_scatter(mine, "dp", scatter_dimension=0, tiled=True)

        parts = grad_qkv.reshape(2, NB, 3, 3, 48, 128).transpose(0, 1, 3, 2, 4, 5)
        parts = jax.vmap(jax.vmap(jax.vmap(unfold_rows)))(parts)
        grad_qkv = owned(parts.transpose(0, 1, 3, 2, 4).reshape(2, D, 3, 192))
        grad_out = owned(jax.vmap(jax.vmap(unfold_rows))(grad_out).reshape(2, D, 192)).T
        grad_up, grad_down = owned(grad_up.reshape(2, D, D)), owned(grad_down.reshape(2, D, D))
        half_sums = jnp.where(core == 0, sums, 0.0)
        norms = [lax.psum_scatter(half_sums[i], ("dp", "tensor"), scatter_dimension=0, tiled=True) for i in range(4)]
    return (
        block_output,
        input_grad,
        grad_qkv,
        grad_out,
        grad_up,
        grad_down.T,
        norms[0],
        norms[1],
        norms[2],
        norms[3],
        counts.reshape(GROUPS),
    )


def solution(mesh):
    both = ("dp", "tensor")
    return jax.shard_map(
        shards,
        mesh=mesh,
        in_specs=(
            P(both, None), P(both, None), P(both), P(), P(), P("dp", None, "tensor"), P("tensor", "dp"), P("dp", "tensor"),
            P("tensor", "dp"), P("dp"), P("dp"), P("dp"), P("dp"),
        ),
        out_specs=(
            P(both, None), P(both, None), P("dp", None, "tensor"), P("tensor", "dp"), P("dp", "tensor"), P("tensor", "dp"),
            P(both), P(both), P(both), P(both), P(),
        ),
        check_vma=False,
    )
```

```python
import functools

import jax
import jax.numpy as jnp
from jax import lax
from jax.experimental import pallas as pl
from jax.experimental.pallas import tpu as pltpu
from jax.sharding import PartitionSpec as P

D = 768
HEAD_DIM = 64
LENGTH = 1024
HALF = 512
GROUPS = 16
TABLE = 8
NB = 8
RB = D // NB
CUT = 512
EPSILON = 1e-05
MASKED_SCORE = -1e30
GELU_C = 0.7978845608028654
GELU_A = 0.044715
MESH = pl.DeviceIdType.MESH
F32 = jnp.float32
BF16 = jnp.bfloat16
NT = (((1,), (1,)), ((), ()))
TN = (((0,), (0,)), ((), ()))
NN = (((1,), (0,)), ((), ()))
VMEM_LIMIT = 58_000_000
WIDE_VMEM_LIMIT = 66_000_000


def mm(a, b, dims=NN):
    return lax.dot_general(a, b, dims, preferred_element_type=F32)


class Place:
    def __init__(self):
        self.d = lax.axis_index("dp")
        self.t = lax.axis_index("tensor")
        self.z = lax.div(self.d, 2)
        self.y = lax.rem(self.d, 2)
        self.x = lax.div(self.t, 2)
        self.c = lax.rem(self.t, 2)
        c = self.c
        self.sibling = (self.d, self.t + 1 - 2 * c)
        self.x1 = lax.rem(self.x + c, 2)
        self.y1 = lax.rem(self.y + 1 - c, 2)
        self.x2 = lax.rem(self.x + 1 - c, 2)
        self.y2 = lax.rem(self.y + c, 2)
        self.p1 = (2 * self.z + self.y1, 2 * self.x1 + c)
        self.p2 = (2 * self.z + self.y2, 2 * self.x2 + c)
        self.others = [lax.rem(self.z + k, 4) for k in (1, 2, 3)]
        self.sources = [lax.rem(self.z + k, 4) for k in (3, 2, 1)]

    def at_z(self, zz):
        return (2 * zz + self.y, self.t)


def entry_barrier(pos, net):
    bar = pltpu.get_barrier_semaphore()
    pl.semaphore_signal(bar, inc=1, device_id=pos.sibling, device_id_type=MESH)
    if not net:
        pl.semaphore_wait(bar, 1)
        return
    for peer in (pos.p1, pos.p2, *[pos.at_z(zz) for zz in pos.others]):
        pl.semaphore_signal(bar, inc=1, device_id=peer, device_id_type=MESH)
    pl.semaphore_wait(bar, 6)


class Gather:
    def __init__(self, pos, g, own, slot, ssem, rsem):
        self.pos, self.g, self.own, self.slot = pos, g, own, slot
        self.ssem, self.rsem = ssem, rsem

    def copy(self, b, dd, link, i, dev, src=None):
        slot = self.slot(b, dd)
        return pltpu.make_async_remote_copy(
            src_ref=slot if src is None else src,
            dst_ref=slot,
            send_sem=self.ssem.at[self.g, link, i],
            recv_sem=self.rsem.at[self.g, b, dd],
            device_id=dev,
            device_id_type=MESH,
        )

    def wait(self, b, dd):
        self.copy(b, dd, 0, 0, self.pos.p1).wait_recv()

    def own_z(self):
        p = self.pos
        for zz in p.others:
            self.copy(p.x, p.d, 0, zz, p.at_z(zz), self.own).start()

    def own_xy(self):
        p = self.pos
        self.copy(p.x, p.d, 1, p.z, p.p1, self.own).start()
        self.copy(p.x, p.d, 2, p.z, p.p2, self.own).start()

    def line(self, *ks):
        p = self.pos
        for k in ks:
            zz = p.sources[k]
            dd = 2 * zz + p.y
            self.wait(p.x, dd)
            self.copy(p.x, dd, 1, zz, p.p1).start()
            self.copy(p.x, dd, 2, zz, p.p2).start()

    def side(self, *ks):
        p = self.pos
        for k in ks:
            zz = p.z if k == 0 else p.sources[k - 1]
            dd = 2 * zz + p.y1
            self.wait(p.x1, dd)
            self.copy(p.x1, dd, 3, zz, p.p2).start()

    def finish(self):
        p = self.pos
        for zz in range(4):
            self.wait(p.x2, 2 * zz + p.y2)
            self.wait(1 - p.x, 2 * zz + 1 - p.y)

    def drain(self):
        p = self.pos
        for zz in p.others:
            self.copy(p.x, p.d, 0, zz, p.at_z(zz), self.own).wait_send()
        for zz in range(4):
            self.copy(p.x, 2 * zz + p.y, 1, zz, p.p1).wait_send()
            self.copy(p.x, 2 * zz + p.y, 2, zz, p.p2).wait_send()
            self.copy(p.x1, 2 * zz + p.y1, 3, zz, p.p2).wait_send()


class GatherZ(Gather):
    def __init__(self, pos, g, own, slot, ssem, rsem, zsem):
        super().__init__(pos, g, own, slot, zsem, rsem)

    def copy(self, b, dd, link, i, dev, src=None):
        slot = self.slot(b, dd)
        return pltpu.make_async_remote_copy(
            src_ref=slot if src is None else src,
            dst_ref=slot,
            send_sem=self.ssem.at[link, i],
            recv_sem=self.rsem.at[self.g, b, dd],
            device_id=dev,
            device_id_type=MESH,
        )

    def column(self, col, zz):
        p = self.pos
        x, y = ((p.x, p.y), (p.x1, p.y1), (p.x2, p.y2), (1 - p.x, 1 - p.y))[col]
        return x, 2 * zz + y

    def own_xy(self):
        p = self.pos
        self.copy(p.x, p.d, 4, 0, p.p1, self.own).start()
        self.copy(p.x, p.d, 4, 1, p.p2, self.own).start()

    def side(self):
        p = self.pos
        b, dd = self.column(1, p.z)
        self.wait(b, dd)
        self.copy(b, dd, 4, 2, p.p2).start()

    def spread(self, *cols):
        p = self.pos
        for col in cols:
            b, dd = self.column(col, p.z)
            if col >= 2:
                self.wait(b, dd)
            for zz in p.others:
                self.copy(b, dd, col, zz, p.at_z(zz), self.own if col == 0 else None).start()

    def finish(self):
        for zz in self.pos.others:
            for col in range(4):
                self.wait(*self.column(col, zz))

    def drain(self):
        p = self.pos
        self.copy(p.x, p.d, 4, 0, p.p1, self.own).wait_send()
        self.copy(p.x, p.d, 4, 1, p.p2, self.own).wait_send()
        b, dd = self.column(1, p.z)
        self.copy(b, dd, 4, 2, p.p2).wait_send()
        for col in range(4):
            b, dd = self.column(col, p.z)
            for zz in p.others:
                self.copy(b, dd, col, zz, p.at_z(zz)).wait_send()


class Reduce:
    def __init__(self, pos, g, slot, r2, rz, ssem, rsem):
        self.pos, self.g, self.slot, self.r2, self.rz = pos, g, slot, r2, rz
        self.ssem, self.rsem = ssem, rsem

    def copy(self, src, dst, link, i, dev, j=None):
        return pltpu.make_async_remote_copy(
            src_ref=src,
            dst_ref=dst,
            send_sem=self.ssem.at[self.g, link, i],
            recv_sem=self.rsem.at[self.g, link, i if j is None else j],
            device_id=dev,
            device_id_type=MESH,
        )

    def to_p2(self, which, zz):
        p = self.pos
        b, dd = (p.x2, 2 * zz + p.y2) if which == 0 else (1 - p.x, 2 * zz + 1 - p.y)
        return self.copy(self.slot(b, dd), self.r2.at[which, zz], which, zz, p.p2)

    def to_p1(self, zz):
        p = self.pos
        return self.copy(self.slot(p.x1, 2 * zz + p.y1), self.rz.at[zz], 2, zz, p.p1)

    def to_z(self, zz):
        p = self.pos
        return self.copy(self.slot(p.x, 2 * zz + p.y), self.rz.at[4 + p.z], 3, zz, p.at_z(zz), p.z)

    def from_z(self, zz):
        p = self.pos
        return self.copy(self.slot(p.x, p.d), self.rz.at[4 + zz], 3, zz, p.at_z(zz))

    def add(self, b, dd, other):
        ref = self.slot(b, dd)
        ref[...] = (ref[...].astype(F32) + other.astype(F32)).astype(ref.dtype)

    def start(self):
        for which in (1, 0):
            for zz in range(4):
                self.to_p2(which, zz).start()

    def mid1(self):
        p = self.pos
        for zz in range(4):
            self.to_p2(1, zz).wait_recv()
            self.add(p.x1, 2 * zz + p.y1, self.r2[1, zz])
            self.to_p1(zz).start()

    def mid0(self):
        p = self.pos
        for zz in range(4):
            self.to_p2(0, zz).wait_recv()
            self.add(p.x, 2 * zz + p.y, self.r2[0, zz])

    def join(self):
        p = self.pos
        for zz in range(4):
            self.to_p1(zz).wait_recv()
            self.add(p.x, 2 * zz + p.y, self.rz[zz])
        for zz in p.others:
            self.to_z(zz).start()

    def finish(self, out):
        p = self.pos
        total = self.slot(p.x, p.d)[...].astype(F32)
        for zz in p.others:
            self.from_z(zz).wait_recv()
            total += self.rz[4 + zz].astype(F32)
        out[...] = total

    def drain(self):
        for zz in range(4):
            self.to_p2(1, zz).wait_send()
            self.to_p2(0, zz).wait_send()
            self.to_p1(zz).wait_send()
        for zz in self.pos.others:
            self.to_z(zz).wait_send()


class ReduceZ:
    def __init__(self, pos, slot, rl, rx, ssem, rsem):
        self.pos, self.slot, self.rl, self.rx = pos, slot, rl, rx
        self.ssem, self.rsem = ssem, rsem

    def column(self, col, zz):
        p = self.pos
        x, y = ((p.x, p.y), (p.x1, p.y1), (p.x2, p.y2), (1 - p.x, 1 - p.y))[col]
        return self.slot(x, 2 * zz + y)

    def copy(self, src, dst, link, i, dev, j=None):
        return pltpu.make_async_remote_copy(
            src_ref=src,
            dst_ref=dst,
            send_sem=self.ssem.at[link, i],
            recv_sem=self.rsem.at[link, i if j is None else j],
            device_id=dev,
            device_id_type=MESH,
        )

    def to_z(self, col, zz):
        p = self.pos
        return self.copy(self.column(col, zz), self.rl.at[col, p.z], col, zz, p.at_z(zz), p.z)

    def from_z(self, col, zz):
        p = self.pos
        return self.copy(self.column(col, p.z), self.rl.at[col, zz], col, zz, p.at_z(zz))

    def to_p2(self, which):
        return self.copy(self.column(2 + which, self.pos.z), self.rx.at[which], 4, which, self.pos.p2)

    def to_p1(self):
        return self.copy(self.column(1, self.pos.z), self.rx.at[2], 4, 2, self.pos.p1)

    def start(self):
        for col in (3, 2, 1, 0):
            for zz in self.pos.others:
                self.to_z(col, zz).start()

    def settle(self, col):
        p = self.pos
        ref = self.column(col, p.z)
        total = ref[...].astype(F32)
        for zz in p.others:
            self.from_z(col, zz).wait_recv()
            total += self.rl[col, zz].astype(F32)
        ref[...] = total.astype(ref.dtype)

    def cross2(self):
        for which in (1, 0):
            self.settle(2 + which)
            self.to_p2(which).start()
        self.settle(1)
        self.settle(0)

    def add(self, col, i):
        ref = self.column(col, self.pos.z)
        ref[...] = (ref[...].astype(F32) + self.rx[i].astype(F32)).astype(ref.dtype)

    def cross1(self):
        self.to_p2(1).wait_recv()
        self.add(1, 1)
        self.to_p1().start()
        self.to_p2(0).wait_recv()
        self.add(0, 0)

    def finish(self, out):
        self.to_p1().wait_recv()
        out[...] = self.column(0, self.pos.z)[...].astype(F32) + self.rx[2].astype(F32)

    def drain(self):
        self.to_p2(0).wait_send()
        self.to_p2(1).wait_send()
        self.to_p1().wait_send()
        for col in range(4):
            for zz in self.pos.others:
                self.to_z(col, zz).wait_send()


class Scatter:
    def __init__(self, pos, part, land, ssem, rsem):
        self.pos, self.part, self.land, self.ssem, self.rsem = pos, part, land, ssem, rsem
        self.me = 2 * pos.d + pos.x

    def copy(self, i, place):
        b, dd = i % 2, i // 2
        return pltpu.make_async_remote_copy(
            src_ref=self.part.at[b, dd],
            dst_ref=self.land.at[place],
            send_sem=self.ssem.at[i],
            recv_sem=self.rsem.at[place],
            device_id=(dd, 2 * b + self.pos.c),
            device_id_type=MESH,
        )

    def each(self, do):
        for i in range(2 * NB):

            @pl.when(i != self.me)
            def _():
                do(i)

    def start(self):
        self.each(lambda i: self.copy(i, self.me).start())

    def finish(self, out):
        out[...] = self.part[self.pos.x, self.pos.d]

        def take(i):
            self.copy(i, i).wait_recv()
            out[...] += self.land[i]

        self.each(take)

    def drain(self):
        self.each(lambda i: self.copy(i, self.me).wait_send())


def rows(start, size):
    return pl.ds(pl.multiple_of(start, size), size)


def swap(pos, src, dst, sems, i):
    return pltpu.make_async_remote_copy(
        src_ref=src,
        dst_ref=dst,
        send_sem=sems.at[0, i],
        recv_sem=sems.at[1, i],
        device_id=pos.sibling,
        device_id_type=MESH,
    )


def norm_stats(values):
    center = values - jnp.mean(values, -1, keepdims=True)
    inv = lax.rsqrt(jnp.mean(center * center, -1, keepdims=True) + EPSILON)
    return center * inv, inv


def lane_half(shape, which):
    lane = lax.broadcasted_iota(jnp.int32, shape, 1)
    return (lane < HEAD_DIM) if which == 0 else (lane >= HEAD_DIM)


def only(values, which):
    return jnp.where(lane_half(values.shape, which), values, jnp.zeros_like(values))


def roll_half(values):
    return pltpu.roll(values.astype(F32), HEAD_DIM, 1).astype(BF16)


def unpack_heads(raw, first, count, wh):
    @pl.loop(0, NB)
    def _(dd):
        at = pl.multiple_of(dd * RB, 16)
        for i in range(count):
            one, two = raw[0, dd, first + i], raw[1, dd, first + i]
            left = lane_half(one.shape, 0)
            wh[first + i, pl.ds(at, 48)] = jnp.where(left, one, roll_half(two))
            wh[first + i, pl.ds(at + 48, 48)] = jnp.where(left, roll_half(one), two)


def pack_head(grad, raw, i):
    left = lane_half((48, 128), 0)
    for dd in range(NB):
        top, bottom = grad[RB * dd : RB * dd + 48], grad[RB * dd + 48 : RB * dd + 96]
        raw[0, dd, i] = jnp.where(left, top, roll_half(bottom))
        raw[1, dd, i] = jnp.where(left, roll_half(top), bottom)


def fold(block):
    return jnp.concatenate([block[0:48], block[48:96]], axis=1)


def unfold(block):
    return jnp.concatenate([block[:, 0:64], block[:, 64:128]], axis=0)


def transpose_rows(src, dst):
    @pl.loop(0, LENGTH // 128)
    def _(i):
        r = rows(i * 128, 128)
        dst[:, r] = src[r, :].T


def cat(pieces):
    return jnp.concatenate(pieces, axis=1)


def block_kernel(net, scale_tokens, nin, *refs):
    h_hid, h_cot, ids, table, weights, *given = refs[:nin]
    o_block, o_counts, o_in, o_small, o_qkv, o_out, o_up, o_down = refs[nin : nin + 8]
    (
        v_small, v_cnt, v_param, v_index, own_q, own_o, v_rq, v_ro, v_up, v_down, v_wh, v_wo,
        v_nrm, v_nrmT, v_n2, v_n2T, v_ups, v_upsT, v_qkv, v_lse, v_ctx, v_dctx, v_mid, v_act, v_slope,
        v_send, v_recv, v_acc, v_dk, v_dv, v_p2, v_p3, v_sums, v_swap, hid, cot, swsem, lsem, *nets,
    ) = refs[nin + 8 :]
    v_low, v_lowT = v_nrm, v_upsT
    pos = Place()
    fetches = [(h_hid, hid), (h_cot, cot)]
    if net:
        fetches = [(given[2], v_up.at[pos.x, pos.d]), (given[3], v_down.at[pos.x, pos.d]), *fetches]
    fetched = [pltpu.make_async_copy(a, b, lsem.at[i]) for i, (a, b) in enumerate(fetches)]
    for cp in fetched:
        cp.start()
    mine = pos.c * HALF
    theirs = HALF - mine

    def exchange(i, src, dst):
        return swap(pos, src, dst, swsem, i)

    def exchange_rows(i, ref):
        return swap(pos, ref.at[rows(mine, HALF)], ref.at[rows(mine, HALF)], swsem, i)

    row_ids = jnp.broadcast_to(ids[...].astype(F32), (128, HALF)).T
    member = row_ids == lax.broadcasted_iota(jnp.int32, (HALF, 128), 1).astype(F32)
    own_counts = jnp.sum(member.astype(F32), 0, keepdims=True)

    if net:
        qkv_w, out_w, _, _, *vectors = given
        own_up, own_down = v_up.at[pos.x, pos.d], v_down.at[pos.x, pos.d]
        (
            v_p0, land_0, ssem_0, rsem_0, r2_q, rz_q, r2_o, rz_o, r2_2, rz_2, r2_3, rz_3, rl_3, rx_3, f_q, f_o,
            gssem, grsem, gzsem, rssem, rrsem, rzssem, rzrsem,
        ) = nets
        v_cnt[2] = jnp.zeros((8, 128), F32)
        for i in range(4):
            v_cnt[2, i : i + 1, 0:RB] = vectors[i][...].astype(F32)
        v_cnt[2, 4:5, :] = own_counts
        out_rows = out_w[...].T
        for j in range(3):
            for part in range(3):
                own_q[3 * j + part] = fold(qkv_w[part][:, 64 * j : 64 * j + 64])
            own_o[j] = fold(out_rows[:, 64 * j : 64 * j + 64])
        entry_barrier(pos, net)
        left, right = slice(0, CUT), slice(CUT, D)
        g0 = Gather(pos, 0, v_cnt.at[2], lambda b, dd: v_small.at[b, dd], gssem, grsem)
        go = Gather(pos, 1, own_o, lambda b, dd: v_ro.at[b, dd], gssem, grsem)
        g2 = Gather(pos, 2, own_up, lambda b, dd: v_up.at[b, dd], gssem, grsem)
        g3 = Gather(pos, 3, own_down.at[:, left], lambda b, dd: v_down.at[b, dd, :, left], gssem, grsem)
        gz = GatherZ(pos, 7, own_down.at[:, right], lambda b, dd: v_down.at[b, dd, :, right], gssem, grsem, gzsem)
        s0 = Scatter(pos, v_p0, land_0, ssem_0, rsem_0)
        so = Reduce(pos, 1, lambda b, dd: v_ro.at[b, dd], r2_o, rz_o, rssem, rrsem)
        s2 = Reduce(pos, 2, lambda b, dd: v_p2.at[b, dd], r2_2, rz_2, rssem, rrsem)
        s3 = Reduce(pos, 3, lambda b, dd: v_p3.at[b, dd, :, left], r2_3, rz_3, rssem, rrsem)
        sz = ReduceZ(pos, lambda b, dd: v_p3.at[b, dd, :, right], rl_3, rx_3, rzssem, rzrsem)

        def gq(j):
            at = pl.ds(3 * j, 3)
            return Gather(pos, 4 + j, own_q.at[at], lambda b, dd: v_rq.at[b, dd, at], gssem, grsem)

        def sq(j):
            at = pl.ds(3 * j, 3)
            return Reduce(pos, 4 + j, lambda b, dd: v_rq.at[b, dd, at], r2_q.at[j], rz_q.at[j], rssem, rrsem)

        q0, q1, q2 = gq(0), gq(1), gq(2)
        for g in (g0, q0, q1, q2, go):
            g.own_z()
        for g in (g0, q0, q1, q2, go):
            g.own_xy()
        for cp in fetched:
            cp.wait()
        g2.own_z()
        v_small[pos.x, pos.d] = v_cnt[2]
        v_rq[pos.x, pos.d] = own_q[...]
        v_ro[pos.x, pos.d] = own_o[...]
        for k in range(3):
            g0.line(k)
            q0.line(k)
        g0.side(0, 1, 2, 3)
        q0.side(0, 1, 2, 3)
        q1.line(0, 1, 2)
        g0.finish()
        v_param[...] = cat([v_small[pos.x, dd, :, 0:RB] for dd in range(NB)])
        total = v_small[0, 0] + v_small[1, 0]
        for dd in range(1, NB):
            total += v_small[0, dd] + v_small[1, dd]
        v_cnt[0] = total
        exchange(0, v_cnt.at[0], v_cnt.at[1]).start()
    else:
        vectors, *wide = given
        entry_barrier(pos, net)
        v_param[...] = vectors[...]
        cps = [pltpu.make_async_copy(a, b, lsem.at[2 + i]) for i, (a, b) in enumerate(zip(wide, (v_rq, v_ro, v_up, v_down)))]
        for cp in cps:
            cp.start()
        for cp in [*fetched, *cps]:
            cp.wait()

    @pl.loop(0, HALF // 64)
    def _(i):
        r = rows(i * 64, 64)
        hat, _inv = norm_stats(hid[r, :].astype(F32))
        v_nrm[rows(mine + i * 64, 64), :] = (hat * v_param[0:1, :] + v_param[1:2, :]).astype(BF16)

    exchange_rows(1, v_nrm).start()

    if net:
        exchange(0, v_cnt.at[0], v_cnt.at[1]).wait()
        counts = (v_cnt[0] + v_cnt[1])[4:5, :]
        v_index[...] = jnp.full(v_index.shape, -1, jnp.int32)
        v_index[0:1, 0:GROUPS] = table[...]
        index = v_index[0:1, :]
        weight = jnp.zeros((1, 128), F32)
        for r in range(TABLE):
            weight = weight + jnp.where(index == r, weights[r], 0.0)
        group_scale = weight * scale_tokens / jnp.maximum(counts, 1.0)
        o_counts[...] = counts[:, 0:GROUPS]
    else:
        o_counts[...] = table[...]
        group_scale = weights[0:1, :]
    row_scale = jnp.sum(jnp.where(member, group_scale, 0.0), 1, keepdims=True)
    v_ups[rows(mine, HALF), :] = (cot[...].astype(F32) * row_scale).astype(BF16)
    exchange_rows(2, v_ups).start()
    for i, ref, turned in ((1, v_nrm, v_nrmT), (2, v_ups, v_upsT)):
        exchange_rows(i, ref).wait_send()
        swap(pos, ref.at[rows(theirs, HALF)], ref.at[rows(theirs, HALF)], swsem, i).wait_recv()
        transpose_rows(ref, turned)

    def on(pair, k, *steps):
        @pl.when(pair == k)
        def _():
            for step in steps:
                step()

    @pl.loop(0, 3)
    def _(pair):
        if net:
            on(pair, 0, lambda: q1.side(0, 1, 2, 3), lambda: q2.line(0, 1, 2), g3.own_z)
            on(pair, 1, lambda: go.side(0, 1, 2, 3), lambda: g2.line(0))
            on(pair, 2, lambda: g2.line(2), lambda: g2.side(0), gz.side, lambda: gz.spread(0, 1))
            gq(pair).finish()
        unpack_heads(v_rq, 3 * pair, 3, v_wh)
        for half, start in enumerate((mine, theirs)):
            res = mm(v_nrm[rows(start, HALF), :], cat([v_wh[3 * pair + part] for part in range(3)])).astype(BF16)
            for part in range(3):
                piece = res[:, 128 * part : 128 * part + 128]
                if part == 0:
                    piece = (piece.astype(F32) * HEAD_DIM**-0.5).astype(BF16)
                v_qkv[3 * part + pair, rows(start, HALF), :] = piece
        if net:
            on(pair, 0, lambda: q2.side(0, 1, 2, 3), lambda: go.line(0, 1, 2), g2.own_xy)
            on(pair, 1, lambda: g2.line(1), gz.own_xy)

        def scores(i, h):
            q = v_qkv[pair, 256 * i : 256 * i + 256, :]
            pieces, peak = [], None
            for j in range(i + 1):
                k = only(v_qkv[3 + pair, 256 * j : 256 * j + 256, :], h)
                s = mm(k, q, NT)
                if j == i:
                    key = lax.broadcasted_iota(jnp.int32, s.shape, 0)
                    query = lax.broadcasted_iota(jnp.int32, s.shape, 1)
                    s = jnp.where(key <= query, s, MASKED_SCORE)
                top = jnp.max(s, 0, keepdims=True)
                peak = top if peak is None else jnp.maximum(peak, top)
                pieces.append(s)
            return pieces, peak

        tasks = [(i, h) for i in range(4) for h in range(2)]
        ahead = scores(*tasks[0])
        for at, (i, h) in enumerate(tasks):
            pieces, peak = ahead
            if at + 1 < len(tasks):
                ahead = scores(*tasks[at + 1])
            total = jnp.zeros((1, 256), F32)
            for j in range(i + 1):
                e = jnp.exp(pieces[j] - peak)
                total += jnp.sum(e, 0, keepdims=True)
                pieces[j] = e
            inv = 1.0 / total
            out = jnp.zeros((256, 128), F32) if h == 0 else out
            for j in range(i + 1):
                v = only(v_qkv[6 + pair, 256 * j : 256 * j + 256, :], h)
                out += mm((pieces[j] * inv).astype(BF16), v, TN)
            v_lse[pair, h : h + 1, 256 * i : 256 * i + 256] = peak + jnp.log(total)
            if h == 1:
                v_ctx[pair, 256 * i : 256 * i + 256, :] = out.astype(BF16)
            if net and (i, h) == (2, 1):
                on(pair, 2, lambda: g2.side(1))

    if net:
        g2.side(2, 3)
        g3.own_xy()
        g3.line(0)
        gz.spread(2, 3)
        go.finish()
    unpack_heads(v_ro, 0, 3, v_wo)

    w_out = cat([v_wo[j] for j in range(3)])
    for half, start in enumerate((theirs, mine)):
        lhs = cat([v_ctx[j, rows(start, HALF), :] for j in range(3)])
        res = mm(lhs, w_out, NT)
        if half == 0:
            v_send[0] = res.astype(BF16)
            exchange(3, v_send.at[0], v_recv.at[0]).start()
        else:
            v_acc[...] = res
    exchange(3, v_send.at[0], v_recv.at[0]).wait()

    @pl.loop(0, HALF // 64)
    def _(i):
        r = rows(i * 64, 64)
        middle = hid[r, :].astype(F32) + v_acc[r, :] + v_recv[0, r, :].astype(F32)
        v_mid[r, :] = middle
        hat, _inv = norm_stats(middle)
        v_n2[rows(mine + i * 64, 64), :] = (hat * v_param[2:3, :] + v_param[3:4, :]).astype(BF16)

    exchange_rows(4, v_n2).start()
    if net:
        g3.line(1, 2)
        g2.finish()

    for half, start in enumerate((mine, theirs)):
        if half == 1:
            swap(pos, v_n2.at[rows(theirs, HALF)], v_n2.at[rows(theirs, HALF)], swsem, 4).wait_recv()

        @pl.loop(0, 6)
        def _(tile):
            b = lax.div(tile, 3)
            cols = pl.ds(pl.multiple_of(lax.rem(tile, 3) * 256, 256), 256)
            pre = mm(v_n2[rows(start, HALF), :], v_up[b, :, :, cols].reshape(D, 256))
            square = pre * pre
            bend = jnp.tanh(pre * (GELU_C + GELU_C * GELU_A * square))
            half_up = 0.5 + 0.5 * bend
            act = pre * half_up
            v_act[b, rows(start, HALF), cols] = act.astype(BF16)
            slope = half_up + act * (1.0 - bend) * (GELU_C + 3.0 * GELU_C * GELU_A * square)
            v_slope[b, rows(start, HALF), cols] = slope.astype(BF16)

        if net and half == 0:
            g3.side(0, 1, 2, 3)

    exchange_rows(4, v_n2).wait_send()
    transpose_rows(v_n2, v_n2T)

    def tile_of(tile):
        return lax.div(tile, 3), pl.ds(pl.multiple_of(lax.rem(tile, 3) * 256, 256), 256)

    @pl.loop(0, 6)
    def _(tile):
        b, cols = tile_of(tile)
        res = mm(v_upsT[...], v_act[b, :, cols])
        v_p3[b, :, :, cols] = res.astype(BF16).reshape(NB, RB, 256)

    if net:
        s3.start()
        sz.start()
        g3.finish()
        gz.finish()
        for g in (go, q0, q1, q2):
            g.drain()

    @pl.loop(0, 6)
    def _(tile):
        b, cols = tile_of(tile)
        res = mm(v_ups[...], v_down[b, :, :, cols].reshape(D, 256))
        pre = (res * v_slope[b, :, cols].astype(F32)).astype(BF16)
        v_slope[b, :, cols] = pre
        res = mm(v_n2T[...], pre)
        v_p2[b, :, :, cols] = res.astype(BF16).reshape(NB, RB, 256)

    if net:
        s2.start()
    for half, start in enumerate((theirs, mine)):
        res = mm(v_slope[0, rows(start, HALF), :], v_up[0].reshape(D, D), NT)
        res += mm(v_slope[1, rows(start, HALF), :], v_up[1].reshape(D, D), NT)
        if half == 0:
            v_send[0] = res.astype(BF16)
            exchange(5, v_send.at[0], v_recv.at[0]).start()
            if net:
                s3.mid1()
        else:
            v_acc[...] = res
    exchange(5, v_send.at[0], v_recv.at[0]).wait()
    v_sums[...] = jnp.zeros_like(v_sums)

    def norm_back(upper, values, gain, at):
        hat, inv = norm_stats(values)
        scaled = upper * gain
        first = jnp.mean(scaled, -1, keepdims=True)
        second = jnp.mean(scaled * hat, -1, keepdims=True)
        v_sums[at : at + 1, :] += jnp.sum(upper * hat, 0, keepdims=True)
        v_sums[at + 1 : at + 2, :] += jnp.sum(upper, 0, keepdims=True)
        return inv * (scaled - first - hat * second)

    @pl.loop(0, HALF // 64)
    def _(i):
        r = rows(i * 64, 64)
        wide = rows(mine + i * 64, 64)
        upper = v_acc[r, :] + v_recv[0, r, :].astype(F32)
        d_mid = v_ups[wide, :].astype(F32) + norm_back(upper, v_mid[r, :], v_param[2:3, :], 2)
        o_in[r, :] = d_mid
        v_low[wide, :] = d_mid.astype(BF16)

    exchange_rows(6, v_low).start()
    if net:
        s3.mid0()
    for half, start in enumerate((mine, theirs)):
        if half == 1:
            swap(pos, v_low.at[rows(theirs, HALF)], v_low.at[rows(theirs, HALF)], swsem, 6).wait_recv()
        res = mm(v_low[rows(start, HALF), :], w_out).astype(BF16)
        for j in range(3):
            v_dctx[j, rows(start, HALF), :] = res[:, 128 * j : 128 * j + 128]
    transpose_rows(v_low, v_lowT)
    res = mm(v_lowT[...], cat([v_ctx[j] for j in range(3)])).astype(BF16)
    for j in range(3):
        pack_head(res[:, 128 * j : 128 * j + 128], v_ro, j)
    if net:
        so.start()

    @pl.loop(0, 3)
    def _(pair):
        if net:
            on(pair, 1, sz.cross2)
            on(pair, 2, s2.mid0, s2.join, so.mid1, so.mid0, sz.cross1)

        v_dk[...] = jnp.zeros_like(v_dk)
        v_dv[...] = jnp.zeros_like(v_dv)
        for i in range(4):
            n = 256 * (i + 1)
            q = v_qkv[pair, 256 * i : n, :]
            up = v_dctx[pair, 256 * i : n, :]
            qs = [only(q, h) for h in range(2)]
            ups = [only(up, h) for h in range(2)]
            dq = jnp.zeros((256, 128), F32)
            probs = [[], []]
            grads = [[], []]
            for h in range(2):
                lse = v_lse[pair, h : h + 1, 256 * i : n]
                delta = jnp.zeros((1, 256), F32)
                for j in range(i + 1):
                    at = slice(256 * j, 256 * j + 256)
                    s = mm(v_qkv[3 + pair, at, :], qs[h], NT)
                    p = jnp.exp(s - lse)
                    if j == i:
                        key = lax.broadcasted_iota(jnp.int32, s.shape, 0)
                        query = lax.broadcasted_iota(jnp.int32, s.shape, 1)
                        p = jnp.where(key <= query, p, 0.0)
                    dp = mm(v_qkv[6 + pair, at, :], ups[h], NT)
                    delta += jnp.sum(p * dp, 0, keepdims=True)
                    probs[h].append(p)
                    grads[h].append(dp)
                for j in range(i + 1):
                    grads[h][j] = (probs[h][j] * (grads[h][j] - delta)).astype(BF16)
                    probs[h][j] = probs[h][j].astype(BF16)
            for j in range(i + 1):
                at = slice(256 * j, 256 * j + 256)
                for h in range(2):
                    k = only(v_qkv[3 + pair, at, :], h)
                    dq += mm(grads[h][j], k, TN)
                v_dv[at, :] += mm(cat([probs[0][j], probs[1][j]]), jnp.concatenate(ups, axis=0))
                v_dk[at, :] += mm(cat([grads[0][j], grads[1][j]]), jnp.concatenate(qs, axis=0))
            v_qkv[pair, 256 * i : n, :] = (dq * HEAD_DIM**-0.5).astype(BF16)
            if net and i == 2:
                on(pair, 0, s3.join, s2.mid1)
        v_qkv[3 + pair] = v_dk[...].astype(BF16)
        v_qkv[6 + pair] = v_dv[...].astype(BF16)
        res = mm(v_nrmT[...], cat([v_qkv[3 * part + pair] for part in range(3)])).astype(BF16)
        for part in range(3):
            pack_head(res[:, 128 * part : 128 * part + 128], v_rq, 3 * pair + part)
        if net:
            sq(pair).start()

    w_qkv = cat([v_wh[3 * j + part] for part in range(3) for j in range(3)])
    if net:
        p0, p1, p2 = sq(0), sq(1), sq(2)
        p0.mid1()
        p0.mid0()
    for half, start in enumerate((theirs, mine)):
        lhs = cat([v_qkv[i, rows(start, HALF), :] for i in range(9)])
        res = mm(lhs, w_qkv, NT)
        if half == 0:
            v_send[1] = res.astype(BF16)
            exchange(7, v_send.at[1], v_recv.at[1]).start()
            if net:
                p1.mid1()
                p1.mid0()
        else:
            v_acc[...] = res
    if net:
        so.join()
    exchange(7, v_send.at[1], v_recv.at[1]).wait()

    @pl.loop(0, HALF // 64)
    def _(i):
        r = rows(i * 64, 64)
        upper = v_acc[r, :] + v_recv[1, r, :].astype(F32)
        o_in[r, :] = o_in[r, :] + norm_back(upper, hid[r, :].astype(F32), v_param[0:1, :], 0)

    v_swap[0] = v_sums[...]
    exchange(8, v_swap.at[0], v_swap.at[1]).start()
    if net:
        p0.join()
        p2.mid1()
        p2.mid0()
    exchange(8, v_swap.at[0], v_swap.at[1]).wait()
    both = v_swap[0] + v_swap[1]
    if net:
        for dd in range(NB):
            piece = cat([both[:, RB * dd : RB * dd + RB], jnp.zeros((8, 128 - RB), F32)])
            v_p0[0, dd] = piece
            v_p0[1, dd] = piece
        s0.start()

    for half, start in enumerate((theirs, mine)):
        res = mm(v_act[0, rows(start, HALF), :], v_down[0].reshape(D, D), NT)
        res += mm(v_act[1, rows(start, HALF), :], v_down[1].reshape(D, D), NT)
        if half == 0:
            v_send[0] = res.astype(BF16)
            exchange(9, v_send.at[0], v_recv.at[0]).start()
            if net:
                p1.join()
        else:
            o_block[...] = v_mid[...] + res
    if net:
        p2.join()
    exchange(9, v_send.at[0], v_recv.at[0]).wait()
    o_block[...] += v_recv[0].astype(F32)
    if net:
        s3.finish(o_down.at[:, left])
        sz.finish(o_down.at[:, right])
        s2.finish(o_up)
        so.finish(f_o)
        o_out[...] = cat([unfold(f_o[j]) for j in range(3)]).T
        p0.finish(f_q.at[0])
        p1.finish(f_q.at[1])
        p2.finish(f_q.at[2])
        for part in range(3):
            o_qkv[part] = cat([unfold(f_q[j, part]) for j in range(3)])
        s0.finish(v_swap.at[0, :, 0:128])
        o_small[...] = pltpu.roll(v_swap[0, :, 0:128], lax.rem(128 - 24 * pos.t, 128), 1)[:, 0:24]
        for g in (g0, g2, g3, gz, s0, so, s2, s3, sz, p0, p1, p2):
            g.drain()
    else:
        o_small[...] = both
        o_qkv[...] = v_rq[...]
        o_out[...] = v_ro[...]
        o_up[...] = v_p2[...]
        o_down[...] = v_p3[...]
    exchange_rows(6, v_low).wait_send()


def fold_rows(block):
    return block.reshape(2, 48, 3, 64).transpose(2, 1, 0, 3).reshape(3, 48, 128)


def unfold_rows(packed):
    return packed.reshape(3, 48, 2, 64).transpose(2, 1, 0, 3).reshape(RB, 192)


def shards(
    hidden_in, cotangent, group_ids, weight_table, table_index, qkv_weight, out_weight, up_weight, down_weight,
    norm1_gain, norm1_bias, norm2_gain, norm2_bias,
):
    n_dp, n_t = lax.axis_size("dp"), lax.axis_size("tensor")
    net = n_dp == NB and n_t == 4
    core = lax.rem(lax.axis_index("tensor"), 2)
    scale_tokens = hidden_in.shape[0] * n_dp * n_t / GROUPS
    ids = group_ids.reshape(1, HALF)
    down = down_weight.T
    vm, dma = pltpu.VMEM, pltpu.SemaphoreType.DMA
    vspec = pl.BlockSpec(memory_space=pltpu.VMEM)
    aspec = pl.BlockSpec(memory_space=pl.ANY)
    norm_vectors = (norm1_gain, norm1_bias, norm2_gain, norm2_bias)
    s_q, s_o, s_w = (3, 48, 128), (3, 48, 128), (RB, D)
    if net:
        vectors = [v.reshape(1, RB) for v in norm_vectors]
        table, weights = table_index.reshape(1, GROUPS), weight_table
        given = [qkv_weight.transpose(1, 0, 2), out_weight, up_weight, down, *vectors]
        weight_spec = pl.BlockSpec(memory_space=pltpu.SMEM)
        given_specs = [vspec, vspec, aspec, aspec] + [vspec] * 4
        grads = [((8, 24), F32), ((3, RB, 192), F32), ((192, RB), F32), (s_w, F32), (s_w, F32)]
        nets = [vm((2, NB, 8, 128), F32), vm((2 * NB, 8, 128), F32), dma((2 * NB,)), dma((2 * NB,))]
        nets += [vm((3, 2, 4) + s_q, BF16), vm((3, 8) + s_q, BF16)]
        for s in (s_o, s_w, (RB, CUT)):
            nets += [vm((2, 4) + s, BF16), vm((8,) + s, BF16)]
        nets += [vm((4, 4, RB, D - CUT), BF16), vm((3, RB, D - CUT), BF16)]
        nets += [vm((3,) + s_q, F32), vm(s_o, F32)]
        nets += [dma((7, 4, 4)), dma((8, 2, NB)), dma((5, 4)), dma((7, 4, 4)), dma((7, 4, 4)), dma((5, 4)), dma((5, 4))]
    else:

        def whole(block, axis):
            full = lax.all_gather(block, "dp", axis=axis, tiled=True)
            every = lax.all_gather(full, "tensor", axis=0)
            return lax.dynamic_index_in_dim(every.reshape((n_t // 2, 2) + full.shape), core, 1, keepdims=False)

        heads = jnp.concatenate([qkv_weight.transpose(1, 0, 2), out_weight.T[None]], axis=0)
        heads = whole(heads, 1).reshape(2, 4, NB, RB, 192).transpose(0, 2, 1, 3, 4)
        folded = jax.vmap(jax.vmap(jax.vmap(fold_rows)))(heads)
        given = [
            jnp.pad(lax.all_gather(jnp.stack(norm_vectors).astype(F32), "dp", axis=1, tiled=True), ((0, 4), (0, 0))),
            folded[:, :, :3].transpose(0, 1, 3, 2, 4, 5).reshape(2, NB, 9, 48, 128),
            folded[:, :, 3],
            whole(up_weight, 0).reshape(2, NB, RB, D),
            whole(down, 0).reshape(2, NB, RB, D),
        ]
        member = (group_ids[:, None] == jnp.arange(GROUPS, dtype=jnp.int32)[None, :]).astype(F32)
        counts = lax.psum(jnp.sum(member, 0), ("dp", "tensor"))
        hits = table_index[:, None] == jnp.arange(TABLE, dtype=jnp.int32)[None, :]
        scale = jnp.sum(jnp.where(hits, weight_table[None, :], 0.0), 1) * scale_tokens / jnp.maximum(counts, 1.0)
        weights = jnp.pad(scale[None, :], ((0, 7), (0, 128 - GROUPS)))
        table = counts.reshape(1, GROUPS)
        weight_spec = vspec
        given_specs = [vspec, aspec, aspec, aspec, aspec]
        grads = [((8, D), F32), ((2, NB, 9, 48, 128), BF16), ((2, NB, 3, 48, 128), BF16)]
        grads += [((2, NB) + s_w, BF16), ((2, NB) + s_w, BF16)]
        nets = []
    shapes = [((HALF, D), F32), ((1, GROUPS), F32), ((HALF, D), F32), *grads]
    outs = pl.pallas_call(
        functools.partial(block_kernel, net, scale_tokens, 5 + len(given)),
        out_shape=[(vm if net else jax.ShapeDtypeStruct)(*s) for s in shapes],
        in_specs=[aspec, aspec, vspec, vspec, weight_spec, *given_specs],
        out_specs=[vspec] * len(shapes),
        scratch_shapes=[
            vm((2, NB, 8, 128), F32), vm((3, 8, 128), F32), vm((8, D), F32), vm((8, 128), jnp.int32), vm((9, 48, 128), BF16),
            vm((3, 48, 128), BF16), vm((2, NB, 9, 48, 128), BF16), vm((2, NB, 3, 48, 128), BF16), vm((2, NB, RB, D), BF16),
            vm((2, NB, RB, D), BF16), vm((9, D, 128), BF16), vm((3, D, 128), BF16),
            vm((LENGTH, D), BF16), vm((D, LENGTH), BF16), vm((LENGTH, D), BF16), vm((D, LENGTH), BF16), vm((LENGTH, D), BF16),
            vm((D, LENGTH), BF16), vm((9, LENGTH, 128), BF16), vm((3, 8, LENGTH), F32), vm((3, LENGTH, 128), BF16),
            vm((3, LENGTH, 128), BF16), vm((HALF, D), F32), vm((2, LENGTH, D), BF16), vm((2, LENGTH, D), BF16),
            vm((2, HALF, D), BF16), vm((2, HALF, D), BF16), vm((HALF, D), F32), vm((LENGTH, 128), F32), vm((LENGTH, 128), F32),
            vm((2, NB, RB, D), BF16), vm((2, NB, RB, D), BF16), vm((8, D), F32), vm((2, 8, D), F32),
            vm((HALF, D), BF16), vm((HALF, D), BF16), dma((2, 10)), dma((6,)), *nets,
        ],
        compiler_params=pltpu.CompilerParams(collective_id=0, has_side_effects=True, vmem_limit_bytes=VMEM_LIMIT if net else WIDE_VMEM_LIMIT),
        name="block",
    )(hidden_in, cotangent, ids, table, weights, *given)
    block_output, counts, input_grad, sums, grad_qkv, grad_out, grad_up, grad_down = outs
    if net:
        norms = [sums[i] for i in range(4)]
        grad_qkv = grad_qkv.transpose(1, 0, 2)
    else:

        def owned(part):
            base = jnp.zeros((n_t // 2, 2) + part.shape[1:], F32)
            base = lax.dynamic_update_index_in_dim(base, part.astype(F32), core, 1)
            flat = base.reshape((n_t,) + part.shape[1:])
            mine = lax.psum_scatter(flat, "tensor", scatter_dimension=0, tiled=False)
            return lax.psum_scatter(mine, "dp", scatter_dimension=0, tiled=True)

        parts = grad_qkv.reshape(2, NB, 3, 3, 48, 128).transpose(0, 1, 3, 2, 4, 5)
        parts = jax.vmap(jax.vmap(jax.vmap(unfold_rows)))(parts)
        grad_qkv = owned(parts.transpose(0, 1, 3, 2, 4).reshape(2, D, 3, 192))
        grad_out = owned(jax.vmap(jax.vmap(unfold_rows))(grad_out).reshape(2, D, 192)).T
        grad_up, grad_down = owned(grad_up.reshape(2, D, D)), owned(grad_down.reshape(2, D, D))
        half_sums = jnp.where(core == 0, sums, 0.0)
        norms = [lax.psum_scatter(half_sums[i], ("dp", "tensor"), scatter_dimension=0, tiled=True) for i in range(4)]
    return (
        block_output,
        input_grad,
        grad_qkv,
        grad_out,
        grad_up,
        grad_down.T,
        norms[0],
        norms[1],
        norms[2],
        norms[3],
        counts.reshape(GROUPS),
    )


def solution(mesh):
    both = ("dp", "tensor")
    return jax.shard_map(
        shards,
        mesh=mesh,
        in_specs=(
            P(both, None), P(both, None), P(both), P(), P(), P("dp", None, "tensor"), P("tensor", "dp"), P("dp", "tensor"),
            P("tensor", "dp"), P("dp"), P("dp"), P("dp"), P("dp"),
        ),
        out_specs=(
            P(both, None), P(both, None), P("dp", None, "tensor"), P("tensor", "dp"), P("dp", "tensor"), P("tensor", "dp"),
            P(both), P(both), P(both), P(both), P(),
        ),
        check_vma=False,
    )
```
